128 devices in a mesh: blk: 16 (over x, z), beam: 8 (over y, core).
Axes of the slice: x: 4, y: 4, z: 4, core: 2. Of those that a mesh axis runs over, the one named last changes fastest.
Arguments:
- embeds: bfloat16 [4, 128, 2048], P(None, 'beam'), may hold values from -6 to 6
- attn_gain: float32 [2048], replicated, may hold values from 0.25 to 1.75
- w_query: bfloat16 [2048, 3072], P(None, 'blk'), may hold values from -0.125 to 0.125
- w_latent: bfloat16 [2048, 576], replicated, may hold values from -0.125 to 0.125
- latent_gain: float32 [512], replicated, may hold values from 0.3 to 3
- w_key_up: bfloat16 [16, 128, 512], P('blk'), may hold values from -0.5 to 0.5
- w_value_up: bfloat16 [16, 512, 128], P('blk'), may hold values from -0.25 to 0.25
- w_out: bfloat16 [2048, 2048], P('blk'), may hold values from -0.125 to 0.125
- ffn_gain: float32 [2048], replicated, may hold values from 0.25 to 1.75
- w_shared_gate: bfloat16 [2048, 2816], P(None, 'blk'), may hold values from -0.125 to 0.125
- w_shared_up: bfloat16 [2048, 2816], P(None, 'blk'), may hold values from -0.125 to 0.125
- w_shared_down: bfloat16 [2816, 2048], P('blk'), may hold values from -0.109375 to 0.109375
- w_expert_gate: bfloat16 [32, 2048, 2816], P('blk', None, 'beam'), may hold values from -0.125 to 0.125
- w_expert_up: bfloat16 [32, 2048, 2816], P('blk', None, 'beam'), may hold values from -0.125 to 0.125
- w_expert_down: bfloat16 [32, 2816, 2048], P('blk', 'beam'), may hold values from -0.15625 to 0.15625
- cache_pool: bfloat16 [16, 96, 128, 576], P('beam', 'blk'), may hold values from -1600 to 1600
- block_tables: int32 [16, 8, 64], P('beam'), may hold values from 0 to 95, as said below
- block_counts: int32 [16], P('beam'), may hold values from 4 to 64
- parents: int32 [4, 16, 8], P(None, 'beam'), may hold values from 0 to 7
- expert_ids: int32 [4, 128, 6], replicated, may hold values from 0 to 63, all different within a row; in each aligned block of 128 rows (0 to 127, 128 to 255, ..., all dimensions but the last counted through in order) at most 24 rows name the same one
- expert_weights: float32 [4, 128, 6], replicated, may hold values from 0.1 to 0.6
Outputs:
- layer_out: float32 [4, 128, 2048], P(None, ('blk', 'beam'))
The draws below stay inside these ranges and needn't reach their ends.
Inputs may be any that keep to these rules, and one draw needn't show every extreme that they name: `block_tables`: for each group g, entries j below block_counts[g] of one beam name different physical blocks; entries at or beyond block_counts[g] are never read. `expert_ids`: the experts of one row differ; within one step all rows together name one expert at most 24 times.
All inputs are finite; a program needn't handle non-finite values.
Results may differ from the reference program's by a relative error of at most 0.034.
Values may be sent and summed in bfloat16 or wider, within the bound.
No kernel may reach another device: no remote copies, remote signals or barrier semaphores. Data moves between devices by JAX's collectives and lax.ppermute only.
A program may use at most 128 MiB of HBM per device.

```python
import math
import jax
import jax.numpy as jnp
import numpy as np
from jax import lax

D = 2048
HEADS = 16
DN = 128
DR = 64
DC = 512
DV = 128
EXPERTS = 64
FFE = 1408
FS = 2816
TOPK = 6
BEAMS = 8
BLOCK = 128
DIV = 4
STEPS = 4
PB_DEV = 6
GROUPS = 16
ROWS = 128
CAP = 24
PBLK = 96
MAXBLK = 64
N_BLK = 16


def block_layout(key):
    count_key = jax.random.fold_in(key, 11)
    counts = jax.random.randint(count_key, (GROUPS,), DIV, MAXBLK + 1)
    longest = jax.random.randint(jax.random.fold_in(key, 12), (), 0, GROUPS)
    shortest = (longest + 1 + jax.random.randint(jax.random.fold_in(key, 14), (), 0, GROUPS - 1)) % GROUPS
    counts = counts.at[longest].set(MAXBLK)
    counts = counts.at[shortest].set(DIV)
    return counts.astype(jnp.int32)


def draw_block_counts(key, part):
    return block_layout(key)


def draw_block_tables(key, part):
    counts = block_layout(key)
    group_keys = jax.random.split(jax.random.fold_in(key, 13), GROUPS)
    orders = jax.vmap(lambda one_key: jax.random.permutation(one_key, PBLK))(group_keys).astype(jnp.int32)
    logical = jnp.arange(MAXBLK, dtype=jnp.int32)[None, None, :]
    beam_ids = jnp.arange(BEAMS, dtype=jnp.int32)[None, :, None]
    tail_start = (counts - DIV)[:, None, None]
    own_block = (logical >= tail_start) & (logical < counts[:, None, None])
    own_position = MAXBLK + beam_ids * DIV + (logical - tail_start)
    position = jnp.where(own_block, own_position, jnp.broadcast_to(logical, own_position.shape))
    spread = jnp.broadcast_to(orders[:, None, :], (GROUPS, BEAMS, PBLK))
    return jnp.take_along_axis(spread, position, axis=2).astype(jnp.int32)


def draw_cache_pool(key, part):
    full_shape = (GROUPS, PBLK, BLOCK, DC + DR)
    background = jnp.clip(jax.random.normal(jax.random.fold_in(key, 21), full_shape, jnp.float32), -6.0, 6.0)
    lowest = 30.0
    highest = 300.0
    group_rank = jax.random.permutation(jax.random.fold_in(key, 22), GROUPS)
    group_on = group_rank < GROUPS // 2
    block_pick = jax.random.randint(jax.random.fold_in(key, 23), (GROUPS, PBLK), 0, 4) == 0
    block_on = block_pick & group_on[:, None]
    start_token = jax.random.randint(jax.random.fold_in(key, 24), (GROUPS, PBLK), 0, BLOCK // 2) * 2
    strength = jnp.exp(jax.random.uniform(jax.random.fold_in(key, 25), (GROUPS, PBLK), jnp.float32, jnp.log(lowest), jnp.log(highest)))
    planted = jnp.clip(jax.random.normal(jax.random.fold_in(key, 26), (GROUPS, PBLK, DR), jnp.float32), -4.0, 4.0)
    planted = planted * strength[:, :, None]
    token_index = jnp.arange(BLOCK, dtype=jnp.int32)[None, None, :]
    lead_token = (token_index == start_token[:, :, None]) & block_on[:, :, None]
    follow_token = (token_index == start_token[:, :, None] + 1) & block_on[:, :, None]
    rope_part = background[..., DC:]
    rope_part = jnp.where(lead_token[..., None], planted[:, :, None, :], rope_part)
    rope_part = jnp.where(follow_token[..., None], 0.99 * planted[:, :, None, :], rope_part)
    return jnp.concatenate([background[..., :DC], rope_part], axis=-1).astype(jnp.bfloat16)


def set_ends(values, own_key, least, largest):
    dims = values.shape
    place = [jax.random.randint(jax.random.fold_in(own_key, axis), (), 0, dims[axis]) for axis in range(len(dims))]
    values = values.at[tuple(place)].set(least)
    longest = dims.index(max(dims))
    place[longest] = (place[longest] + 1) % dims[longest]
    return values.at[tuple(place)].set(largest)


def block_scale(own_key, dims, shards, low, top_value):
    def one(dim, shards_of):
        steps = jax.random.uniform(jax.random.fold_in(jax.random.fold_in(own_key, 6), dim), (shards_of,), jnp.float32, low / len(shards), top_value / len(shards))
        return jnp.repeat(jnp.exp(steps), dims[dim] // shards_of).reshape((-1,) + (1,) * (len(dims) - dim - 1))

    level = one(*shards[0])
    for cut in shards[1:]:
        level = level * one(*cut)
    return level


def routed_block(key, own, number, rows, amount, top, limit, lean):
    order = jax.random.permutation(key, amount)
    crowded, usual = load_shares(amount, rows * top, limit, lean, True), load_shares(amount, rows * top, limit, lean, False)
    places = jnp.arange(amount)

    def named(tallies, turn):
        used = int((tallies > 0).sum())
        fixed = max(1, used // 4)
        passed = fixed + (places - fixed + turn * (used - fixed)) % max(1, amount - fixed)
        return jnp.zeros((amount,), jnp.int32).at[order[jnp.where(places < fixed, places, passed)]].set(jnp.asarray(tallies, jnp.int32))

    tallies = jnp.where(number % 4 == 0, named(crowded, number // 4), named(usual, number - number // 4 - 1))
    mixed = jax.random.permutation(jax.random.fold_in(own, 3), amount)
    source_of, sink = mixed[0:amount // 2 * 2:2], mixed[1:amount // 2 * 2:2]
    slack = jnp.minimum(tallies[source_of] - 1, limit - tallies[sink]) // 2
    slack = jnp.where((source_of == order[0]) | (sink == order[0]) | (tallies[sink] == 0), 0, jnp.maximum(slack, 0))
    passed = jax.random.randint(jax.random.fold_in(own, 4), (amount // 2,), 0, 1 << 20) % (slack + 1)
    tallies = tallies.at[source_of].add(-passed).at[sink].add(passed)
    items = jnp.searchsorted(jnp.cumsum(tallies), jnp.arange(rows * top), side="right").astype(jnp.int32)
    grid = items.reshape(top, rows).T
    grid = grid[jax.random.permutation(jax.random.fold_in(own, 1), rows)]
    turn = jax.random.randint(jax.random.fold_in(own, 2), (rows, 1), 0, top)
    return jnp.take_along_axis(grid, (jnp.arange(top)[None, :] + turn) % top, axis=1)


def load_shares(amount, total, limit, lean, full):
    weights = [(1 << 20) // math.isqrt(standing ** lean) + 1 for standing in range(1, amount + 1)]
    largest = limit if full else min(limit, max(-(-total // amount), total * weights[0] // sum(weights)))
    least = 1 if total - largest >= amount - 1 else 0
    given, spare = [largest] + [least] * (amount - 1), total - largest - least * (amount - 1)
    while spare > 0:
        movable = [i for i in range(1, amount) if given[i] < largest] or [i for i in range(1, amount) if given[i] < limit]
        whole, budget = sum([weights[i] for i in movable]), spare
        for i in movable:
            more = min(limit - given[i], max(1, budget * weights[i] // whole), spare)
            given[i] = given[i] + more
            spare = spare - more
    return np.array(given)


def scatter_about(stream_key, shape, deviation, bound, cuts=(), held_as=jnp.bfloat16):
    result = jax.random.normal(stream_key, shape, jnp.float32) * deviation
    if len(cuts) > 0:
        result = block_scale(stream_key, shape, cuts, -0.22, 0.18) * result
    return jnp.clip(result, min=-bound, max=bound).astype(held_as)


def setup_inputs(seed: int = 0) -> dict:
    splits = jax.random.split(jax.random.key(seed), 22)
    embeds = scatter_about(splits[0], (STEPS, ROWS, D), 1.0, 6.0, ((1, 8),))
    attn_gain = jnp.clip(1.0 + 0.15 * jax.random.normal(splits[1], (D,), jnp.float32), 0.25, 1.75)
    w_query = scatter_about(splits[2], (D, HEADS * (DN + DR)), D ** -0.5, 0.125, ((1, 16),))
    w_latent = scatter_about(splits[3], (D, DC + DR), D ** -0.5, 0.125)
    latent_gain = jnp.clip(jnp.exp(jax.random.uniform(splits[4], (DC,), jnp.float32, math.log(0.3), math.log(3.0))), 0.3, 3.0)
    w_key_up = scatter_about(splits[5], (HEADS, DN, DC), DN ** -0.5, 0.5, ((0, 16),))
    w_value_up = scatter_about(splits[6], (HEADS, DC, DV), DC ** -0.5, 0.25, ((0, 16),))
    w_out = scatter_about(splits[7], (HEADS * DV, D), (HEADS * DV) ** -0.5, 0.125, ((0, 16),))
    ffn_gain = jnp.clip(1.0 + 0.15 * jax.random.normal(splits[8], (D,), jnp.float32), 0.25, 1.75)
    w_shared_gate = scatter_about(splits[9], (D, FS), D ** -0.5, 0.125, ((1, 16),))
    w_shared_up = scatter_about(splits[10], (D, FS), D ** -0.5, 0.125, ((1, 16),))
    w_shared_down = scatter_about(splits[11], (FS, D), FS ** -0.5, 0.109375, ((0, 16),))
    w_expert_gate = scatter_about(splits[12], (EXPERTS // 2, D, 2 * FFE), D ** -0.5, 0.125, ((0, 16), (2, 8)))
    w_expert_up = scatter_about(splits[13], (EXPERTS // 2, D, 2 * FFE), D ** -0.5, 0.125, ((0, 16), (2, 8)))
    w_expert_down = scatter_about(splits[14], (EXPERTS // 2, 2 * FFE, D), FFE ** -0.5, 0.15625, ((0, 16), (1, 8)))
    cache_pool = draw_cache_pool(jax.random.fold_in(splits[21], 71), 0)
    block_tables = draw_block_tables(jax.random.fold_in(splits[21], 71), 0)
    block_counts = draw_block_counts(jax.random.fold_in(splits[21], 71), 0)
    parents = set_ends(jax.random.randint(splits[18], (STEPS, GROUPS, BEAMS), 0, BEAMS), jax.random.fold_in(splits[18], 1), 0, BEAMS - 1).astype(jnp.int32)
    expert_ids_keys = jax.random.split(jax.random.fold_in(splits[19], 1), STEPS * ROWS // ROWS)
    expert_ids_turns = jax.random.permutation(jax.random.fold_in(splits[19], 3), STEPS * ROWS // ROWS)
    expert_ids = jax.vmap(lambda own, number: routed_block(jax.random.fold_in(splits[19], 2), own, number, ROWS, EXPERTS, TOPK, CAP, 2))(expert_ids_keys, expert_ids_turns).reshape((STEPS, ROWS, TOPK))
    expert_weights = jnp.clip(jax.random.uniform(splits[20], (STEPS, ROWS, TOPK), jnp.float32, 0.1, 0.6), 0.1, 0.6)
    return {"embeds": embeds, "attn_gain": attn_gain, "w_query": w_query, "w_latent": w_latent, "latent_gain": latent_gain, "w_key_up": w_key_up, "w_value_up": w_value_up, "w_out": w_out, "ffn_gain": ffn_gain, "w_shared_gate": w_shared_gate, "w_shared_up": w_shared_up, "w_shared_down": w_shared_down, "w_expert_gate": w_expert_gate, "w_expert_up": w_expert_up, "w_expert_down": w_expert_down, "cache_pool": cache_pool, "block_tables": block_tables, "block_counts": block_counts, "parents": parents, "expert_ids": expert_ids, "expert_weights": expert_weights}


THETA = 50000.0
EPS = 1e-06
NEG = -1e+30

def rms_scale(values, gain):
    mean_sq = lax.optimization_barrier(jnp.mean(values * values, axis=-1, keepdims=True))
    return values * lax.rsqrt(mean_sq + EPS) * gain

def rotate(values, position):
    half_dim = values.shape[-1] // 2
    frequency = THETA ** (-jnp.arange(half_dim, dtype=jnp.float32) * 2.0 / values.shape[-1])
    angles = position[..., None] * frequency
    cosine = jnp.cos(angles)
    sine_part = jnp.sin(angles)
    lower_half = values[..., :half_dim]
    upper_half = values[..., half_dim:]
    return jnp.concatenate([lower_half * cosine - upper_half * sine_part, lower_half * sine_part + upper_half * cosine], axis=-1)

def combine(earlier, later):
    top_first, sum_first, lat_first = earlier
    top_second, sum_second, lat_second = later
    top_score = jnp.maximum(top_first, top_second)
    scale_first = jnp.exp(top_first - top_score)
    scale_second = jnp.exp(top_second - top_score)
    return (top_score, sum_first * scale_first + sum_second * scale_second, lat_first * scale_first[..., None] + lat_second * scale_second[..., None])

def partial_attend(scores, key_mask, values, form):
    masked = jnp.where(key_mask, scores, NEG)
    top_score = lax.optimization_barrier(jnp.max(masked, axis=-1))
    weights = jnp.where(key_mask, jnp.exp(masked - top_score[..., None]), 0.0)
    weight_sum = lax.optimization_barrier(jnp.sum(weights, axis=-1))
    rounded = weights.astype(jnp.bfloat16).astype(jnp.float32)
    latent_sum = jnp.einsum(form, rounded, values.astype(jnp.float32))
    return (top_score, weight_sum, latent_sum)

def reference(embeds, attn_gain, w_query, w_latent, latent_gain, w_key_up, w_value_up, w_out, ffn_gain, w_shared_gate, w_shared_up, w_shared_down, w_expert_gate, w_expert_up, w_expert_down, cache_pool, block_tables, block_counts, parents, expert_ids, expert_weights):
    score_scale = (DN + DR) ** (-0.5)
    capacity = CAP
    set_len = PB_DEV * BLOCK
    entry_width = DC + DR
    recent = jnp.zeros((GROUPS, BEAMS, STEPS, entry_width), jnp.bfloat16)
    tables = block_tables
    base_pos = (block_counts * BLOCK).astype(jnp.float32)
    valid = jnp.arange(MAXBLK, dtype=jnp.int32)[None, None, :] < block_counts[:, None, None]
    physical = jnp.arange(PBLK, dtype=jnp.int32)
    results = []
    for decode_step in range(STEPS):
        parent = parents[decode_step]
        recent = jnp.take_along_axis(recent, parent[:, :, None, None], axis=1)
        tables = jnp.take_along_axis(tables, parent[:, :, None], axis=1)
        tokens = embeds[decode_step]
        normed = rms_scale(tokens.astype(jnp.float32), attn_gain).astype(jnp.bfloat16)
        queries = jnp.dot(normed, w_query, preferred_element_type=jnp.float32).astype(jnp.bfloat16)
        queries = queries.reshape(ROWS, HEADS, DN + DR)
        position = jnp.repeat(base_pos + decode_step, BEAMS)
        query_latent = jnp.einsum('rhn,hnc->rhc', queries[:, :, :DN].astype(jnp.float32), w_key_up.astype(jnp.float32))
        query_rope = rotate(queries[:, :, DN:].astype(jnp.float32), position[:, None])
        query_full = jnp.concatenate([query_latent, query_rope], axis=-1).astype(jnp.bfloat16)
        projected = jnp.dot(normed, w_latent, preferred_element_type=jnp.float32)
        new_entry = jnp.concatenate([rms_scale(projected[:, :DC], latent_gain), rotate(projected[:, DC:], position)], axis=-1).astype(jnp.bfloat16)
        recent = recent.at[:, :, decode_step].set(new_entry.reshape(GROUPS, BEAMS, entry_width))
        block_used = lax.optimization_barrier(jnp.sum(((tables[..., None] == physical) & valid[..., None]).astype(jnp.int32), axis=2)) > 0

        def per_group(group_item):
            group_queries, pool_blocks, used_blocks = group_item
            cache_keys = pool_blocks.reshape(N_BLK, set_len, entry_width).astype(jnp.float32)
            flat_queries = group_queries.reshape(BEAMS * HEADS, entry_width).astype(jnp.float32)
            scores = jnp.einsum('qe,ske->sqk', flat_queries, cache_keys) * score_scale
            key_mask = jnp.repeat(jnp.repeat(used_blocks, BLOCK, axis=1), HEADS, axis=0)
            key_mask = key_mask.reshape(BEAMS * HEADS, N_BLK, set_len).transpose(1, 0, 2)
            top_score, weight_sum, latent_sum = partial_attend(scores, key_mask, cache_keys[:, :, :DC], 'sqk,skc->sqc')
            best = lax.optimization_barrier(jnp.max(top_score, axis=0))
            factor = jnp.exp(top_score - best[None])
            total = lax.optimization_barrier(jnp.sum(weight_sum * factor, axis=0))
            latent_all = lax.optimization_barrier(jnp.sum(latent_sum * factor[..., None], axis=0))
            return (best, total, latent_all)
        pooled = lax.map(per_group, (query_full.reshape(GROUPS, BEAMS, HEADS, entry_width), cache_pool, block_used))
        pooled = (pooled[0].reshape(ROWS, HEADS), pooled[1].reshape(ROWS, HEADS), pooled[2].reshape(ROWS, HEADS, DC))
        recent_rows = recent.reshape(ROWS, STEPS, entry_width)[:, :decode_step + 1].astype(jnp.float32)
        recent_scores = jnp.einsum('rhe,rse->rhs', query_full.astype(jnp.float32), recent_rows) * score_scale
        recent_part = partial_attend(recent_scores, jnp.ones(recent_scores.shape, bool), recent_rows[:, :, :DC], 'rhs,rsc->rhc')
        top_score, weight_sum, latent_sum = combine(pooled, recent_part)
        attended = (latent_sum / weight_sum[..., None]).astype(jnp.bfloat16)
        head_out = jnp.einsum('rhc,hcv->rhv', attended.astype(jnp.float32), w_value_up.astype(jnp.float32)).astype(jnp.bfloat16)
        resid = tokens.astype(jnp.float32) + jnp.dot(head_out.reshape(ROWS, HEADS * DV), w_out, preferred_element_type=jnp.float32)
        ffn_in = rms_scale(resid, ffn_gain).astype(jnp.bfloat16)
        shared_act = (jax.nn.silu(jnp.dot(ffn_in, w_shared_gate, preferred_element_type=jnp.float32)) * jnp.dot(ffn_in, w_shared_up, preferred_element_type=jnp.float32)).astype(jnp.bfloat16)
        shared_out = jnp.dot(shared_act, w_shared_down, preferred_element_type=jnp.float32)
        matches = expert_ids[decode_step][:, :, None] == jnp.arange(EXPERTS, dtype=jnp.int32)
        routed = jnp.any(matches, axis=1)
        row_weight = lax.optimization_barrier(jnp.sum(jnp.where(matches, expert_weights[decode_step][:, :, None], 0.0), axis=1))
        slot_index = jnp.cumsum(routed.astype(jnp.int32), axis=0) - 1
        slot_index = jnp.where(routed, slot_index, capacity)
        expert_cols = jnp.broadcast_to(jnp.arange(EXPERTS, dtype=jnp.int32)[None, :], (ROWS, EXPERTS))
        row_numbers = jnp.broadcast_to(jnp.arange(ROWS, dtype=jnp.int32)[:, None], (ROWS, EXPERTS))
        slot_rows = jnp.full((EXPERTS, capacity), ROWS, jnp.int32).at[expert_cols, slot_index].set(row_numbers, mode='drop')
        weight_pad = jnp.concatenate([row_weight.T, jnp.zeros((EXPERTS, 1), row_weight.dtype)], axis=1)
        slot_weight = jnp.take_along_axis(weight_pad, slot_rows, axis=1)
        pair_rows = slot_rows.reshape(EXPERTS // 2, 2, capacity)

        def per_pair(pair_item):
            rows_here, gate_mat, up_mat, down_mat = pair_item
            outputs = []
            for pair_half in range(2):
                picked = jnp.take(ffn_in, rows_here[pair_half], axis=0, mode='fill', fill_value=0)
                gate_part = gate_mat[:, pair_half * FFE:(pair_half + 1) * FFE]
                up_part = up_mat[:, pair_half * FFE:(pair_half + 1) * FFE]
                down_part = down_mat[pair_half * FFE:(pair_half + 1) * FFE]
                activation = (jax.nn.silu(jnp.dot(picked, gate_part, preferred_element_type=jnp.float32)) * jnp.dot(picked, up_part, preferred_element_type=jnp.float32)).astype(jnp.bfloat16)
                outputs.append(jnp.dot(activation, down_part, preferred_element_type=jnp.float32))
            return jnp.stack(outputs)
        down_out = lax.map(per_pair, (pair_rows, w_expert_gate, w_expert_up, w_expert_down)).reshape(EXPERTS, capacity, D)
        routed_sum = jnp.zeros((ROWS, D), jnp.float32).at[slot_rows.reshape(-1)].add((down_out * slot_weight[..., None]).reshape(-1, D), mode='drop')
        results.append(resid + shared_out + routed_sum)
    return jnp.stack(results)
```

```python
import jax
import jax.numpy as jnp
from jax import lax
from jax.experimental import pallas as pl
from jax.experimental.pallas import tpu as pltpu
from jax.sharding import Mesh, PartitionSpec as P

FFE = 1408
THETA = 50000.0
EPS = 1e-06
NEG = -1e30

BLK = ("x", "z")
BEAM = ("y", "core")
ROWS_ORDER = BEAM + BLK
OUT_ORDER = BLK + BEAM


def rms_scale(values, gain):
    mean_sq = jnp.mean(values * values, axis=-1, keepdims=True)
    return values * lax.rsqrt(mean_sq + EPS) * gain


def rotate(values, cosine, sine):
    half = values.shape[-1] // 2
    lower, upper = values[..., :half], values[..., half:]
    return jnp.concatenate(
        [lower * cosine - upper * sine, lower * sine + upper * cosine], axis=-1
    )


def shifted(value, axis, size, by):
    return lax.ppermute(value, axis, [(i, (i + by) % size) for i in range(size)])


def gather_blk(value):
    nx, nz = lax.axis_size("x"), lax.axis_size("z")
    along_x = jnp.stack([value] + [shifted(value, "x", nx, s) for s in range(1, nx)])
    both = [along_x] + [shifted(along_x, "z", nz, s) for s in range(1, nz)]
    return jnp.concatenate(both, axis=0)


def attend_kernel(
    info_ref, q_ref, cache_ref, entry_ref, parent_ref, table_ref, wv_ref, out_ref, lat_ref, lse_ref
):
    heads, groups, rows, width = q_ref.shape
    beams, max_blocks = table_ref.shape[1:]
    steps = rows // beams
    pool, block_len = cache_ref.shape[1:3]
    latent = wv_ref.shape[1]
    scale = (width - latent + 128) ** (-0.5)
    blk = info_ref[heads]
    lane = lambda shape: lax.broadcasted_iota(jnp.int32, shape, len(shape) - 1)
    sub = lambda shape: lax.broadcasted_iota(jnp.int32, shape, len(shape) - 2)
    f32 = jnp.float32
    for g in range(groups):
        shape = (beams, 128)
        origin = (lane(shape) == sub(shape)).astype(f32)
        kept = []
        for t in range(steps):
            choose = (lane((beams, beams)) == parent_ref[g, :, t : t + 1]).astype(f32)
            origin = jnp.dot(choose, origin, preferred_element_type=f32)
            origin = origin + (lane(shape) == sub(shape) + beams * (1 + t)).astype(f32)
            kept.append(origin)
        origin = jnp.concatenate(kept, axis=0)
        table = table_ref[g]
        live = lane(table.shape) < info_ref[heads + 1 + g]
        used = jnp.zeros((beams, 128), f32)
        for p in range(pool):
            hit = jnp.where((table == blk * pool + p) & live, 1.0, 0.0)
            hit = jnp.max(hit, axis=1, keepdims=True)
            used = used + jnp.where(lane(used.shape) == p, hit, 0.0)
        used = jnp.dot(origin[:, :beams], used, preferred_element_type=f32)
        bias = jnp.concatenate(
            [jnp.broadcast_to(used[:, p : p + 1], (rows, block_len)) for p in range(pool)], axis=1
        )
        bias = jnp.where(bias > 0.5, 0.0, NEG)
        seen = origin[:, beams : beams + rows]
        recent_bias = jnp.where((seen > 0.5) & (blk == 0), 0.0, NEG)

        q = q_ref[:, g].reshape(heads * rows, width)
        keys = cache_ref[g].reshape(pool * block_len, width)
        entry = entry_ref[g]
        over_width = (((1,), (1,)), ((), ()))
        scores = lax.dot_general(q, keys, over_width, preferred_element_type=f32)
        scores = scores.reshape(heads, rows, pool * block_len) * scale + bias[None]
        recent = lax.dot_general(q, entry, over_width, preferred_element_type=f32)
        recent = recent.reshape(heads, rows, rows) * scale + recent_bias[None]
        top = jnp.maximum(
            jnp.max(scores, axis=-1, keepdims=True), jnp.max(recent, axis=-1, keepdims=True)
        )
        weights = jnp.exp(scores - top)
        recent = jnp.exp(recent - top)
        total = jnp.sum(weights, axis=-1, keepdims=True) + jnp.sum(recent, axis=-1, keepdims=True)
        weights = weights.astype(jnp.bfloat16).reshape(heads * rows, pool * block_len)
        recent = recent.astype(jnp.bfloat16).reshape(heads * rows, rows)
        lat = jnp.dot(weights, keys[:, :latent], preferred_element_type=f32)
        lat = lat + jnp.dot(recent, entry[:, :latent], preferred_element_type=f32)
        lat = lat.reshape(heads, rows, latent) / total
        lat_ref[:, g * rows : (g + 1) * rows, :] = lat.astype(jnp.bfloat16)
        lse = jnp.where(top > 0.1 * NEG, top + jnp.log(total), NEG)
        lse_ref[:, g * rows : (g + 1) * rows, :] = jnp.broadcast_to(lse, (heads, rows, 128))

    rows_all = groups * rows
    diagonal = lane((rows_all, 128)) == sub((rows_all, 128))
    for h in range(heads):
        home = info_ref[h]
        value = jnp.dot(lat_ref[h], wv_ref[home], preferred_element_type=f32)
        out_ref[home, :rows_all, :] = value.astype(jnp.bfloat16)
        line = jnp.sum(jnp.where(diagonal, lse_ref[h], 0.0), axis=0, keepdims=True)
        first = line.astype(jnp.bfloat16).astype(f32)
        second = (line - first).astype(jnp.bfloat16).astype(f32)
        third = line - first - second
        place = sub((16, 128))
        tail = jnp.where(place == 0, first, 0.0)
        tail = jnp.where(place == 1, second, tail)
        tail = jnp.where(place == 2, third, tail)
        out_ref[home, rows_all:, :] = tail.astype(jnp.bfloat16)


def attend(info, queries, cache, entries, parents, tables, w_value):
    heads, groups, rows, _ = queries.shape
    value = w_value.shape[2]
    rows_all = groups * rows
    vmem = pl.BlockSpec(memory_space=pltpu.VMEM)
    return pl.pallas_call(
        attend_kernel,
        out_shape=jax.ShapeDtypeStruct((heads, rows_all + 16, value), jnp.bfloat16),
        in_specs=[pl.BlockSpec(memory_space=pltpu.SMEM)] + [vmem] * 6,
        out_specs=vmem,
        scratch_shapes=[
            pltpu.VMEM((heads, rows_all, w_value.shape[1]), jnp.bfloat16),
            pltpu.VMEM((heads, rows_all, 128), jnp.float32),
        ],
        compiler_params=pltpu.CompilerParams(vmem_limit_bytes=48 << 20),
        name="attend",
    )(info, queries, cache, entries, parents, tables, w_value)


def per_device(
    embeds,
    attn_gain,
    w_query,
    w_latent,
    latent_gain,
    w_key_up,
    w_value_up,
    w_out,
    ffn_gain,
    w_shared_gate,
    w_shared_up,
    w_shared_down,
    w_expert_gate,
    w_expert_up,
    w_expert_down,
    cache_pool,
    block_tables,
    block_counts,
    parents,
    expert_ids,
    expert_weights,
):
    f32, bf16 = jnp.float32, jnp.bfloat16
    steps, row_dev, width = embeds.shape
    groups, beams, _ = block_tables.shape
    head_in, latent = w_key_up.shape[1:]
    entry_width = cache_pool.shape[3]
    block_len = cache_pool.shape[2]
    rope = entry_width - latent
    pair_dev, _, unit_dev = w_expert_gate.shape
    total_rows = expert_ids.shape[1]
    nx, nz = lax.axis_size("x"), lax.axis_size("z")
    blk_size = nx * nz
    x, z = lax.axis_index("x"), lax.axis_index("z")
    blk = lax.axis_index(BLK)
    beam = lax.axis_index(BEAM)

    w_value = lax.all_gather(w_value_up, BLK, axis=0, tiled=True)

    tokens = embeds.reshape(steps, groups, beams, width).transpose(1, 0, 2, 3)
    tokens = tokens.reshape(steps * row_dev, width)
    normed = rms_scale(tokens.astype(f32), attn_gain).astype(bf16)
    queries = jnp.dot(normed, w_query, preferred_element_type=f32).astype(bf16)
    position = (block_counts * block_len).astype(f32)[:, None] + jnp.arange(steps, dtype=f32)
    position = jnp.repeat(position.reshape(-1), beams)
    frequency = THETA ** (-jnp.arange(rope // 2, dtype=f32) * 2.0 / rope)
    angles = position[:, None] * frequency
    cosine, sine = jnp.cos(angles), jnp.sin(angles)
    query_latent = jnp.dot(queries[:, :head_in], w_key_up[0], preferred_element_type=f32)
    query_rope = rotate(queries[:, head_in:].astype(f32), cosine, sine)
    query_full = jnp.concatenate([query_latent, query_rope], axis=-1).astype(bf16)
    all_queries = gather_blk(query_full)

    projected = jnp.dot(normed, w_latent, preferred_element_type=f32)
    entries = jnp.concatenate(
        [rms_scale(projected[:, :latent], latent_gain), rotate(projected[:, latent:], cosine, sine)],
        axis=-1,
    ).astype(bf16)

    near = jnp.arange(blk_size, dtype=jnp.int32)
    homes = (x - near % nx) % nx * nz + (z - near // nx) % nz
    info = jnp.concatenate([homes, blk[None], block_counts]).astype(jnp.int32)
    partial_heads = attend(
        info,
        all_queries.reshape(blk_size, groups, steps * beams, entry_width),
        cache_pool,
        entries.reshape(groups, steps * beams, entry_width),
        parents.transpose(1, 2, 0),
        block_tables,
        w_value,
    )
    rows_all = steps * row_dev
    parts = lax.all_to_all(partial_heads, BLK, 0, 0)
    lse = jnp.sum(parts[:, rows_all : rows_all + 3, :rows_all].astype(f32), axis=1)
    share = jnp.exp(lse - jnp.max(lse, axis=0))
    share = share / jnp.sum(share, axis=0)
    head_out = jnp.sum(parts[:, :rows_all].astype(f32) * share[:, :, None], axis=0).astype(bf16)
    head_out = head_out.reshape(groups, steps, beams, -1).transpose(0, 2, 1, 3)
    attn_part = jnp.dot(head_out.reshape(rows_all, -1), w_out, preferred_element_type=f32)
    attn_part = attn_part.astype(bf16).reshape(row_dev, steps, width)
    attn_total = jnp.sum(lax.all_to_all(attn_part, BLK, 0, 0).astype(f32), axis=0)
    own_tokens = lax.dynamic_slice_in_dim(embeds, blk, 1, 1)[:, 0].astype(f32)
    resid = own_tokens + attn_total
    ffn_in = rms_scale(resid, ffn_gain).astype(bf16)

    spread = jnp.broadcast_to(ffn_in, (total_rows, steps, width))
    all_rows = lax.all_to_all(spread, ROWS_ORDER, 0, 0).reshape(total_rows * steps, width)

    pair_half = beam * unit_dev // FFE
    local_experts = (blk * pair_dev + jnp.arange(pair_dev, dtype=jnp.int32)) * 2 + pair_half
    matches = expert_ids[:, :, :, None] == local_experts
    row_weight = jnp.sum(jnp.where(matches, expert_weights[:, :, :, None], 0.0), axis=2)
    row_weight = row_weight.transpose(1, 0, 2).reshape(total_rows * steps, pair_dev)
    total = None
    for e in range(pair_dev):
        gate_val = jnp.dot(all_rows, w_expert_gate[e], preferred_element_type=f32)
        up_val = jnp.dot(all_rows, w_expert_up[e], preferred_element_type=f32)
        activation = (jax.nn.silu(gate_val) * up_val * row_weight[:, e : e + 1]).astype(bf16)
        down = jnp.dot(activation, w_expert_down[e], preferred_element_type=f32)
        total = down if total is None else total + down

    beam_rows = lax.dynamic_slice_in_dim(all_rows, beam * rows_all, rows_all, 0)
    shared_act = (
        jax.nn.silu(jnp.dot(beam_rows, w_shared_gate, preferred_element_type=f32))
        * jnp.dot(beam_rows, w_shared_up, preferred_element_type=f32)
    ).astype(bf16)
    own = jnp.dot(shared_act, w_shared_down, preferred_element_type=f32)
    own_resid = lax.dynamic_update_slice_in_dim(jnp.zeros_like(own), resid, blk * steps, 0)
    own = own + own_resid
    held = lax.dynamic_slice_in_dim(total, beam * rows_all, rows_all, 0)
    total = lax.dynamic_update_slice_in_dim(total, held + own, beam * rows_all, 0)
    total = total.astype(bf16).reshape(total_rows, steps, width)
    result = jnp.sum(lax.all_to_all(total, OUT_ORDER, 0, 0).astype(f32), axis=0)
    return result[:, None]


def solution(mesh):
    devices = mesh.devices.reshape(4, 4, 4, 2)
    split = Mesh(devices, ("x", "z", "y", "core"))
    placed = (
        P(None, BEAM, None),
        P(),
        P(None, BLK),
        P(),
        P(),
        P(BLK, None, None),
        P(BLK, None, None),
        P(BLK, None),
        P(),
        P(None, BLK),
        P(None, BLK),
        P(BLK, None),
        P(BLK, None, BEAM),
        P(BLK, None, BEAM),
        P(BLK, BEAM, None),
        P(BEAM, BLK, None, None),
        P(BEAM, None, None),
        P(BEAM),
        P(None, BEAM, None),
        P(),
        P(),
    )
    return jax.shard_map(
        per_device,
        mesh=split,
        in_specs=placed,
        out_specs=P(None, OUT_ORDER, None),
        check_vma=False,
    )
```

```python
import functools

import jax
import jax.numpy as jnp
import numpy as np
from jax import lax
from jax.experimental import pallas as pl
from jax.experimental.pallas import tpu as pltpu
from jax.sharding import Mesh, PartitionSpec as P

FFE = 1408
THETA = 50000.0
EPS = 1e-06
NEG = -1e30
CAPACITY = 24
SLOTS = 4 * CAPACITY
OWN_ROWS = 64

BLK = ("x", "z")
BEAM = ("y", "core")
OUT_ORDER = BLK + BEAM
CORES = [(0, 1), (1, 0)]

f32, bf16 = jnp.float32, jnp.bfloat16
LAST = (((1,), (1,)), ((), ()))


def lanes(shape):
    return lax.broadcasted_iota(jnp.int32, shape, len(shape) - 1)


def sublanes(shape):
    return lax.broadcasted_iota(jnp.int32, shape, len(shape) - 2)


def kernel_call(body, name, outs, scratch, cost, smem, *args):
    vmem = pl.BlockSpec(memory_space=pltpu.VMEM)
    first = [pl.BlockSpec(memory_space=pltpu.SMEM)] if smem else []
    return pl.pallas_call(
        body,
        out_shape=[jax.ShapeDtypeStruct(shape, dtype) for shape, dtype in outs],
        in_specs=first + [vmem] * (len(args) - len(first)),
        out_specs=[vmem] * len(outs),
        scratch_shapes=scratch,
        compiler_params=pltpu.CompilerParams(vmem_limit_bytes=24 << 20),
        cost_estimate=pl.CostEstimate(flops=cost[0], bytes_accessed=cost[1], transcendentals=cost[2]),
        name=name,
    )(*args)


def shifted(value, axis, by):
    size = lax.axis_size(axis)
    return lax.ppermute(value, axis, [(i, (i + by) % size) for i in range(size)])


def gather_blk(value, near, far):
    first = jnp.stack([value] + [shifted(value, near, s) for s in range(1, 4)])
    return [first] + [shifted(first, far, s) for s in range(1, 4)]


def rope_parts(cos_ref, rows):
    cosine, sine = cos_ref[:, :64], cos_ref[:, 64:]
    wide = lambda v: jnp.concatenate([jnp.broadcast_to(v[k : k + 1], (8, 64)) for k in range(rows // 8)], axis=0)
    return wide(cosine), wide(sine)


def turned(values, precision=None):
    i, j = sublanes((64, 64)), lanes((64, 64))
    turn = jnp.where(i == j - 32, 1.0, 0.0) - jnp.where(i == j + 32, 1.0, 0.0)
    return jnp.dot(values, turn.astype(values.dtype), precision=precision, preferred_element_type=f32)


def query_kernel(embeds_ref, gain_ref, query_ref, key_up_ref, cos_ref, first_ref, second_ref, normed_ref):
    steps, _, width = embeds_ref.shape
    tokens = [embeds_ref[t].astype(f32) for t in range(steps)]
    tokens = jnp.concatenate([tokens[t][8 * g : 8 * g + 8] for g in range(2) for t in range(steps)], axis=0)
    mean_sq = jnp.sum(tokens * tokens, axis=1, keepdims=True) * (1.0 / width)
    normed = (tokens * lax.rsqrt(mean_sq + EPS) * gain_ref[...]).astype(bf16)
    normed_ref[...] = normed
    queries = lax.dot_general(normed, query_ref[...], LAST, preferred_element_type=f32).astype(bf16)
    latent = jnp.dot(queries[:, :128], key_up_ref[0], preferred_element_type=f32).astype(bf16)
    rope = queries[:, 128:]
    cosine, sine = rope_parts(cos_ref, 64)
    rope = (rope.astype(f32) * cosine + turned(rope) * sine).astype(bf16)
    for g, ref in enumerate((first_ref, second_ref)):
        ref[:, :512] = latent[32 * g : 32 * g + 32]
        ref[:, 512:] = rope[32 * g : 32 * g + 32]


def entry_kernel(normed_ref, latent_ref, gain_ref, cos_ref, out_ref):
    projected = lax.dot_general(normed_ref[...], latent_ref[...], LAST, preferred_element_type=f32)
    latent, rope = projected[:, :512], projected[:, 512:]
    mean_sq = jnp.sum(latent * latent, axis=1, keepdims=True) * (1.0 / 512)
    out_ref[:, :512] = (latent * lax.rsqrt(mean_sq + EPS) * gain_ref[...]).astype(bf16)
    cosine, sine = rope_parts(cos_ref, 64)
    out_ref[:, 512:] = (rope * cosine + turned(rope, lax.Precision.HIGHEST) * sine).astype(bf16)


def split_terms(line):
    first = line.astype(bf16).astype(f32)
    second = (line - first).astype(bf16).astype(f32)
    third = line - first - second
    place = sublanes((16, line.shape[1]))
    tile = jnp.where(place == 0, first, 0.0)
    tile = jnp.where(place == 1, second, tile)
    return jnp.where(place == 2, third, tile).astype(bf16)


def joined_terms(tile):
    tile = tile.astype(f32)
    return tile[0:1] + tile[1:2] + tile[2:3]


def as_line(column, offset=0):
    shape = (column.shape[0], 128)
    return jnp.sum(jnp.where(lanes(shape) == sublanes(shape) + offset, column, 0.0), axis=0, keepdims=True)


def as_column(line, count, offset=0):
    shape = (count, 128)
    return jnp.sum(jnp.where(lanes(shape) == sublanes(shape) + offset, line, 0.0), axis=1, keepdims=True)


def attend_kernel(g, info_ref, *refs):
    q_refs = refs[:4]
    cache_ref, entry_ref, parent_ref, table_ref = refs[4:8]
    out_refs = refs[8:]
    near, rows, width = q_refs[0].shape
    heads = 4 * near
    beams = table_ref.shape[1]
    steps = rows // beams
    pool, _, block_len = cache_ref.shape[1:]
    latent = out_refs[0].shape[1]
    scale = (width - latent + 128) ** (-0.5)
    blk = info_ref[0]
    shape = (beams, 128)
    origin = (lanes(shape) == sublanes(shape)).astype(f32)
    kept = []
    for t in range(steps):
        choose = (lanes((beams, beams)) == parent_ref[g, :, t : t + 1]).astype(f32)
        origin = jnp.dot(choose, origin, preferred_element_type=f32)
        origin = origin + (lanes(shape) == sublanes(shape) + beams * (1 + t)).astype(f32)
        kept.append(origin)
    origin = jnp.concatenate(kept, axis=0)
    table = table_ref[g]
    live = lanes(table.shape) < info_ref[1 + g]
    used = jnp.zeros((beams, 128), f32)
    for p in range(pool):
        hit = jnp.where((table == blk * pool + p) & live, 1.0, 0.0)
        hit = jnp.max(hit, axis=1, keepdims=True)
        used = used + jnp.where(lanes(used.shape) == p, hit, 0.0)
    used = jnp.dot(origin[:, :beams], used, preferred_element_type=f32)
    bias = jnp.concatenate(
        [jnp.broadcast_to(used[:, p : p + 1], (rows, block_len)) for p in range(pool)], axis=1
    )
    bias = jnp.where(bias > 0.5, 0.0, NEG)
    seen = origin[:, beams : beams + rows]
    recent_bias = jnp.where((seen > 0.5) & (blk == 0), 0.0, NEG)

    q = jnp.concatenate([ref[...] for ref in q_refs], axis=0).reshape(heads * rows, width)
    keys = jnp.concatenate([cache_ref[g, p] for p in range(pool)], axis=1)
    entry = entry_ref[g * rows : (g + 1) * rows]
    scores = jnp.dot(q, keys, preferred_element_type=f32)
    scores = scores.reshape(heads, rows, pool * block_len) * scale + bias[None]
    recent = lax.dot_general(q, entry, LAST, preferred_element_type=f32)
    recent = recent.reshape(heads, rows, rows) * scale + recent_bias[None]
    top = jnp.maximum(
        jnp.max(scores, axis=-1, keepdims=True), jnp.max(recent, axis=-1, keepdims=True)
    )
    weights = jnp.exp(scores - top)
    recent = jnp.exp(recent - top)
    total = jnp.sum(weights, axis=-1, keepdims=True) + jnp.sum(recent, axis=-1, keepdims=True)
    weights = weights.astype(bf16).reshape(heads * rows, pool * block_len)
    recent = recent.astype(bf16).reshape(heads * rows, rows)
    lat = lax.dot_general(weights, keys[:latent], LAST, preferred_element_type=f32)
    lat = lat + jnp.dot(recent, entry[:, :latent], preferred_element_type=f32)
    lat = (lat.reshape(heads, rows, latent) / total).astype(bf16)
    lse = jnp.where(top > 0.1 * NEG, top + jnp.log(total), NEG)
    for s, ref in enumerate(out_refs):
        for f in range(4):
            ref[f * rows : (f + 1) * rows, :] = lat[f * near + s]
        column = jnp.concatenate([lse[f * near + s] for f in range(4)], axis=0)
        ref[4 * rows :, :128] = split_terms(as_line(column))
        ref[4 * rows :, 128:] = jnp.zeros((16, latent - 128), bf16)


def shares(sums):
    best = functools.reduce(jnp.maximum, sums)
    parts = [jnp.exp(v - best) for v in sums]
    whole = functools.reduce(jnp.add, parts)
    return [p / whole for p in parts], best + jnp.log(whole)


def merge_kernel(*refs):
    parts, outs = refs[:4], refs[4:]
    part_share, whole = shares([joined_terms(ref[128:, :128]) for ref in parts])
    merged = sum(as_column(p, 128) * ref[:128, :].astype(f32) for p, ref in zip(part_share, parts))
    merged = merged.astype(bf16)
    tile = split_terms(whole)
    for f, ref in enumerate(outs):
        ref[:32, :] = merged[32 * f : 32 * f + 32]
        ref[32:, :128] = tile
        ref[32:, 128:] = jnp.zeros((16, ref.shape[1] - 128), bf16)


def output_kernel(*refs):
    value_ref, out_ref, result_ref = refs[8:]
    joined = []
    for g in range(2):
        parts = refs[4 * g : 4 * g + 4]
        lines = [joined_terms(ref[32:, :128]) for ref in parts]
        columns = [as_column(line, 32, 32 * f) for f, line in enumerate(lines)]
        part_share, _ = shares(columns)
        joined.append(sum(p * ref[:32, :].astype(f32) for p, ref in zip(part_share, parts)))
    attended = jnp.concatenate(joined, axis=0).astype(bf16)
    head_out = jnp.dot(attended, value_ref[0], preferred_element_type=f32).astype(bf16)
    line, row = sublanes((128, 64)), lanes((128, 64))
    source = 32 * (line >> 6) + 8 * ((line >> 1) & 3) + ((line >> 3) & 7)
    result = None
    for q in range(2):
        take = jnp.where((source == row) & ((line & 1) == q), 1.0, 0.0).astype(bf16)
        rows = jnp.dot(take, head_out, preferred_element_type=f32).astype(bf16)
        term = jnp.dot(rows, out_ref[:, q * 1024 : (q + 1) * 1024], preferred_element_type=f32)
        result = term if result is None else result + term
    result_ref[...] = result.astype(bf16)


def norm_kernel(info_ref, parts_ref, embeds_ref, gain_ref, spread_ref, resid_ref):
    blk = info_ref[1]
    steps, rows, width = embeds_ref.shape
    half = width // 2
    line = sublanes((2 * steps, half))
    resid = jnp.sum(parts_ref[...].astype(f32), axis=0)
    gain = jnp.zeros((2 * steps, half), f32)
    for q in range(2):
        columns = slice(q * half, (q + 1) * half)
        gain = gain + jnp.where((line & 1) == q, gain_ref[:, columns], 0.0)
        for t in range(steps):
            token = jnp.where(sublanes((rows, half)) == blk, embeds_ref[t, :, columns].astype(f32), 0.0)
            token = jnp.sum(token, axis=0, keepdims=True)
            resid = resid + jnp.where(line == 2 * t + q, token, 0.0)
    resid_ref[...] = resid
    sums = jnp.broadcast_to(jnp.sum(resid * resid, axis=1, keepdims=True), (2 * steps, 128))
    pair = jnp.where((sublanes((8, 8)) >> 1) == (lanes((8, 8)) >> 1), 1.0, 0.0)
    sums = jnp.dot(pair, sums, precision=lax.Precision.HIGHEST, preferred_element_type=f32)
    normed = (resid * lax.rsqrt(sums[:, :1] * (1.0 / width) + EPS) * gain).astype(bf16)
    spread_ref[...] = jnp.broadcast_to(normed[None], spread_ref.shape)


def line_row(line, core):
    chip = (line >> 3) & 63
    return 32 * (chip >> 4) + 16 * ((line >> 9) ^ core) + (chip & 15)


def route_kernel(info_ref, ids_ref, weights_ref, out_ref):
    core = info_ref[0]
    top, steps, rows = ids_ref.shape
    line = lanes((rows, out_ref.shape[1]))
    row = line_row(line, core)
    earlier = jnp.where(sublanes((rows, rows)) < lanes((rows, rows)), 1.0, 0.0).astype(bf16)
    slots, weights = [], []
    for e in range(2):
        expert = info_ref[3 + e]
        weight = jnp.zeros((steps, rows), f32)
        routed = jnp.zeros((steps, rows), f32)
        for k in range(top):
            match = ids_ref[k] == expert
            weight = weight + jnp.where(match, weights_ref[k], 0.0)
            routed = routed + jnp.where(match, 1.0, 0.0)
        wide = jnp.concatenate([routed, jnp.zeros((8 - steps, rows), f32)], axis=0).astype(bf16)
        rank = jnp.dot(wide, earlier, preferred_element_type=f32)[:steps]
        first = (sublanes((steps, rows)) * CAPACITY + 1).astype(f32)
        slots.append(jnp.where(routed > 0.5, rank + first, 0.0))
        weights.append(weight)
    total = jnp.zeros(out_ref.shape, f32)
    for t in range(steps):
        place = sublanes((8, rows))
        values = jnp.zeros((8, rows), f32)
        for k, value in enumerate(slots + weights):
            values = jnp.where(place == k, value[t : t + 1], values)
        take = jnp.where((sublanes(line.shape) == row) & (((line >> 1) & 3) == t), 1.0, 0.0)
        total = total + jnp.dot(values, take, precision=lax.Precision.HIGHEST, preferred_element_type=f32)
    out_ref[...] = total


def moe_kernel(
    info_ref,
    mine_ref,
    other_ref,
    route_ref,
    resid_ref,
    gate_ref,
    up_ref,
    down_ref,
    shared_gate_ref,
    shared_up_ref,
    shared_down_ref,
    own_out_ref,
    other_out_ref,
    x_ref,
    y_ref,
):
    f32, bf16 = jnp.float32, jnp.bfloat16
    core, blk, y = info_ref[0], info_ref[1], info_ref[2]
    lines, half = mine_ref.shape
    experts, units, width = gate_ref.shape
    slots, own_rows = SLOTS, OWN_ROWS
    total = experts * slots + own_rows
    line = lanes((1, 2 * lines))
    step = (line >> 1) & 3
    row = line_row(line, core)
    place = ((row & 1) ^ core) * (lines // 2) + (row >> 1) * 4 + step
    first = (line & 1) == 0

    hits = []
    for e in range(experts):
        slot = sublanes((slots, 2 * lines)) + 1
        hits.append(slot == route_ref[e : e + 1, :].astype(jnp.int32))
    own_line = jnp.where(line < lines, (line >> 1) - y * own_rows, -1)
    hits.append(sublanes((own_rows, 2 * lines)) == own_line)
    weights = [
        jnp.sum(jnp.where(hits[e] & first, route_ref[experts + e : experts + e + 1, :], 0.0), axis=1, keepdims=True)
        for e in range(experts)
    ]
    hit = jnp.concatenate([jnp.where(h, 1.0, 0.0) for h in hits], axis=0)
    for q in range(2):
        pick = jnp.where((line & 1) == q, hit, 0.0).astype(bf16)
        rows = jnp.dot(pick[:, :lines], mine_ref[...], preferred_element_type=f32)
        rows = rows + jnp.dot(pick[:, lines:], other_ref[...], preferred_element_type=f32)
        x_ref[:, q * half : (q + 1) * half] = rows.astype(bf16)
    parts = place + 1
    parts = jnp.where(sublanes((8, 2 * lines)) == 0, parts >> 4, parts & 15).astype(f32)
    parts = jnp.where(first, parts, 0.0).astype(bf16)
    spot = lax.dot_general(parts, hit.astype(bf16), LAST, preferred_element_type=f32)
    spot = (spot[0:1] * 16.0 + spot[1:2] - 1.0).astype(jnp.int32)

    def gated(x, gate, up):
        gate_val = lax.dot_general(x, gate, LAST, preferred_element_type=f32)
        up_val = lax.dot_general(x, up, LAST, preferred_element_type=f32)
        return (gate_val / (1.0 + jnp.exp(-gate_val)) * up_val).astype(bf16)

    for e in range(experts):
        part = slice(e * slots, (e + 1) * slots)
        act = gated(x_ref[part, :], gate_ref[e], up_ref[e])
        down = jnp.dot(act, down_ref[e], preferred_element_type=f32)
        y_ref[part, :] = (down * weights[e]).astype(bf16)
    part = slice(experts * slots, total)
    act = gated(x_ref[part, :], shared_gate_ref[...], shared_up_ref[...])
    own = jnp.dot(act, shared_down_ref[...], preferred_element_type=f32)
    for t in range(4):
        whole = jnp.concatenate([resid_ref[2 * t + q : 2 * t + q + 1, :] for q in range(2)], axis=1)
        own = own + jnp.where(sublanes((own_rows, 1)) == blk * 4 + t, whole, 0.0)
    y_ref[part, :] = own.astype(bf16)

    for side, ref in ((0, own_out_ref), (1, other_out_ref)):
        out_line = sublanes((lines, 1))
        out_place = (out_line >> 1) + side * (lines // 2)
        put = jnp.where(out_place == spot, 1.0, 0.0)
        result = None
        for q in range(2):
            put_q = jnp.where((out_line & 1) == q, put, 0.0).astype(bf16)
            term = jnp.dot(put_q, y_ref[:, q * half : (q + 1) * half], preferred_element_type=f32)
            result = term if result is None else result + term
        ref[...] = result.astype(bf16)


def per_device(
    embeds,
    attn_gain,
    w_query,
    w_latent,
    latent_gain,
    w_key_up,
    w_value_up,
    w_out,
    ffn_gain,
    w_shared_gate,
    w_shared_up,
    w_shared_down,
    w_expert_gate,
    w_expert_up,
    w_expert_down,
    cache_pool,
    block_tables,
    block_counts,
    parents,
    expert_ids,
    expert_weights,
):
    steps, row_dev, width = embeds.shape
    groups, beams, _ = block_tables.shape
    latent = w_key_up.shape[2]
    block_len, entry_width = cache_pool.shape[2:]
    rope = entry_width - latent
    pair_dev, _, unit_dev = w_expert_gate.shape
    half = width // 2
    chips = expert_ids.shape[1] // 2
    lines = chips * 2 * steps
    y, core = lax.axis_index("y"), lax.axis_index("core")
    blk, beam = lax.axis_index(BLK), lax.axis_index(BEAM)
    expert = blk * pair_dev * 2 + beam * unit_dev // FFE
    place = jnp.stack([core, blk, y, expert, expert + 2]).astype(jnp.int32)
    counts = jnp.concatenate([blk[None], block_counts]).astype(jnp.int32)

    position = (block_counts * block_len).astype(f32)[:, None] + jnp.arange(steps, dtype=f32)
    frequency = np.float64(THETA) ** (-np.arange(rope // 2) * 2.0 / rope)
    frequency = np.tile(frequency.astype(np.float32), 4)
    turn = np.repeat(np.array([0.0, 1.0], np.float32), rope)
    angles = position.reshape(-1, 1) * frequency
    cosines = jnp.where(turn == 0.0, jnp.cos(angles), jnp.sin(angles))
    rows_group = steps * beams
    rows_all = groups * rows_group
    query = ((rows_group, entry_width), bf16)
    first, second, normed = kernel_call(
        query_kernel,
        "query",
        [query, query, ((rows_all, width), bf16)],
        [],
        (60_000_000, 1_500_000, 0),
        False,
        embeds,
        attn_gain.reshape(1, width),
        w_query.T,
        w_key_up,
        cosines,
    )
    queries = (gather_blk(first, "x", "z"), gather_blk(second, "z", "x"))
    (entries,) = kernel_call(
        entry_kernel,
        "entry",
        [((rows_all, entry_width), bf16)],
        [],
        (150_000_000, 2_700_000, 0),
        False,
        normed,
        w_latent.T,
        latent_gain.reshape(1, latent),
        cosines,
    )
    (route,) = kernel_call(
        route_kernel,
        "route",
        [((8, 2 * lines), f32)],
        [],
        (60_000_000, 60_000, 0),
        True,
        place,
        expert_ids.transpose(2, 0, 1),
        expert_weights.transpose(2, 0, 1),
    )
    cache = cache_pool.transpose(0, 1, 3, 2)
    ancestry = parents.transpose(1, 2, 0)
    part = ((4 * rows_group + 16, latent), bf16)
    last = ((rows_group + 16, latent), bf16)
    final = []
    for g, (near, far) in enumerate((("x", "z"), ("z", "x"))):
        parts = kernel_call(
            functools.partial(attend_kernel, g),
            "attend",
            [part] * 4,
            [],
            (900_000_000, 2_500_000, 400_000),
            True,
            counts,
            *queries[g],
            cache,
            entries,
            ancestry,
            block_tables,
        )
        parts = [parts[0]] + [shifted(parts[s], near, -s) for s in range(1, 4)]
        merged = kernel_call(merge_kernel, "merge", [last] * 4, [], (2_000_000, 800_000, 1_000), False, *parts)
        final += [merged[0]] + [shifted(merged[f], far, -f) for f in range(1, 4)]
    (attn_part,) = kernel_call(
        output_kernel,
        "output",
        [((row_dev * 2 * steps, half), bf16)],
        [],
        (80_000_000, 1_500_000, 1_000),
        False,
        *final,
        w_value_up,
        w_out,
    )
    attn_part = lax.all_to_all(attn_part.reshape(row_dev, 2 * steps, half), BLK, 0, 0)
    spread, resid = kernel_call(
        norm_kernel,
        "norm",
        [((chips, 2 * steps, half), bf16), ((2 * steps, half), f32)],
        [],
        (1_000_000, 1_700_000, 0),
        True,
        place,
        attn_part,
        embeds,
        ffn_gain.reshape(1, width),
    )

    mine = lax.all_to_all(spread, ("y", "x", "z"), 0, 0).reshape(lines, half)
    other = lax.ppermute(mine, "core", CORES)
    total = pair_dev * SLOTS + OWN_ROWS
    own_out, other_out = kernel_call(
        moe_kernel,
        "moe",
        [((lines, half), bf16)] * 2,
        [pltpu.VMEM((total, width), bf16)] * 2,
        (4_000_000_000, 15_000_000, 300_000),
        True,
        place,
        mine,
        other,
        route,
        resid,
        w_expert_gate.transpose(0, 2, 1),
        w_expert_up.transpose(0, 2, 1),
        w_expert_down,
        w_shared_gate.T,
        w_shared_up.T,
        w_shared_down,
    )
    own_out = own_out.astype(f32) + lax.ppermute(other_out, "core", CORES).astype(f32)
    own_out = own_out.astype(bf16).reshape(chips, 2 * steps, half)
    result = jnp.sum(lax.all_to_all(own_out, ("x", "z", "y"), 0, 0).astype(f32), axis=0)
    return result.reshape(steps, 1, width)


def solution(mesh):
    devices = mesh.devices.reshape(4, 4, 4, 2)
    split = Mesh(devices, ("x", "z", "y", "core"))
    placed = (
        P(None, BEAM, None),
        P(),
        P(None, BLK),
        P(),
        P(),
        P(BLK, None, None),
        P(BLK, None, None),
        P(BLK, None),
        P(),
        P(None, BLK),
        P(None, BLK),
        P(BLK, None),
        P(BLK, None, BEAM),
        P(BLK, None, BEAM),
        P(BLK, BEAM, None),
        P(BEAM, BLK, None, None),
        P(BEAM, None, None),
        P(BEAM),
        P(None, BEAM, None),
        P(),
        P(),
    )
    return jax.shard_map(
        per_device,
        mesh=split,
        in_specs=placed,
        out_specs=P(None, OUT_ORDER, None),
        check_vma=False,
    )
```

```python
import functools

import jax
import jax.numpy as jnp
import numpy as np
from jax import lax
from jax.experimental import pallas as pl
from jax.experimental.pallas import tpu as pltpu
from jax.sharding import Mesh, PartitionSpec as P

FFE = 1408
THETA = 50000.0
EPS = 1e-06
NEG = -1e30
CAPACITY = 24
SLOTS = 4 * CAPACITY
OWN_ROWS = 64

BLK = ("x", "z")
BEAM = ("y", "core")
OUT_ORDER = BLK + BEAM
CORES = [(0, 1), (1, 0)]
SCALARS = (pltpu.SMEM,)

f32, bf16 = jnp.float32, jnp.bfloat16
LAST = (((1,), (1,)), ((), ()))


def lanes(shape):
    return lax.broadcasted_iota(jnp.int32, shape, len(shape) - 1)


def sublanes(shape):
    return lax.broadcasted_iota(jnp.int32, shape, len(shape) - 2)


def kernel_call(body, name, outs, scratch, cost, first, *args):
    vmem = pl.BlockSpec(memory_space=pltpu.VMEM)
    first = [pl.BlockSpec(memory_space=space) for space in first]
    return pl.pallas_call(
        body,
        out_shape=[jax.ShapeDtypeStruct(shape, dtype) for shape, dtype in outs],
        in_specs=first + [vmem] * (len(args) - len(first)),
        out_specs=[vmem] * len(outs),
        scratch_shapes=scratch,
        compiler_params=pltpu.CompilerParams(vmem_limit_bytes=24 << 20),
        cost_estimate=pl.CostEstimate(flops=cost[0], bytes_accessed=cost[1], transcendentals=cost[2]),
        name=name,
    )(*args)


def fetch(sources, targets, sems):
    copies = [pltpu.make_async_copy(a, b, sems.at[k]) for k, (a, b) in enumerate(zip(sources, targets))]
    for copy in copies:
        copy.start()
    return copies


def in_hbm(*arrays):
    return [pltpu.with_memory_space_constraint(a, pltpu.HBM) for a in arrays]


def room_for(arrays):
    return [pltpu.VMEM(a.shape, a.dtype) for a in arrays] + [pltpu.SemaphoreType.DMA((len(arrays),))]


def shifted(value, axis, by):
    size = lax.axis_size(axis)
    return lax.ppermute(value, axis, [(i, (i + by) % size) for i in range(size)])


def gather(value, axis):
    arrived = {s: shifted(value, axis, s) for s in (1, 3, 2)}
    return [value] + [arrived[s] for s in range(1, 4)]


def rope_parts(cos_ref, rows):
    cosine, sine = cos_ref[:, :64], cos_ref[:, 64:]
    wide = lambda v: jnp.concatenate([jnp.broadcast_to(v[k : k + 1], (8, 64)) for k in range(rows // 8)], axis=0)
    return wide(cosine), wide(sine)


def turned(values, precision=None):
    i, j = sublanes((64, 64)), lanes((64, 64))
    turn = jnp.where(i == j - 32, 1.0, 0.0) - jnp.where(i == j + 32, 1.0, 0.0)
    return jnp.dot(values, turn.astype(values.dtype), precision=precision, preferred_element_type=f32)


def query_kernel(
    embeds_hbm, query_hbm, key_up_hbm, gain_hbm, frequency_hbm, counts_hbm,
    first_ref, second_ref, normed_ref, cos_ref,
    embeds_ref, query_ref, key_up_ref, gain_ref, frequency_ref, counts_ref, sems,
):
    steps, _, width = embeds_ref.shape
    copies = fetch(
        (embeds_hbm, query_hbm, key_up_hbm, gain_hbm, frequency_hbm, counts_hbm),
        (embeds_ref, query_ref, key_up_ref, gain_ref, frequency_ref, counts_ref),
        sems,
    )
    copies[4].wait()
    copies[5].wait()
    line = sublanes((8, 128))
    position = jnp.where(line < steps, counts_ref[0], counts_ref[1]) * 128 + (line & (steps - 1))
    angles = position.astype(f32) * frequency_ref[...]
    cos_ref[...] = jnp.where(lanes((8, 128)) < 64, jnp.cos(angles), jnp.sin(angles))
    copies[0].wait()
    copies[3].wait()
    tokens = [embeds_ref[t].astype(f32) for t in range(steps)]
    tokens = jnp.concatenate([tokens[t][8 * g : 8 * g + 8] for g in range(2) for t in range(steps)], axis=0)
    mean_sq = jnp.sum(tokens * tokens, axis=1, keepdims=True) * (1.0 / width)
    normed = (tokens * lax.rsqrt(mean_sq + EPS) * gain_ref[...]).astype(bf16)
    normed_ref[...] = normed
    copies[1].wait()
    queries = lax.dot_general(normed, query_ref[...], LAST, preferred_element_type=f32).astype(bf16)
    copies[2].wait()
    latent = jnp.dot(queries[:, :128], key_up_ref[0], preferred_element_type=f32).astype(bf16)
    rope = queries[:, 128:]
    cosine, sine = rope_parts(cos_ref, 64)
    rope = (rope.astype(f32) * cosine + turned(rope) * sine).astype(bf16)
    for g, ref in enumerate((first_ref, second_ref)):
        ref[:, :512] = latent[32 * g : 32 * g + 32]
        ref[:, 512:] = rope[32 * g : 32 * g + 32]


def entry_kernel(normed_ref, latent_ref, gain_ref, cos_ref, out_ref):
    projected = lax.dot_general(normed_ref[...], latent_ref[...], LAST, preferred_element_type=f32)
    latent, rope = projected[:, :512], projected[:, 512:]
    mean_sq = jnp.sum(latent * latent, axis=1, keepdims=True) * (1.0 / 512)
    out_ref[:, :512] = (latent * lax.rsqrt(mean_sq + EPS) * gain_ref[...]).astype(bf16)
    cosine, sine = rope_parts(cos_ref, 64)
    out_ref[:, 512:] = (rope * cosine + turned(rope, lax.Precision.HIGHEST) * sine).astype(bf16)


def split_terms(line):
    first = line.astype(bf16).astype(f32)
    second = (line - first).astype(bf16).astype(f32)
    third = line - first - second
    place = sublanes((8, line.shape[1]))
    tile = jnp.where(place == 0, first, 0.0)
    tile = jnp.where(place == 1, second, tile)
    return jnp.where(place == 2, third, tile).astype(bf16)


def joined_terms(tile):
    tile = tile.astype(f32)
    return tile[0:1] + tile[1:2] + tile[2:3]


def as_line(column, offset=0):
    shape = (column.shape[0], 128)
    return jnp.sum(jnp.where(lanes(shape) == sublanes(shape) + offset, column, 0.0), axis=0, keepdims=True)


def as_column(line, count, offset=0):
    shape = (count, 128)
    return jnp.sum(jnp.where(lanes(shape) == sublanes(shape) + offset, line, 0.0), axis=1, keepdims=True)


def attend_kernel(info_ref, *refs):
    q_refs = (refs[:4], refs[4:8])
    cache_ref, entry_ref, parent_ref, table_ref, out_ref, sum_ref = refs[8:]
    near, rows, width = q_refs[0][0].shape
    heads = 4 * near
    groups, beams, _ = table_ref.shape
    pool, _, block_len = cache_ref.shape[1:]
    latent = out_ref.shape[2]
    steps = rows // beams
    scale = (width - latent + 128) ** (-0.5)
    blk = info_ref[0]
    for g in range(groups):
        shape = (beams, 128)
        origin = (lanes(shape) == sublanes(shape)).astype(f32)
        kept = []
        for t in range(steps):
            diagonal = lanes((beams, beams)) == sublanes((beams, beams))
            parent = jnp.where(diagonal, parent_ref[t, g : g + 1, :].astype(f32), 0.0)
            parent = jnp.sum(parent, axis=1, keepdims=True).astype(jnp.int32)
            choose = (lanes((beams, beams)) == parent).astype(f32)
            origin = jnp.dot(choose, origin, preferred_element_type=f32)
            origin = origin + (lanes(shape) == sublanes(shape) + beams * (1 + t)).astype(f32)
            kept.append(origin)
        origin = jnp.concatenate(kept, axis=0)
        table = table_ref[g]
        live = lanes(table.shape) < info_ref[1 + g]
        used = jnp.zeros((beams, 128), f32)
        for p in range(pool):
            hit = jnp.where((table == blk * pool + p) & live, 1.0, 0.0)
            hit = jnp.max(hit, axis=1, keepdims=True)
            used = used + jnp.where(lanes(used.shape) == p, hit, 0.0)
        used = jnp.dot(origin[:, :beams], used, preferred_element_type=f32)
        bias = jnp.concatenate(
            [jnp.broadcast_to(used[:, p : p + 1], (rows, block_len)) for p in range(pool)], axis=1
        )
        bias = jnp.where(bias > 0.5, 0.0, NEG)
        seen = origin[:, beams : beams + rows]
        recent_bias = jnp.where((seen > 0.5) & (blk == 0), 0.0, NEG)

        part = slice(g * rows, (g + 1) * rows)
        q = jnp.concatenate([ref[...] for ref in q_refs[g]], axis=0).reshape(heads * rows, width)
        keys = jnp.concatenate([cache_ref[g, p] for p in range(pool)], axis=1)
        entry = entry_ref[part]
        scores = jnp.dot(q, keys, preferred_element_type=f32)
        scores = scores.reshape(heads, rows, pool * block_len) * scale + bias[None]
        recent = lax.dot_general(q, entry, LAST, preferred_element_type=f32)
        recent = recent.reshape(heads, rows, rows) * scale + recent_bias[None]
        top = jnp.maximum(
            jnp.max(scores, axis=-1, keepdims=True), jnp.max(recent, axis=-1, keepdims=True)
        )
        weights = jnp.exp(scores - top)
        recent = jnp.exp(recent - top)
        total = jnp.sum(weights, axis=-1, keepdims=True) + jnp.sum(recent, axis=-1, keepdims=True)
        weights = weights.astype(bf16).reshape(heads * rows, pool * block_len)
        recent = recent.astype(bf16).reshape(heads * rows, rows)
        lat = lax.dot_general(weights, keys[:latent], LAST, preferred_element_type=f32)
        lat = lat + jnp.dot(recent, entry[:, :latent], preferred_element_type=f32)
        lat = (lat.reshape(heads, rows, latent) / total).astype(bf16)
        lse = jnp.where(top > 0.1 * NEG, top + jnp.log(total), NEG)
        lse = jnp.broadcast_to(lse, (heads, rows, 128))
        for f in range(4):
            for s in range(near):
                dx, dz = (s, f) if g == 0 else (f, s)
                home = (((blk >> 2) - dx) & 3) * 4 + ((blk - dz) & 3)
                out_ref[home, part, :] = lat[f * near + s]
                sum_ref[home, part, :] = lse[f * near + s]
    for h in range(heads):
        tile = split_terms(as_line(sum_ref[h]))
        out_ref[h, groups * rows :, :128] = tile
        out_ref[h, groups * rows :, 128:] = jnp.zeros((8, latent - 128), bf16)


def output_kernel(parts_ref, value_ref, out_ref, result_ref):
    count, rows = parts_ref.shape[0], 64
    sums = [joined_terms(parts_ref[k, rows:, :128]) for k in range(count)]
    best = functools.reduce(jnp.maximum, sums)
    shares = [jnp.exp(v - best) for v in sums]
    whole = functools.reduce(jnp.add, shares)
    joined = sum(as_column(p / whole, rows) * parts_ref[k, :rows, :].astype(f32) for k, p in enumerate(shares))
    head_out = jnp.dot(joined.astype(bf16), value_ref[0], preferred_element_type=f32).astype(bf16)
    line, row = sublanes((128, rows)), lanes((128, rows))
    source = 32 * (line >> 6) + 8 * ((line >> 1) & 3) + ((line >> 3) & 7)
    result = None
    for q in range(2):
        take = jnp.where((source == row) & ((line & 1) == q), 1.0, 0.0).astype(bf16)
        picked_rows = jnp.dot(take, head_out, preferred_element_type=f32).astype(bf16)
        term = jnp.dot(picked_rows, out_ref[:, q * 1024 : (q + 1) * 1024], preferred_element_type=f32)
        result = term if result is None else result + term
    result_ref[...] = result.astype(bf16)


def norm_kernel(info_ref, parts_ref, embeds_ref, gain_ref, spread_ref, resid_ref):
    blk = info_ref[1]
    steps, rows, width = embeds_ref.shape
    half = width // 2
    line = sublanes((2 * steps, half))
    resid = jnp.sum(parts_ref[...].astype(f32), axis=0)
    gain = jnp.zeros((2 * steps, half), f32)
    for q in range(2):
        columns = slice(q * half, (q + 1) * half)
        gain = gain + jnp.where((line & 1) == q, gain_ref[:, columns], 0.0)
        for t in range(steps):
            token = jnp.where(sublanes((rows, half)) == blk, embeds_ref[t, :, columns].astype(f32), 0.0)
            token = jnp.sum(token, axis=0, keepdims=True)
            resid = resid + jnp.where(line == 2 * t + q, token, 0.0)
    resid_ref[...] = resid
    sums = jnp.broadcast_to(jnp.sum(resid * resid, axis=1, keepdims=True), (2 * steps, 128))
    pair = jnp.where((sublanes((8, 8)) >> 1) == (lanes((8, 8)) >> 1), 1.0, 0.0)
    sums = jnp.dot(pair, sums, precision=lax.Precision.HIGHEST, preferred_element_type=f32)
    normed = (resid * lax.rsqrt(sums[:, :1] * (1.0 / width) + EPS) * gain).astype(bf16)
    spread_ref[...] = jnp.broadcast_to(normed[None], spread_ref.shape)


def line_row(line, core):
    chip = (line >> 3) & 63
    return 32 * (chip >> 4) + 16 * ((line >> 9) ^ core) + (chip & 15)


def route_kernel(info_ref, ids_ref, weights_ref, out_ref):
    core = info_ref[0]
    top, steps, rows = ids_ref.shape
    line = lanes((rows, out_ref.shape[1]))
    row = line_row(line, core)
    earlier = jnp.where(sublanes((rows, rows)) < lanes((rows, rows)), 1.0, 0.0).astype(bf16)
    slots, weights = [], []
    for e in range(2):
        expert = info_ref[3 + e]
        weight = jnp.zeros((steps, rows), f32)
        routed = jnp.zeros((steps, rows), f32)
        for k in range(top):
            match = ids_ref[k] == expert
            weight = weight + jnp.where(match, weights_ref[k], 0.0)
            routed = routed + jnp.where(match, 1.0, 0.0)
        wide = jnp.concatenate([routed, jnp.zeros((8 - steps, rows), f32)], axis=0).astype(bf16)
        rank = jnp.dot(wide, earlier, preferred_element_type=f32)[:steps]
        first = (sublanes((steps, rows)) * CAPACITY + 1).astype(f32)
        slots.append(jnp.where(routed > 0.5, rank + first, 0.0))
        weights.append(weight)
    total = jnp.zeros(out_ref.shape, f32)
    for t in range(steps):
        place = sublanes((8, rows))
        values = jnp.zeros((8, rows), f32)
        for k, value in enumerate(slots + weights):
            values = jnp.where(place == k, value[t : t + 1], values)
        take = jnp.where((sublanes(line.shape) == row) & (((line >> 1) & 3) == t), 1.0, 0.0)
        total = total + jnp.dot(values, take, precision=lax.Precision.HIGHEST, preferred_element_type=f32)
    out_ref[...] = total


def line_places(line, core, lines):
    row = line_row(line, core)
    return ((row & 1) ^ core) * (lines // 2) + (row >> 1) * 4 + ((line >> 1) & 3)


def picked(source_ref, hit, line, place, weights):
    halves = []
    for q in range(2):
        pick = jnp.where((line & 1) == q, hit, 0.0).astype(bf16)
        halves.append(jnp.dot(pick, source_ref[...], preferred_element_type=f32))
    first = jnp.where((line & 1) == 0, 1.0, 0.0)
    scale = [
        jnp.sum(hit[e * SLOTS : (e + 1) * SLOTS] * (first * weights[e]), axis=1, keepdims=True)
        for e in range(len(weights))
    ]
    parts = jnp.where(sublanes((8, line.shape[1])) == 0, (place + 1) >> 4, (place + 1) & 15).astype(f32)
    spot = lax.dot_general((parts * first).astype(bf16), hit.astype(bf16), LAST, preferred_element_type=f32)
    return halves, jnp.concatenate(scale, axis=0), spot


def pick_kernel(info_ref, mine_ref, route_ref, x_ref, scale_ref, spot_ref):
    core, y = info_ref[0], info_ref[2]
    lines, half = mine_ref.shape
    line = lanes((1, lines))
    hits = [sublanes((SLOTS, lines)) + 1 == route_ref[e : e + 1, :lines].astype(jnp.int32) for e in range(2)]
    hits.append(sublanes((OWN_ROWS, lines)) == (line >> 1) - y * OWN_ROWS)
    hit = jnp.concatenate([jnp.where(h, 1.0, 0.0) for h in hits], axis=0)
    place = line_places(line, core, lines)
    halves, scale, spot = picked(mine_ref, hit, line, place, [route_ref[2 + e : 3 + e, :lines] for e in range(2)])
    for q in range(2):
        x_ref[:, q * half : (q + 1) * half] = halves[q].astype(bf16)
    scale_ref[...] = jnp.broadcast_to(scale, scale_ref.shape)
    spot_ref[...] = spot


def put(ref, y_ref, spot, side):
    lines, half = ref.shape
    line = sublanes((lines, 1))
    found = jnp.where((line >> 1) + side * (lines // 2) == spot, 1.0, 0.0)
    result = None
    for q in range(2):
        found_q = jnp.where((line & 1) == q, found, 0.0).astype(bf16)
        term = jnp.dot(found_q, y_ref[:, q * half : (q + 1) * half], preferred_element_type=f32)
        result = term if result is None else result + term
    ref[...] = result.astype(bf16)


def expert_kernel(
    info_ref, shared_down_hbm, mine_x_ref, mine_scale_ref, mine_spot_ref, other_ref, route_ref, resid_ref,
    gate_ref, up_ref, down_ref, shared_gate_ref, shared_up_ref,
    other_out_ref, y_ref, spot_ref,
    x_ref, shared_down_ref, sems,
):
    core, blk = info_ref[0], info_ref[1]
    lines, half = other_ref.shape
    (copy,) = fetch((shared_down_hbm,), (shared_down_ref,), sems)
    line = lanes((1, lines)) + lines
    hits = [sublanes((SLOTS, lines)) + 1 == route_ref[e : e + 1, lines:].astype(jnp.int32) for e in range(2)]
    hit = jnp.concatenate([jnp.where(h, 1.0, 0.0) for h in hits], axis=0)
    place = line_places(line, core, lines)
    halves, scale, spot = picked(other_ref, hit, line, place, [route_ref[2 + e : 3 + e, lines:] for e in range(2)])
    routed = 2 * SLOTS
    for q in range(2):
        columns = slice(q * half, (q + 1) * half)
        x_ref[:, columns] = (mine_x_ref[:routed, columns].astype(f32) + halves[q]).astype(bf16)
    scale = scale + mine_scale_ref[:, :1]
    spot = jnp.concatenate([spot, jnp.zeros((8, OWN_ROWS), f32)], axis=1) + mine_spot_ref[...]
    spot = (spot[0:1] * 16.0 + spot[1:2] - 1.0).astype(jnp.int32)
    spot_ref[...] = jnp.broadcast_to(spot, spot_ref.shape)

    def gated(x, gate, up):
        gate_val = lax.dot_general(x, gate, LAST, preferred_element_type=f32)
        up_val = lax.dot_general(x, up, LAST, preferred_element_type=f32)
        return (gate_val / (1.0 + jnp.exp(-gate_val)) * up_val).astype(bf16)

    for e in range(2):
        part = slice(e * SLOTS, (e + 1) * SLOTS)
        act = gated(x_ref[part, :], gate_ref[e], up_ref[e])
        down = jnp.dot(act, down_ref[e], preferred_element_type=f32)
        y_ref[part, :] = (down * scale[part]).astype(bf16)
    act = gated(mine_x_ref[routed:, :], shared_gate_ref[...], shared_up_ref[...])
    copy.wait()
    own = jnp.dot(act, shared_down_ref[...], preferred_element_type=f32)
    for t in range(4):
        whole = jnp.concatenate([resid_ref[2 * t + q : 2 * t + q + 1, :] for q in range(2)], axis=1)
        own = own + jnp.where(sublanes((OWN_ROWS, 1)) == blk * 4 + t, whole, 0.0)
    y_ref[routed:, :] = own.astype(bf16)
    put(other_out_ref, y_ref, spot, 1)


def put_kernel(y_ref, spot_ref, out_ref):
    put(out_ref, y_ref, spot_ref[0:1], 0)


def per_device(
    embeds,
    attn_gain,
    w_query,
    w_latent,
    latent_gain,
    w_key_up,
    w_value_up,
    w_out,
    ffn_gain,
    w_shared_gate,
    w_shared_up,
    w_shared_down,
    w_expert_gate,
    w_expert_up,
    w_expert_down,
    cache_pool,
    block_tables,
    block_counts,
    parents,
    expert_ids,
    expert_weights,
):
    steps, row_dev, width = embeds.shape
    groups, beams, _ = block_tables.shape
    latent = w_key_up.shape[2]
    block_len, entry_width = cache_pool.shape[2:]
    rope = entry_width - latent
    pair_dev, _, unit_dev = w_expert_gate.shape
    half = width // 2
    chips = expert_ids.shape[1] // 2
    lines = chips * 2 * steps
    y, core = lax.axis_index("y"), lax.axis_index("core")
    blk, beam = lax.axis_index(BLK), lax.axis_index(BEAM)
    expert = blk * pair_dev * 2 + beam * unit_dev // FFE
    place = jnp.stack([core, blk, y, expert, expert + 2]).astype(jnp.int32)
    counts = jnp.concatenate([blk[None], block_counts]).astype(jnp.int32)

    frequency = np.float64(THETA) ** (-np.arange(rope // 2) * 2.0 / rope)
    frequency = np.tile(frequency.astype(np.float32), 4).reshape(1, 128)
    rows_all = groups * steps * beams
    blk_size = lax.axis_size("x") * lax.axis_size("z")
    sources = (embeds, w_query.T, w_key_up, attn_gain.reshape(1, width), jnp.asarray(frequency), block_counts)
    query = ((steps * beams, entry_width), bf16)
    first, second, normed, cosines = kernel_call(
        query_kernel,
        "query",
        [query, query, ((rows_all, width), bf16), ((8, 128), f32)],
        [pltpu.VMEM(a.shape, a.dtype) for a in sources[:-1]]
        + [pltpu.SMEM(block_counts.shape, jnp.int32), pltpu.SemaphoreType.DMA((len(sources),))],
        (60_000_000, 20_000_000, 0),
        (pltpu.HBM,) * len(sources),
        *in_hbm(*sources),
    )
    first, second = jnp.stack(gather(first, "x")), jnp.stack(gather(second, "z"))
    queries = gather(first, "z") + gather(second, "x")
    (entries,) = kernel_call(
        entry_kernel,
        "entry",
        [((rows_all, entry_width), bf16)],
        [],
        (150_000_000, 40_000_000, 0),
        (),
        normed,
        w_latent.T,
        latent_gain.reshape(1, latent),
        cosines,
    )
    cache = cache_pool.transpose(0, 1, 3, 2)
    (parts,) = kernel_call(
        attend_kernel,
        "attend",
        [((blk_size, rows_all + 8, latent), bf16)],
        [pltpu.VMEM((blk_size, rows_all, 128), f32)],
        (1_800_000_000, 5_000_000, 800_000),
        SCALARS,
        counts,
        *queries,
        cache,
        entries,
        parents,
        block_tables,
    )
    expert_ids, parts = lax.optimization_barrier((expert_ids, parts))
    parts = lax.all_to_all(parts, BLK, 0, 0)
    (route,) = kernel_call(
        route_kernel,
        "route",
        [((8, 2 * lines), f32)],
        [],
        (60_000_000, 60_000, 0),
        SCALARS,
        place,
        expert_ids.transpose(2, 0, 1),
        expert_weights.transpose(2, 0, 1),
    )
    parts, route = lax.optimization_barrier((parts, route))
    (attn_part,) = kernel_call(
        output_kernel,
        "output",
        [((row_dev * 2 * steps, half), bf16)],
        [],
        (80_000_000, 90_000_000, 1_000),
        (),
        parts,
        w_value_up,
        w_out,
    )
    attn_part = lax.all_to_all(attn_part.reshape(row_dev, 2 * steps, half), BLK, 0, 0)
    spread, resid = kernel_call(
        norm_kernel,
        "norm",
        [((chips, 2 * steps, half), bf16), ((2 * steps, half), f32)],
        [],
        (1_000_000, 90_000_000, 0),
        SCALARS,
        place,
        attn_part,
        embeds,
        ffn_gain.reshape(1, width),
    )

    mine = lax.all_to_all(spread, ("y", "x", "z"), 0, 0).reshape(lines, half)
    other = lax.ppermute(mine, "core", CORES)
    routed = pair_dev * SLOTS
    total = routed + OWN_ROWS
    slots = [((total, width), bf16), ((routed, 128), f32), ((8, total), f32)]
    x_mine, scale, spot = kernel_call(
        pick_kernel,
        "pick",
        slots,
        [],
        (1_000_000_000, 20_000_000, 0),
        SCALARS,
        place,
        mine,
        route,
    )
    other_out, outs, spot = kernel_call(
        expert_kernel,
        "experts",
        [((lines, half), bf16), ((total, width), bf16), ((8, total), jnp.int32)],
        [pltpu.VMEM((routed, width), bf16)] + room_for((w_shared_down,)),
        (3_000_000_000, 15_000_000, 300_000),
        SCALARS + (pltpu.HBM,),
        place,
        *in_hbm(w_shared_down),
        x_mine,
        scale,
        spot,
        other,
        route,
        resid,
        w_expert_gate.transpose(0, 2, 1),
        w_expert_up.transpose(0, 2, 1),
        w_expert_down,
        w_shared_gate.T,
        w_shared_up.T,
    )
    arrived = lax.ppermute(other_out, "core", CORES)
    (own_out,) = kernel_call(
        put_kernel, "put", [((lines, half), bf16)], [], (500_000_000, 2_000_000, 0), (), outs, spot
    )
    own_out = own_out.astype(f32) + arrived.astype(f32)
    own_out = own_out.astype(bf16).reshape(chips, 2 * steps, half)
    result = jnp.sum(lax.all_to_all(own_out, ("x", "z", "y"), 0, 0).astype(f32), axis=0)
    return result.reshape(steps, 1, width)


def solution(mesh):
    devices = mesh.devices.reshape(4, 4, 4, 2)
    split = Mesh(devices, ("x", "z", "y", "core"))
    placed = (
        P(None, BEAM, None),
        P(),
        P(None, BLK),
        P(),
        P(),
        P(BLK, None, None),
        P(BLK, None, None),
        P(BLK, None),
        P(),
        P(None, BLK),
        P(None, BLK),
        P(BLK, None),
        P(BLK, None, BEAM),
        P(BLK, None, BEAM),
        P(BLK, BEAM, None),
        P(BEAM, BLK, None, None),
        P(BEAM, None, None),
        P(BEAM),
        P(None, BEAM, None),
        P(),
        P(),
    )
    return jax.shard_map(
        per_device,
        mesh=split,
        in_specs=placed,
        out_specs=P(None, OUT_ORDER, None),
        check_vma=False,
    )
```

```python
import functools

import jax
import jax.numpy as jnp
import numpy as np
from jax import lax
from jax.experimental import pallas as pl
from jax.experimental.pallas import tpu as pltpu
from jax.sharding import Mesh, PartitionSpec as P

FFE = 1408
THETA = 50000.0
EPS = 1e-06
NEG = -1e30
CAPACITY = 24
SLOTS = 4 * CAPACITY
OWN_ROWS = 64

BLK = ("x", "z")
BEAM = ("y", "core")
OUT_ORDER = BLK + BEAM
CORES = [(0, 1), (1, 0)]
SCALARS = (pltpu.SMEM,)
VMEM_MIB = {"attend": 20, "pick": 16, "experts": 16, "put": 12}

f32, bf16 = jnp.float32, jnp.bfloat16
LAST = (((1,), (1,)), ((), ()))


def lanes(shape):
    return lax.broadcasted_iota(jnp.int32, shape, len(shape) - 1)


def sublanes(shape):
    return lax.broadcasted_iota(jnp.int32, shape, len(shape) - 2)


def kernel_call(body, name, outs, scratch, cost, first, *args):
    vmem = pl.BlockSpec(memory_space=pltpu.VMEM)
    first = [pl.BlockSpec(memory_space=space) for space in first]
    return pl.pallas_call(
        body,
        out_shape=[jax.ShapeDtypeStruct(shape, dtype) for shape, dtype in outs],
        in_specs=first + [vmem] * (len(args) - len(first)),
        out_specs=[vmem] * len(outs),
        scratch_shapes=scratch,
        compiler_params=pltpu.CompilerParams(vmem_limit_bytes=VMEM_MIB.get(name, 6) << 20),
        cost_estimate=pl.CostEstimate(flops=cost[0], bytes_accessed=cost[1], transcendentals=cost[2]),
        name=name,
    )(*args)


def fetch(sources, targets, sems):
    copies = [pltpu.make_async_copy(a, b, sems.at[k]) for k, (a, b) in enumerate(zip(sources, targets))]
    for copy in copies:
        copy.start()
    return copies


def in_hbm(*arrays):
    return [pltpu.with_memory_space_constraint(a, pltpu.HBM) for a in arrays]


def room_for(arrays):
    return [pltpu.VMEM(a.shape, a.dtype) for a in arrays] + [pltpu.SemaphoreType.DMA((len(arrays),))]


def shifted(value, turn, by):
    pairs = []
    for x in range(4):
        for z in range(4):
            for core in range(2):
                along_x = core == turn
                to = ((x + by) % 4, z) if along_x else (x, (z + by) % 4)
                pairs.append((8 * x + 2 * z + core, 8 * to[0] + 2 * to[1] + core))
    return lax.ppermute(value, ("x", "z", "core"), pairs)


def gather(value, turn):
    arrived = {s: shifted(value, turn, s) for s in (1, 3, 2)}
    return [value] + [arrived[s] for s in range(1, 4)]


def rope_parts(cos_ref, rows):
    cosine, sine = cos_ref[:, :64], cos_ref[:, 64:]
    wide = lambda v: jnp.concatenate([jnp.broadcast_to(v[k : k + 1], (8, 64)) for k in range(rows // 8)], axis=0)
    return wide(cosine), wide(sine)


def turned(values, precision=None):
    i, j = sublanes((64, 64)), lanes((64, 64))
    turn = jnp.where(i == j - 32, 1.0, 0.0) - jnp.where(i == j + 32, 1.0, 0.0)
    return jnp.dot(values, turn.astype(values.dtype), precision=precision, preferred_element_type=f32)


def query_kernel(
    embeds_hbm, query_hbm, key_up_hbm, gain_hbm, frequency_hbm, counts_hbm, latent_hbm,
    result_ref, normed_ref, cos_ref, latent_ref,
    embeds_ref, query_ref, key_up_ref, gain_ref, frequency_ref, counts_ref, sems,
):
    steps, _, width = embeds_ref.shape
    copies = fetch(
        (embeds_hbm, query_hbm, key_up_hbm, gain_hbm, frequency_hbm, counts_hbm, latent_hbm),
        (embeds_ref, query_ref, key_up_ref, gain_ref, frequency_ref, counts_ref, latent_ref),
        sems,
    )
    copies[4].wait()
    copies[5].wait()
    line = sublanes((8, 128))
    position = jnp.where(line < steps, counts_ref[0], counts_ref[1]) * 128 + (line & (steps - 1))
    angles = position.astype(f32) * frequency_ref[...]
    cos_ref[...] = jnp.where(lanes((8, 128)) < 64, jnp.cos(angles), jnp.sin(angles))
    copies[0].wait()
    copies[3].wait()
    tokens = [embeds_ref[t].astype(f32) for t in range(steps)]
    tokens = jnp.concatenate([tokens[t][8 * g : 8 * g + 8] for g in range(2) for t in range(steps)], axis=0)
    mean_sq = jnp.sum(tokens * tokens, axis=1, keepdims=True) * (1.0 / width)
    normed = (tokens * lax.rsqrt(mean_sq + EPS) * gain_ref[...]).astype(bf16)
    normed_ref[...] = normed
    copies[1].wait()
    queries = lax.dot_general(normed, query_ref[...], LAST, preferred_element_type=f32).astype(bf16)
    copies[2].wait()
    latent = jnp.dot(queries[:, :128], key_up_ref[0], preferred_element_type=f32).astype(bf16)
    rope = queries[:, 128:]
    cosine, sine = rope_parts(cos_ref, 64)
    rope = (rope.astype(f32) * cosine + turned(rope) * sine).astype(bf16)
    result_ref[:, :512] = latent
    result_ref[:, 512:] = rope
    copies[6].wait()


def entry_kernel(normed_ref, latent_ref, gain_ref, cos_ref, out_ref):
    projected = lax.dot_general(normed_ref[...], latent_ref[...], LAST, preferred_element_type=f32)
    latent, rope = projected[:, :512], projected[:, 512:]
    mean_sq = jnp.sum(latent * latent, axis=1, keepdims=True) * (1.0 / 512)
    out_ref[:, :512] = (latent * lax.rsqrt(mean_sq + EPS) * gain_ref[...]).astype(bf16)
    cosine, sine = rope_parts(cos_ref, 64)
    out_ref[:, 512:] = (rope * cosine + turned(rope, lax.Precision.HIGHEST) * sine).astype(bf16)


def split_terms(lines):
    place = sublanes((8, lines[0].shape[1]))
    tile = jnp.zeros(place.shape, f32)
    for k, line in enumerate(lines):
        first = line.astype(bf16).astype(f32)
        second = (line - first).astype(bf16).astype(f32)
        for j, term in enumerate((first, second, line - first - second)):
            tile = jnp.where(place == 3 * k + j, term, tile)
    return tile.astype(bf16)


def joined_terms(tile, k):
    tile = tile.astype(f32)[3 * k : 3 * k + 3]
    return tile[0:1] + tile[1:2] + tile[2:3]


def as_line(column, offset=0):
    shape = (column.shape[0], 128)
    return jnp.sum(jnp.where(lanes(shape) == sublanes(shape) + offset, column, 0.0), axis=0, keepdims=True)


def as_column(line, count, offset=0):
    shape = (count, 128)
    return jnp.sum(jnp.where(lanes(shape) == sublanes(shape) + offset, line, 0.0), axis=1, keepdims=True)


def attend_kernel(info_ref, *refs):
    q_refs, out_refs = refs[:4], refs[8:12]
    cache_ref, entry_ref, parent_ref, table_ref = refs[4:8]
    sum_ref = refs[12]
    near, rows_all, width = q_refs[0].shape
    heads = 4 * near
    groups, beams, _ = table_ref.shape
    rows = rows_all // groups
    pool, _, block_len = cache_ref.shape[1:]
    latent = out_refs[0].shape[1]
    steps = rows // beams
    scale = (width - latent + 128) ** (-0.5)
    blk = info_ref[0]
    for g in range(groups):
        shape = (beams, 128)
        origin = (lanes(shape) == sublanes(shape)).astype(f32)
        kept = []
        for t in range(steps):
            diagonal = lanes((beams, beams)) == sublanes((beams, beams))
            parent = jnp.where(diagonal, parent_ref[t, g : g + 1, :].astype(f32), 0.0)
            parent = jnp.sum(parent, axis=1, keepdims=True).astype(jnp.int32)
            choose = (lanes((beams, beams)) == parent).astype(f32)
            origin = jnp.dot(choose, origin, preferred_element_type=f32)
            origin = origin + (lanes(shape) == sublanes(shape) + beams * (1 + t)).astype(f32)
            kept.append(origin)
        origin = jnp.concatenate(kept, axis=0)
        table = table_ref[g]
        live = lanes(table.shape) < info_ref[1 + g]
        used = jnp.zeros((beams, 128), f32)
        for p in range(pool):
            hit = jnp.where((table == blk * pool + p) & live, 1.0, 0.0)
            hit = jnp.max(hit, axis=1, keepdims=True)
            used = used + jnp.where(lanes(used.shape) == p, hit, 0.0)
        used = jnp.dot(origin[:, :beams], used, preferred_element_type=f32)
        bias = jnp.concatenate(
            [jnp.broadcast_to(used[:, p : p + 1], (rows, block_len)) for p in range(pool)], axis=1
        )
        bias = jnp.where(bias > 0.5, 0.0, NEG)
        seen = origin[:, beams : beams + rows]
        recent_bias = jnp.where((seen > 0.5) & (blk == 0), 0.0, NEG)

        part = slice(g * rows, (g + 1) * rows)
        q = jnp.concatenate([ref[:, part, :] for ref in q_refs], axis=0).reshape(heads * rows, width)
        keys = jnp.concatenate([cache_ref[g, p] for p in range(pool)], axis=1)
        entry = entry_ref[part]
        scores = jnp.dot(q, keys, preferred_element_type=f32)
        scores = scores.reshape(heads, rows, pool * block_len) * scale + bias[None]
        recent = lax.dot_general(q, entry, LAST, preferred_element_type=f32)
        recent = recent.reshape(heads, rows, rows) * scale + recent_bias[None]
        top = jnp.maximum(
            jnp.max(scores, axis=-1, keepdims=True), jnp.max(recent, axis=-1, keepdims=True)
        )
        weights = jnp.exp(scores - top)
        recent = jnp.exp(recent - top)
        total = jnp.sum(weights, axis=-1, keepdims=True) + jnp.sum(recent, axis=-1, keepdims=True)
        weights = weights.astype(bf16).reshape(heads * rows, pool * block_len)
        recent = recent.astype(bf16).reshape(heads * rows, rows)
        lat = lax.dot_general(weights, keys[:latent], LAST, preferred_element_type=f32)
        lat = lat + jnp.dot(recent, entry[:, :latent], preferred_element_type=f32)
        lat = (lat.reshape(heads, rows, latent) / total).astype(bf16)
        lse = jnp.where(top > 0.1 * NEG, top + jnp.log(total), NEG)
        lse = jnp.broadcast_to(lse, (heads, rows, 128))
        for s in range(near):
            for f in range(4):
                first = f * rows_all + g * rows
                out_refs[s][first : first + rows, :] = lat[f * near + s]
                sum_ref[s, first : first + rows, :] = lse[f * near + s]
    for s, ref in enumerate(out_refs):
        lines = [as_line(sum_ref[s, 128 * k : 128 * k + 128, :]) for k in range(2)]
        ref[4 * rows_all :, :128] = split_terms(lines)
        ref[4 * rows_all :, 128:] = jnp.zeros((8, latent - 128), bf16)


def shares(sums):
    best = functools.reduce(jnp.maximum, sums)
    parts = [jnp.exp(v - best) for v in sums]
    whole = functools.reduce(jnp.add, parts)
    return [p / whole for p in parts], best + jnp.log(whole)


def merge_kernel(*refs):
    parts, outs = refs[:4], refs[4:]
    rows = 64
    lines = []
    for k in range(2):
        part_share, whole = shares([joined_terms(ref[4 * rows :, :128], k) for ref in parts])
        lines.append(whole)
        own = slice(128 * k, 128 * k + 128)
        merged = sum(as_column(p, 128) * ref[own, :].astype(f32) for p, ref in zip(part_share, parts))
        merged = merged.astype(bf16)
        for f in range(2):
            outs[2 * k + f][:rows, :] = merged[rows * f : rows * f + rows]
    tile = split_terms(lines)
    for ref in outs:
        ref[rows:, :128] = tile
        ref[rows:, 128:] = jnp.zeros((8, ref.shape[1] - 128), bf16)


def output_kernel(*refs):
    parts, (value_ref, out_ref, result_ref) = refs[:4], refs[4:]
    rows = 64
    sums = [as_column(joined_terms(ref[rows:, :128], f // 2), rows, rows * (f % 2)) for f, ref in enumerate(parts)]
    part_share, _ = shares(sums)
    joined = sum(p * ref[:rows, :].astype(f32) for p, ref in zip(part_share, parts))
    head_out = jnp.dot(joined.astype(bf16), value_ref[0], preferred_element_type=f32).astype(bf16)
    line, row = sublanes((128, rows)), lanes((128, rows))
    source = 32 * (line >> 6) + 8 * ((line >> 1) & 3) + ((line >> 3) & 7)
    result = None
    for q in range(2):
        take = jnp.where((source == row) & ((line & 1) == q), 1.0, 0.0).astype(bf16)
        picked_rows = jnp.dot(take, head_out, preferred_element_type=f32).astype(bf16)
        term = jnp.dot(picked_rows, out_ref[:, q * 1024 : (q + 1) * 1024], preferred_element_type=f32)
        result = term if result is None else result + term
    result_ref[...] = result.astype(bf16)


def norm_kernel(info_ref, parts_ref, embeds_ref, gain_ref, spread_ref, resid_ref):
    blk = info_ref[1]
    steps, rows, width = embeds_ref.shape
    half = width // 2
    line = sublanes((2 * steps, half))
    resid = jnp.sum(parts_ref[...].astype(f32), axis=0)
    gain = jnp.zeros((2 * steps, half), f32)
    for q in range(2):
        columns = slice(q * half, (q + 1) * half)
        gain = gain + jnp.where((line & 1) == q, gain_ref[:, columns], 0.0)
        for t in range(steps):
            token = jnp.where(sublanes((rows, half)) == blk, embeds_ref[t, :, columns].astype(f32), 0.0)
            token = jnp.sum(token, axis=0, keepdims=True)
            resid = resid + jnp.where(line == 2 * t + q, token, 0.0)
    resid_ref[...] = resid
    sums = jnp.broadcast_to(jnp.sum(resid * resid, axis=1, keepdims=True), (2 * steps, 128))
    pair = jnp.where((sublanes((8, 8)) >> 1) == (lanes((8, 8)) >> 1), 1.0, 0.0)
    sums = jnp.dot(pair, sums, precision=lax.Precision.HIGHEST, preferred_element_type=f32)
    normed = (resid * lax.rsqrt(sums[:, :1] * (1.0 / width) + EPS) * gain).astype(bf16)
    spread_ref[...] = jnp.broadcast_to(normed[None], spread_ref.shape)


def line_row(line, core):
    chip = (line >> 3) & 63
    return 32 * (chip >> 4) + 16 * ((line >> 9) ^ core) + 4 * (chip & 3) + ((chip >> 2) & 3)


def route_kernel(info_ref, ids_ref, weights_ref, out_ref):
    core = info_ref[0]
    top, steps, rows = ids_ref.shape
    line = lanes((rows, out_ref.shape[1]))
    row = line_row(line, core)
    earlier = jnp.where(sublanes((rows, rows)) < lanes((rows, rows)), 1.0, 0.0).astype(bf16)
    slots, weights = [], []
    for e in range(2):
        expert = info_ref[3 + e]
        weight = jnp.zeros((steps, rows), f32)
        routed = jnp.zeros((steps, rows), f32)
        for k in range(top):
            match = ids_ref[k] == expert
            weight = weight + jnp.where(match, weights_ref[k], 0.0)
            routed = routed + jnp.where(match, 1.0, 0.0)
        wide = jnp.concatenate([routed, jnp.zeros((8 - steps, rows), f32)], axis=0).astype(bf16)
        rank = jnp.dot(wide, earlier, preferred_element_type=f32)[:steps]
        first = (sublanes((steps, rows)) * CAPACITY + 1).astype(f32)
        slots.append(jnp.where(routed > 0.5, rank + first, 0.0))
        weights.append(weight)
    total = jnp.zeros(out_ref.shape, f32)
    for t in range(steps):
        place = sublanes((8, rows))
        values = jnp.zeros((8, rows), f32)
        for k, value in enumerate(slots + weights):
            values = jnp.where(place == k, value[t : t + 1], values)
        take = jnp.where((sublanes(line.shape) == row) & (((line >> 1) & 3) == t), 1.0, 0.0)
        total = total + jnp.dot(values, take, precision=lax.Precision.HIGHEST, preferred_element_type=f32)
    out_ref[...] = total


def line_places(line, core, lines):
    row = line_row(line, core)
    chip = 16 * ((row >> 1) & 3) + 4 * ((row >> 3) & 3) + (row >> 5)
    return ((row & 1) ^ core) * (lines // 2) + chip * 4 + ((line >> 1) & 3)


def picked(source_ref, hit, line, place, weights):
    halves = []
    for q in range(2):
        pick = jnp.where((line & 1) == q, hit, 0.0).astype(bf16)
        halves.append(jnp.dot(pick, source_ref[...], preferred_element_type=f32))
    first = jnp.where((line & 1) == 0, 1.0, 0.0)
    scale = [
        jnp.sum(hit[e * SLOTS : (e + 1) * SLOTS] * (first * weights[e]), axis=1, keepdims=True)
        for e in range(len(weights))
    ]
    parts = jnp.where(sublanes((8, line.shape[1])) == 0, (place + 1) >> 4, (place + 1) & 15).astype(f32)
    spot = lax.dot_general((parts * first).astype(bf16), hit.astype(bf16), LAST, preferred_element_type=f32)
    return halves, jnp.concatenate(scale, axis=0), spot


def gated(x, gate, up):
    gate_val = lax.dot_general(x, gate, LAST, preferred_element_type=f32)
    up_val = lax.dot_general(x, up, LAST, preferred_element_type=f32)
    return (gate_val / (1.0 + jnp.exp(-gate_val)) * up_val).astype(bf16)


def pick_kernel(
    info_ref, gate_hbm, up_hbm, down_hbm, mine_ref, route_ref, resid_ref,
    x_ref, own_ref, scale_ref, spot_ref,
    gate_ref, up_ref, down_ref, sems,
):
    core, blk, y = info_ref[0], info_ref[1], info_ref[2]
    own_chip = 4 * (blk & 3) + (blk >> 2)
    lines, half = mine_ref.shape
    routed = 2 * SLOTS
    copies = fetch((gate_hbm, up_hbm, down_hbm), (gate_ref, up_ref, down_ref), sems)
    line = lanes((1, lines))
    hits = [sublanes((SLOTS, lines)) + 1 == route_ref[e : e + 1, :lines].astype(jnp.int32) for e in range(2)]
    hits.append(sublanes((OWN_ROWS, lines)) == (line >> 1) - y * OWN_ROWS)
    hit = jnp.concatenate([jnp.where(h, 1.0, 0.0) for h in hits], axis=0)
    place = line_places(line, core, lines)
    halves, scale, spot = picked(mine_ref, hit, line, place, [route_ref[2 + e : 3 + e, :lines] for e in range(2)])
    for q in range(2):
        x_ref[:, q * half : (q + 1) * half] = halves[q][:routed].astype(bf16)
    scale_ref[...] = jnp.broadcast_to(scale, scale_ref.shape)
    spot_ref[...] = spot
    own_rows = jnp.concatenate([v[routed:].astype(bf16) for v in halves], axis=1)
    for copy in copies:
        copy.wait()
    act = gated(own_rows, gate_ref[...], up_ref[...])
    own = jnp.dot(act, down_ref[...], preferred_element_type=f32)
    for t in range(4):
        whole = jnp.concatenate([resid_ref[2 * t + q : 2 * t + q + 1, :] for q in range(2)], axis=1)
        own = own + jnp.where(sublanes((OWN_ROWS, 1)) == own_chip * 4 + t, whole, 0.0)
    own_ref[...] = own.astype(bf16)


def put(ref, y_ref, spot, side):
    lines, half = ref.shape
    line = sublanes((lines, 1))
    found = jnp.where((line >> 1) + side * (lines // 2) == spot, 1.0, 0.0)
    result = None
    for q in range(2):
        found_q = jnp.where((line & 1) == q, found, 0.0).astype(bf16)
        term = jnp.dot(found_q, y_ref[:, q * half : (q + 1) * half], preferred_element_type=f32)
        result = term if result is None else result + term
    ref[...] = result.astype(bf16)


def expert_kernel(
    info_ref, mine_x_ref, own_ref, mine_scale_ref, mine_spot_ref, other_ref, route_ref,
    gate_ref, up_ref, down_ref,
    other_out_ref, y_ref, spot_ref, x_ref,
):
    core = info_ref[0]
    lines, half = other_ref.shape
    line = lanes((1, lines)) + lines
    hits = [sublanes((SLOTS, lines)) + 1 == route_ref[e : e + 1, lines:].astype(jnp.int32) for e in range(2)]
    hit = jnp.concatenate([jnp.where(h, 1.0, 0.0) for h in hits], axis=0)
    place = line_places(line, core, lines)
    halves, scale, spot = picked(other_ref, hit, line, place, [route_ref[2 + e : 3 + e, lines:] for e in range(2)])
    routed = 2 * SLOTS
    for q in range(2):
        columns = slice(q * half, (q + 1) * half)
        x_ref[:, columns] = (mine_x_ref[:, columns].astype(f32) + halves[q]).astype(bf16)
    scale = scale + mine_scale_ref[:, :1]
    spot = jnp.concatenate([spot, jnp.zeros((8, OWN_ROWS), f32)], axis=1) + mine_spot_ref[...]
    spot = (spot[0:1] * 16.0 + spot[1:2] - 1.0).astype(jnp.int32)
    spot_ref[...] = jnp.broadcast_to(spot, spot_ref.shape)

    for e in range(2):
        part = slice(e * SLOTS, (e + 1) * SLOTS)
        act = gated(x_ref[part, :], gate_ref[e], up_ref[e])
        down = jnp.dot(act, down_ref[e], preferred_element_type=f32)
        y_ref[part, :] = (down * scale[part]).astype(bf16)
    y_ref[routed:, :] = own_ref[...]
    put(other_out_ref, y_ref, spot, 1)


def put_kernel(y_ref, spot_ref, out_ref):
    put(out_ref, y_ref, spot_ref[0:1], 0)


def per_device(
    embeds,
    attn_gain,
    w_query,
    w_latent,
    latent_gain,
    w_key_up,
    w_value_up,
    w_out,
    ffn_gain,
    w_shared_gate,
    w_shared_up,
    w_shared_down,
    w_expert_gate,
    w_expert_up,
    w_expert_down,
    cache_pool,
    block_tables,
    block_counts,
    parents,
    expert_ids,
    expert_weights,
):
    steps, row_dev, width = embeds.shape
    groups, beams, _ = block_tables.shape
    latent = w_key_up.shape[2]
    entry_width = cache_pool.shape[3]
    rope = entry_width - latent
    pair_dev, _, unit_dev = w_expert_gate.shape
    half = width // 2
    chips = expert_ids.shape[1] // 2
    lines = chips * 2 * steps
    y, core = lax.axis_index("y"), lax.axis_index("core")
    blk, beam = lax.axis_index(BLK), lax.axis_index(BEAM)
    expert = blk * pair_dev * 2 + beam * unit_dev // FFE
    place = jnp.stack([core, blk, y, expert, expert + 2]).astype(jnp.int32)
    counts = jnp.concatenate([blk[None], block_counts]).astype(jnp.int32)

    frequency = np.float64(THETA) ** (-np.arange(rope // 2) * 2.0 / rope)
    frequency = np.tile(frequency.astype(np.float32), 4).reshape(1, 128)
    rows_all = groups * steps * beams
    blk_size = lax.axis_size("x") * lax.axis_size("z")
    sources = (embeds, w_query.T, w_key_up, attn_gain.reshape(1, width), jnp.asarray(frequency), block_counts, w_latent.T)
    query, normed, cosines, latent_weights = kernel_call(
        query_kernel,
        "query",
        [((rows_all, entry_width), bf16), ((rows_all, width), bf16), ((8, 128), f32), ((entry_width, width), bf16)],
        [pltpu.VMEM(a.shape, a.dtype) for a in sources[:-2]]
        + [pltpu.SMEM(block_counts.shape, jnp.int32), pltpu.SemaphoreType.DMA((len(sources),))],
        (60_000_000, 20_000_000, 0),
        (pltpu.HBM,) * len(sources),
        *in_hbm(*sources),
    )
    query = jnp.stack(gather(query, 0))
    queries = gather(query, 1)
    _, normed, expert_ids = lax.optimization_barrier((query, normed, expert_ids))
    (entries,) = kernel_call(
        entry_kernel,
        "entry",
        [((rows_all, entry_width), bf16)],
        [],
        (150_000_000, 3_000_000, 0),
        (),
        normed,
        latent_weights,
        latent_gain.reshape(1, latent),
        cosines,
    )
    cache = cache_pool.transpose(0, 1, 3, 2)
    (route,) = kernel_call(
        route_kernel,
        "route",
        [((8, 2 * lines), f32)],
        [],
        (60_000_000, 60_000, 0),
        SCALARS,
        place,
        expert_ids.transpose(2, 0, 1),
        expert_weights.transpose(2, 0, 1),
    )
    counts, route = lax.optimization_barrier((counts, route))
    part = ((4 * rows_all + 8, latent), bf16)
    parts = kernel_call(
        attend_kernel,
        "attend",
        [part] * 4,
        [pltpu.VMEM((4, 4 * rows_all, 128), f32)],
        (1_800_000_000, 5_000_000, 800_000),
        SCALARS,
        counts,
        *queries,
        cache,
        entries,
        parents,
        block_tables,
    )
    moved = {s: shifted(parts[s], 0, -s) for s in (1, 3, 2)}
    parts = [parts[0]] + [moved[s] for s in range(1, 4)]
    last = ((rows_all + 8, latent), bf16)
    parts = kernel_call(merge_kernel, "merge", [last] * 4, [], (4_000_000, 30_000_000, 2_000), (), *parts)
    moved = {f: shifted(parts[f], 1, -f) for f in (1, 3, 2)}
    parts = [parts[0]] + [moved[f] for f in range(1, 4)]
    (attn_part,) = kernel_call(
        output_kernel,
        "output",
        [((row_dev * 2 * steps, half), bf16)],
        [],
        (80_000_000, 90_000_000, 1_000),
        (),
        *parts,
        w_value_up,
        w_out,
    )
    attn_part = lax.all_to_all(attn_part.reshape(row_dev, 2 * steps, half), BLK, 0, 0)
    spread, resid = kernel_call(
        norm_kernel,
        "norm",
        [((chips, 2 * steps, half), bf16), ((2 * steps, half), f32)],
        [],
        (1_000_000, 90_000_000, 0),
        SCALARS,
        place,
        attn_part,
        embeds,
        ffn_gain.reshape(1, width),
    )

    mine = lax.all_to_all(spread, ("y", "z", "x"), 0, 0).reshape(lines, half)
    other = lax.ppermute(mine, "core", CORES)
    routed = pair_dev * SLOTS
    total = routed + OWN_ROWS
    slots = [((routed, width), bf16), ((OWN_ROWS, width), bf16), ((routed, 128), f32), ((8, total), f32)]
    fetched = (w_shared_gate.T, w_shared_up.T, w_shared_down)
    x_mine, own, scale, spot = kernel_call(
        pick_kernel,
        "pick",
        slots,
        room_for(fetched),
        (1_000_000_000, 20_000_000, 0),
        SCALARS + (pltpu.HBM,) * len(fetched),
        place,
        *in_hbm(*fetched),
        mine,
        route,
        resid,
    )
    other_out, outs, spot = kernel_call(
        expert_kernel,
        "experts",
        [((lines, half), bf16), ((total, width), bf16), ((8, total), jnp.int32)],
        [pltpu.VMEM((routed, width), bf16)],
        (3_000_000_000, 15_000_000, 300_000),
        SCALARS,
        place,
        x_mine,
        own,
        scale,
        spot,
        other,
        route,
        w_expert_gate.transpose(0, 2, 1),
        w_expert_up.transpose(0, 2, 1),
        w_expert_down,
    )
    arrived = lax.ppermute(other_out, "core", CORES)
    (own_out,) = kernel_call(
        put_kernel, "put", [((lines, half), bf16)], [], (500_000_000, 2_000_000, 0), (), outs, spot
    )
    own_out = own_out.astype(f32) + arrived.astype(f32)
    own_out = own_out.astype(bf16).reshape(chips, 2 * steps, half)
    result = jnp.sum(lax.all_to_all(own_out, ("y", "z", "x"), 0, 0).astype(f32), axis=0)
    return result.reshape(steps, 1, width)


def solution(mesh):
    devices = mesh.devices.reshape(4, 4, 4, 2)
    split = Mesh(devices, ("x", "z", "y", "core"))
    placed = (
        P(None, BEAM, None),
        P(),
        P(None, BLK),
        P(),
        P(),
        P(BLK, None, None),
        P(BLK, None, None),
        P(BLK, None),
        P(),
        P(None, BLK),
        P(None, BLK),
        P(BLK, None),
        P(BLK, None, BEAM),
        P(BLK, None, BEAM),
        P(BLK, BEAM, None),
        P(BEAM, BLK, None, None),
        P(BEAM, None, None),
        P(BEAM),
        P(None, BEAM, None),
        P(),
        P(),
    )
    return jax.shard_map(
        per_device,
        mesh=split,
        in_specs=placed,
        out_specs=P(None, OUT_ORDER, None),
        check_vma=False,
    )
```

```python
import functools

import jax
import jax.numpy as jnp
import numpy as np
from jax import lax
from jax.experimental import pallas as pl
from jax.experimental.pallas import tpu as pltpu
from jax.sharding import Mesh, PartitionSpec as P

FFE = 1408
THETA = 50000.0
EPS = 1e-06
NEG = -1e30
CAPACITY = 24
SLOTS = 4 * CAPACITY
OWN_ROWS = 64

BLK = ("x", "z")
BEAM = ("y", "core")
OUT_ORDER = BLK + BEAM
CORES = [(0, 1), (1, 0)]
SCALARS = (pltpu.SMEM,)
VMEM_MIB = {"attend": 20, "pick": 16, "experts": 16, "put": 12}

f32, bf16 = jnp.float32, jnp.bfloat16
LAST = (((1,), (1,)), ((), ()))


def lanes(shape):
    return lax.broadcasted_iota(jnp.int32, shape, len(shape) - 1)


def sublanes(shape):
    return lax.broadcasted_iota(jnp.int32, shape, len(shape) - 2)


def kernel_call(body, name, outs, scratch, cost, first, *args):
    vmem = pl.BlockSpec(memory_space=pltpu.VMEM)
    first = [pl.BlockSpec(memory_space=space) for space in first]
    return pl.pallas_call(
        body,
        out_shape=[jax.ShapeDtypeStruct(shape, dtype) for shape, dtype in outs],
        in_specs=first + [vmem] * (len(args) - len(first)),
        out_specs=[vmem] * len(outs),
        scratch_shapes=scratch,
        compiler_params=pltpu.CompilerParams(vmem_limit_bytes=VMEM_MIB.get(name, 6) << 20),
        cost_estimate=pl.CostEstimate(flops=cost[0], bytes_accessed=cost[1], transcendentals=cost[2]),
        name=name,
    )(*args)


def fetch(sources, targets, sems):
    copies = [pltpu.make_async_copy(a, b, sems.at[k]) for k, (a, b) in enumerate(zip(sources, targets))]
    for copy in copies:
        copy.start()
    return copies


def in_hbm(*arrays):
    return [pltpu.with_memory_space_constraint(a, pltpu.HBM) for a in arrays]


def room_for(arrays):
    return [pltpu.VMEM(a.shape, a.dtype) for a in arrays] + [pltpu.SemaphoreType.DMA((len(arrays),))]


def shifted(value, turn, by):
    pairs = []
    for x in range(4):
        for z in range(4):
            for core in range(2):
                along_x = core == turn
                to = ((x + by) % 4, z) if along_x else (x, (z + by) % 4)
                pairs.append((8 * x + 2 * z + core, 8 * to[0] + 2 * to[1] + core))
    return lax.ppermute(value, ("x", "z", "core"), pairs)


def gather(value, turn):
    arrived = {s: shifted(value, turn, s) for s in (1, 3, 2)}
    return [value] + [arrived[s] for s in range(1, 4)]


def rope_parts(cos_ref, rows):
    cosine, sine = cos_ref[:, :64], cos_ref[:, 64:]
    wide = lambda v: jnp.concatenate([jnp.broadcast_to(v[k : k + 1], (8, 64)) for k in range(rows // 8)], axis=0)
    return wide(cosine), wide(sine)


def turned(values, precision=None):
    i, j = sublanes((64, 64)), lanes((64, 64))
    turn = jnp.where(i == j - 32, 1.0, 0.0) - jnp.where(i == j + 32, 1.0, 0.0)
    return jnp.dot(values, turn.astype(values.dtype), precision=precision, preferred_element_type=f32)


def query_kernel(
    embeds_hbm, query_hbm, key_up_hbm, gain_hbm, frequency_hbm, counts_hbm, latent_hbm,
    result_ref, normed_ref, cos_ref, latent_ref,
    embeds_ref, query_ref, key_up_ref, gain_ref, frequency_ref, counts_ref, sems,
):
    steps, _, width = embeds_ref.shape
    copies = fetch(
        (embeds_hbm, query_hbm, key_up_hbm, gain_hbm, frequency_hbm, counts_hbm, latent_hbm),
        (embeds_ref, query_ref, key_up_ref, gain_ref, frequency_ref, counts_ref, latent_ref),
        sems,
    )
    copies[4].wait()
    copies[5].wait()
    line = sublanes((8, 128))
    position = jnp.where(line < steps, counts_ref[0], counts_ref[1]) * 128 + (line & (steps - 1))
    angles = position.astype(f32) * frequency_ref[...]
    cos_ref[...] = jnp.where(lanes((8, 128)) < 64, jnp.cos(angles), jnp.sin(angles))
    copies[0].wait()
    copies[3].wait()
    tokens = [embeds_ref[t].astype(f32) for t in range(steps)]
    tokens = jnp.concatenate([tokens[t][8 * g : 8 * g + 8] for g in range(2) for t in range(steps)], axis=0)
    mean_sq = jnp.sum(tokens * tokens, axis=1, keepdims=True) * (1.0 / width)
    normed = (tokens * lax.rsqrt(mean_sq + EPS) * gain_ref[...]).astype(bf16)
    normed_ref[...] = normed
    copies[1].wait()
    queries = lax.dot_general(normed, query_ref[...], LAST, preferred_element_type=f32).astype(bf16)
    copies[2].wait()
    latent = jnp.dot(queries[:, :128], key_up_ref[0], preferred_element_type=f32).astype(bf16)
    rope = queries[:, 128:]
    cosine, sine = rope_parts(cos_ref, 64)
    rope = (rope.astype(f32) * cosine + turned(rope) * sine).astype(bf16)
    result_ref[:64, :] = latent
    result_ref[64:, :] = jnp.concatenate([rope[8 * k : 8 * k + 8] for k in range(8)], axis=1)
    copies[6].wait()


def entry_kernel(normed_ref, latent_ref, gain_ref, cos_ref, out_ref):
    projected = lax.dot_general(normed_ref[...], latent_ref[...], LAST, preferred_element_type=f32)
    latent, rope = projected[:, :512], projected[:, 512:]
    mean_sq = jnp.sum(latent * latent, axis=1, keepdims=True) * (1.0 / 512)
    out_ref[:, :512] = (latent * lax.rsqrt(mean_sq + EPS) * gain_ref[...]).astype(bf16)
    cosine, sine = rope_parts(cos_ref, 64)
    out_ref[:, 512:] = (rope * cosine + turned(rope, lax.Precision.HIGHEST) * sine).astype(bf16)


def split_terms(lines):
    place = sublanes((8, lines[0].shape[1]))
    tile = jnp.zeros(place.shape, f32)
    for k, line in enumerate(lines):
        first = line.astype(bf16).astype(f32)
        second = (line - first).astype(bf16).astype(f32)
        for j, term in enumerate((first, second, line - first - second)):
            tile = jnp.where(place == 3 * k + j, term, tile)
    return tile.astype(bf16)


def joined_terms(tile, k):
    tile = tile.astype(f32)[3 * k : 3 * k + 3]
    return tile[0:1] + tile[1:2] + tile[2:3]


def as_line(column, offset=0):
    shape = (column.shape[0], 128)
    return jnp.sum(jnp.where(lanes(shape) == sublanes(shape) + offset, column, 0.0), axis=0, keepdims=True)


def as_column(line, count, offset=0):
    shape = (count, 128)
    return jnp.sum(jnp.where(lanes(shape) == sublanes(shape) + offset, line, 0.0), axis=1, keepdims=True)


def attend_kernel(info_ref, *refs):
    q_refs, out_refs = refs[:4], refs[8:12]
    cache_ref, entry_ref, parent_ref, table_ref = refs[4:8]
    sum_ref = refs[12]
    near, heads, rows_all, width = 4, 16, 64, entry_ref.shape[1]
    groups, beams, _ = table_ref.shape
    rows = rows_all // groups
    pool, _, block_len = cache_ref.shape[1:]
    latent = out_refs[0].shape[1]
    steps = rows // beams
    scale = (width - latent + 128) ** (-0.5)
    blk = info_ref[0]
    for g in range(groups):
        shape = (beams, 128)
        origin = (lanes(shape) == sublanes(shape)).astype(f32)
        kept = []
        for t in range(steps):
            diagonal = lanes((beams, beams)) == sublanes((beams, beams))
            parent = jnp.where(diagonal, parent_ref[t, g : g + 1, :].astype(f32), 0.0)
            parent = jnp.sum(parent, axis=1, keepdims=True).astype(jnp.int32)
            choose = (lanes((beams, beams)) == parent).astype(f32)
            origin = jnp.dot(choose, origin, preferred_element_type=f32)
            origin = origin + (lanes(shape) == sublanes(shape) + beams * (1 + t)).astype(f32)
            kept.append(origin)
        origin = jnp.concatenate(kept, axis=0)
        table = table_ref[g]
        live = lanes(table.shape) < info_ref[1 + g]
        used = jnp.zeros((beams, 128), f32)
        for p in range(pool):
            hit = jnp.where((table == blk * pool + p) & live, 1.0, 0.0)
            hit = jnp.max(hit, axis=1, keepdims=True)
            used = used + jnp.where(lanes(used.shape) == p, hit, 0.0)
        used = jnp.dot(origin[:, :beams], used, preferred_element_type=f32)
        bias = jnp.concatenate(
            [jnp.broadcast_to(used[:, p : p + 1], (rows, block_len)) for p in range(pool)], axis=1
        )
        bias = jnp.where(bias > 0.5, 0.0, NEG)
        seen = origin[:, beams : beams + rows]
        recent_bias = jnp.where((seen > 0.5) & (blk == 0), 0.0, NEG)

        part = slice(g * rows, (g + 1) * rows)
        lat_part = jnp.concatenate([ref[:, part, :] for ref in q_refs], axis=0)
        rope_tile = jnp.concatenate([ref[:, rows_all:, :] for ref in q_refs], axis=0)
        rope_part = [rope_tile[:, :, 64 * k : 64 * k + 64] for k in range(steps * g, steps * g + steps)]
        q = jnp.concatenate([lat_part, jnp.concatenate(rope_part, axis=1)], axis=2).reshape(heads * rows, width)
        keys = jnp.concatenate([cache_ref[g, p] for p in range(pool)], axis=1)
        entry = entry_ref[part]
        scores = jnp.dot(q, keys, preferred_element_type=f32)
        scores = scores.reshape(heads, rows, pool * block_len) * scale + bias[None]
        recent = lax.dot_general(q, entry, LAST, preferred_element_type=f32)
        recent = recent.reshape(heads, rows, rows) * scale + recent_bias[None]
        top = jnp.maximum(
            jnp.max(scores, axis=-1, keepdims=True), jnp.max(recent, axis=-1, keepdims=True)
        )
        weights = jnp.exp(scores - top)
        recent = jnp.exp(recent - top)
        total = jnp.sum(weights, axis=-1, keepdims=True) + jnp.sum(recent, axis=-1, keepdims=True)
        weights = weights.astype(bf16).reshape(heads * rows, pool * block_len)
        recent = recent.astype(bf16).reshape(heads * rows, rows)
        lat = lax.dot_general(weights, keys[:latent], LAST, preferred_element_type=f32)
        lat = lat + jnp.dot(recent, entry[:, :latent], preferred_element_type=f32)
        lat = (lat.reshape(heads, rows, latent) * (1.0 / total)).astype(bf16)
        lse = jnp.where(top > 0.1 * NEG, top + jnp.log(total), NEG)
        lse = jnp.broadcast_to(lse, (heads, rows, 128))
        for s in range(near):
            for f in range(4):
                first = f * rows_all + g * rows
                out_refs[s][first : first + rows, :] = lat[f * near + s]
                sum_ref[s, first : first + rows, :] = lse[f * near + s]
    for s, ref in enumerate(out_refs):
        lines = [as_line(sum_ref[s, 128 * k : 128 * k + 128, :]) for k in range(2)]
        ref[4 * rows_all :, :128] = split_terms(lines)
        ref[4 * rows_all :, 128:] = jnp.zeros((8, latent - 128), bf16)


def shares(sums):
    best = functools.reduce(jnp.maximum, sums)
    parts = [jnp.exp(v - best) for v in sums]
    whole = functools.reduce(jnp.add, parts)
    return [p / whole for p in parts], best + jnp.log(whole)


def merge_kernel(*refs):
    parts, outs = refs[:4], refs[4:]
    rows = 64
    lines = []
    for k in range(2):
        part_share, whole = shares([joined_terms(ref[4 * rows :, :128], k) for ref in parts])
        lines.append(whole)
        own = slice(128 * k, 128 * k + 128)
        merged = sum(as_column(p, 128) * ref[own, :].astype(f32) for p, ref in zip(part_share, parts))
        merged = merged.astype(bf16)
        for f in range(2):
            outs[2 * k + f][:rows, :] = merged[rows * f : rows * f + rows]
    tile = split_terms(lines)
    for ref in outs:
        ref[rows:, :128] = tile
        ref[rows:, 128:] = jnp.zeros((8, ref.shape[1] - 128), bf16)


def output_kernel(*refs):
    parts, (value_ref, out_ref, result_ref) = refs[:4], refs[4:]
    rows = 64
    sums = [as_column(joined_terms(ref[rows:, :128], f // 2), rows, rows * (f % 2)) for f, ref in enumerate(parts)]
    part_share, _ = shares(sums)
    joined = sum(p * ref[:rows, :].astype(f32) for p, ref in zip(part_share, parts))
    head_out = jnp.dot(joined.astype(bf16), value_ref[0], preferred_element_type=f32).astype(bf16)
    line, row = sublanes((128, rows)), lanes((128, rows))
    source = 32 * (line >> 6) + 8 * ((line >> 1) & 3) + ((line >> 3) & 7)
    result = None
    for q in range(2):
        take = jnp.where((source == row) & ((line & 1) == q), 1.0, 0.0).astype(bf16)
        picked_rows = jnp.dot(take, head_out, preferred_element_type=f32).astype(bf16)
        term = jnp.dot(picked_rows, out_ref[:, q * 1024 : (q + 1) * 1024], preferred_element_type=f32)
        result = term if result is None else result + term
    result_ref[...] = result.astype(bf16)


def norm_kernel(info_ref, parts_ref, embeds_ref, gain_ref, spread_ref, resid_ref):
    blk = info_ref[1]
    steps, rows, width = embeds_ref.shape
    half = width // 2
    line = sublanes((2 * steps, half))
    resid = jnp.sum(parts_ref[...].astype(f32), axis=0)
    gain = jnp.zeros((2 * steps, half), f32)
    for q in range(2):
        columns = slice(q * half, (q + 1) * half)
        gain = gain + jnp.where((line & 1) == q, gain_ref[:, columns], 0.0)
        for t in range(steps):
            token = jnp.where(sublanes((rows, half)) == blk, embeds_ref[t, :, columns].astype(f32), 0.0)
            token = jnp.sum(token, axis=0, keepdims=True)
            resid = resid + jnp.where(line == 2 * t + q, token, 0.0)
    resid_ref[...] = resid
    sums = jnp.broadcast_to(jnp.sum(resid * resid, axis=1, keepdims=True), (2 * steps, 128))
    pair = jnp.where((sublanes((8, 8)) >> 1) == (lanes((8, 8)) >> 1), 1.0, 0.0)
    sums = jnp.dot(pair, sums, precision=lax.Precision.HIGHEST, preferred_element_type=f32)
    normed = (resid * lax.rsqrt(sums[:, :1] * (1.0 / width) + EPS) * gain).astype(bf16)
    spread_ref[...] = jnp.broadcast_to(normed[None], spread_ref.shape)


def line_row(line, core):
    chip = (line >> 3) & 63
    return 32 * (chip >> 4) + 16 * ((line >> 9) ^ core) + 4 * (chip & 3) + ((chip >> 2) & 3)


def route_kernel(info_ref, ids_ref, weights_ref, out_ref):
    core = info_ref[0]
    top, steps, rows = ids_ref.shape
    line = lanes((rows, out_ref.shape[1]))
    row = line_row(line, core)
    earlier = jnp.where(sublanes((rows, rows)) < lanes((rows, rows)), 1.0, 0.0).astype(bf16)
    slots, weights = [], []
    for e in range(2):
        expert = info_ref[3 + e]
        weight = jnp.zeros((steps, rows), f32)
        routed = jnp.zeros((steps, rows), f32)
        for k in range(top):
            match = ids_ref[k] == expert
            weight = weight + jnp.where(match, weights_ref[k], 0.0)
            routed = routed + jnp.where(match, 1.0, 0.0)
        wide = jnp.concatenate([routed, jnp.zeros((8 - steps, rows), f32)], axis=0).astype(bf16)
        rank = jnp.dot(wide, earlier, preferred_element_type=f32)[:steps]
        first = (sublanes((steps, rows)) * CAPACITY + 1).astype(f32)
        slots.append(jnp.where(routed > 0.5, rank + first, 0.0))
        weights.append(weight)
    total = jnp.zeros(out_ref.shape, f32)
    for t in range(steps):
        place = sublanes((8, rows))
        values = jnp.zeros((8, rows), f32)
        for k, value in enumerate(slots + weights):
            values = jnp.where(place == k, value[t : t + 1], values)
        take = jnp.where((sublanes(line.shape) == row) & (((line >> 1) & 3) == t), 1.0, 0.0)
        total = total + jnp.dot(values, take, precision=lax.Precision.HIGHEST, preferred_element_type=f32)
    out_ref[...] = total


def line_places(line, core, lines):
    row = line_row(line, core)
    return ((row & 1) ^ core) * (lines // 2) + (row >> 1) * 4 + ((line >> 1) & 3)


def picked(source_ref, hit, line, place, weights):
    halves = []
    for q in range(2):
        pick = jnp.where((line & 1) == q, hit, 0.0).astype(bf16)
        halves.append(jnp.dot(pick, source_ref[...], preferred_element_type=f32))
    first = jnp.where((line & 1) == 0, 1.0, 0.0)
    scale = [
        jnp.sum(hit[e * SLOTS : (e + 1) * SLOTS] * (first * weights[e]), axis=1, keepdims=True)
        for e in range(len(weights))
    ]
    parts = jnp.where(sublanes((8, line.shape[1])) == 0, (place + 1) >> 4, (place + 1) & 15).astype(f32)
    spot = lax.dot_general((parts * first).astype(bf16), hit.astype(bf16), LAST, preferred_element_type=f32)
    return halves, jnp.concatenate(scale, axis=0), spot


def gated(x, gate, up):
    gate_val = lax.dot_general(x, gate, LAST, preferred_element_type=f32)
    up_val = lax.dot_general(x, up, LAST, preferred_element_type=f32)
    return (gate_val / (1.0 + jnp.exp(-gate_val)) * up_val).astype(bf16)


def pick_kernel(
    info_ref, gate_hbm, up_hbm, down_hbm, mine_ref, route_ref, resid_ref,
    x_ref, own_ref, scale_ref, spot_ref,
    gate_ref, up_ref, down_ref, sems,
):
    core, blk, y = info_ref[0], info_ref[1], info_ref[2]
    own_chip = 4 * (blk & 3) + (blk >> 2)
    lines, half = mine_ref.shape
    routed = 2 * SLOTS
    copies = fetch((gate_hbm, up_hbm, down_hbm), (gate_ref, up_ref, down_ref), sems)
    line = lanes((1, lines))
    hits = [sublanes((SLOTS, lines)) + 1 == route_ref[e : e + 1, :lines].astype(jnp.int32) for e in range(2)]
    hits.append(sublanes((OWN_ROWS, lines)) == (line >> 1) - y * OWN_ROWS)
    hit = jnp.concatenate([jnp.where(h, 1.0, 0.0) for h in hits], axis=0)
    place = line_places(line, core, lines)
    halves, scale, spot = picked(mine_ref, hit, line, place, [route_ref[2 + e : 3 + e, :lines] for e in range(2)])
    for q in range(2):
        x_ref[:, q * half : (q + 1) * half] = halves[q][:routed].astype(bf16)
    scale_ref[...] = jnp.broadcast_to(scale, scale_ref.shape)
    spot_ref[...] = spot
    own_rows = jnp.concatenate([v[routed:].astype(bf16) for v in halves], axis=1)
    for copy in copies:
        copy.wait()
    act = gated(own_rows, gate_ref[...], up_ref[...])
    own = jnp.dot(act, down_ref[...], preferred_element_type=f32)
    for t in range(4):
        whole = jnp.concatenate([resid_ref[2 * t + q : 2 * t + q + 1, :] for q in range(2)], axis=1)
        own = own + jnp.where(sublanes((OWN_ROWS, 1)) == own_chip * 4 + t, whole, 0.0)
    own_ref[...] = own.astype(bf16)


def put(ref, y_ref, spot, side):
    lines, half = ref.shape
    line = sublanes((lines, 1))
    found = jnp.where((line >> 1) + side * (lines // 2) == spot, 1.0, 0.0)
    result = None
    for q in range(2):
        found_q = jnp.where((line & 1) == q, found, 0.0).astype(bf16)
        term = jnp.dot(found_q, y_ref[:, q * half : (q + 1) * half], preferred_element_type=f32)
        result = term if result is None else result + term
    ref[...] = result.astype(bf16)


def expert_kernel(
    info_ref, mine_x_ref, own_ref, mine_scale_ref, mine_spot_ref, other_ref, route_ref,
    gate_ref, up_ref, down_ref,
    other_out_ref, y_ref, spot_ref, x_ref,
):
    core = info_ref[0]
    lines, half = other_ref.shape
    line = lanes((1, lines)) + lines
    hits = [sublanes((SLOTS, lines)) + 1 == route_ref[e : e + 1, lines:].astype(jnp.int32) for e in range(2)]
    hit = jnp.concatenate([jnp.where(h, 1.0, 0.0) for h in hits], axis=0)
    place = line_places(line, core, lines)
    halves, scale, spot = picked(other_ref, hit, line, place, [route_ref[2 + e : 3 + e, lines:] for e in range(2)])
    routed = 2 * SLOTS
    for q in range(2):
        columns = slice(q * half, (q + 1) * half)
        x_ref[:, columns] = (mine_x_ref[:, columns].astype(f32) + halves[q]).astype(bf16)
    scale = scale + mine_scale_ref[:, :1]
    spot = jnp.concatenate([spot, jnp.zeros((8, OWN_ROWS), f32)], axis=1) + mine_spot_ref[...]
    spot = (spot[0:1] * 16.0 + spot[1:2] - 1.0).astype(jnp.int32)
    spot_ref[...] = jnp.broadcast_to(spot, spot_ref.shape)

    for e in range(2):
        part = slice(e * SLOTS, (e + 1) * SLOTS)
        act = gated(x_ref[part, :], gate_ref[e], up_ref[e])
        down = jnp.dot(act, down_ref[e], preferred_element_type=f32)
        y_ref[part, :] = (down * scale[part]).astype(bf16)
    y_ref[routed:, :] = own_ref[...]
    put(other_out_ref, y_ref, spot, 1)


def put_kernel(y_ref, spot_ref, out_ref):
    put(out_ref, y_ref, spot_ref[0:1], 0)


def per_device(
    embeds,
    attn_gain,
    w_query,
    w_latent,
    latent_gain,
    w_key_up,
    w_value_up,
    w_out,
    ffn_gain,
    w_shared_gate,
    w_shared_up,
    w_shared_down,
    w_expert_gate,
    w_expert_up,
    w_expert_down,
    cache_pool,
    block_tables,
    block_counts,
    parents,
    expert_ids,
    expert_weights,
):
    steps, row_dev, width = embeds.shape
    groups, beams, _ = block_tables.shape
    latent = w_key_up.shape[2]
    entry_width = cache_pool.shape[3]
    rope = entry_width - latent
    pair_dev, _, unit_dev = w_expert_gate.shape
    half = width // 2
    chips = expert_ids.shape[1] // 2
    lines = chips * 2 * steps
    y, core = lax.axis_index("y"), lax.axis_index("core")
    blk, beam = lax.axis_index(BLK), lax.axis_index(BEAM)
    expert = blk * pair_dev * 2 + beam * unit_dev // FFE
    place = jnp.stack([core, blk, y, expert, expert + 2]).astype(jnp.int32)
    counts = jnp.concatenate([blk[None], block_counts]).astype(jnp.int32)

    frequency = np.float64(THETA) ** (-np.arange(rope // 2) * 2.0 / rope)
    frequency = np.tile(frequency.astype(np.float32), 4).reshape(1, 128)
    rows_all = groups * steps * beams
    blk_size = lax.axis_size("x") * lax.axis_size("z")
    sources = (embeds, w_query.T, w_key_up, attn_gain.reshape(1, width), jnp.asarray(frequency), block_counts, w_latent.T)
    query, normed, cosines, latent_weights = kernel_call(
        query_kernel,
        "query",
        [((rows_all + 8, latent), bf16), ((rows_all, width), bf16), ((8, 128), f32), ((entry_width, width), bf16)],
        [pltpu.VMEM(a.shape, a.dtype) for a in sources[:-2]]
        + [pltpu.SMEM(block_counts.shape, jnp.int32), pltpu.SemaphoreType.DMA((len(sources),))],
        (60_000_000, 20_000_000, 0),
        (pltpu.HBM,) * len(sources),
        *in_hbm(*sources),
    )
    query = jnp.stack(gather(query, 0))
    queries = gather(query, 1)
    _, normed, expert_ids = lax.optimization_barrier((query, normed, expert_ids))
    (entries,) = kernel_call(
        entry_kernel,
        "entry",
        [((rows_all, entry_width), bf16)],
        [],
        (150_000_000, 3_000_000, 0),
        (),
        normed,
        latent_weights,
        latent_gain.reshape(1, latent),
        cosines,
    )
    cache = cache_pool.transpose(0, 1, 3, 2)
    (route,) = kernel_call(
        route_kernel,
        "route",
        [((8, 2 * lines), f32)],
        [],
        (60_000_000, 60_000, 0),
        SCALARS,
        place,
        expert_ids.transpose(2, 0, 1),
        expert_weights.transpose(2, 0, 1),
    )
    counts, route = lax.optimization_barrier((counts, route))
    part = ((4 * rows_all + 8, latent), bf16)
    parts = kernel_call(
        attend_kernel,
        "attend",
        [part] * 4,
        [pltpu.VMEM((4, 4 * rows_all, 128), f32)],
        (1_800_000_000, 5_000_000, 800_000),
        SCALARS,
        counts,
        *queries,
        cache,
        entries,
        parents,
        block_tables,
    )
    moved = {s: shifted(parts[s], 0, -s) for s in (1, 3, 2)}
    parts = [parts[0]] + [moved[s] for s in range(1, 4)]
    last = ((rows_all + 8, latent), bf16)
    parts = kernel_call(merge_kernel, "merge", [last] * 4, [], (4_000_000, 30_000_000, 2_000), (), *parts)
    moved = {f: shifted(parts[f], 1, -f) for f in (1, 3, 2)}
    parts = [parts[0]] + [moved[f] for f in range(1, 4)]
    (attn_part,) = kernel_call(
        output_kernel,
        "output",
        [((row_dev * 2 * steps, half), bf16)],
        [],
        (80_000_000, 90_000_000, 1_000),
        (),
        *parts,
        w_value_up,
        w_out,
    )
    attn_part = lax.all_to_all(attn_part.reshape(row_dev, 2 * steps, half), BLK, 0, 0)
    spread, resid = kernel_call(
        norm_kernel,
        "norm",
        [((chips, 2 * steps, half), bf16), ((2 * steps, half), f32)],
        [],
        (1_000_000, 90_000_000, 0),
        SCALARS,
        place,
        attn_part,
        embeds,
        ffn_gain.reshape(1, width),
    )

    mine = lax.all_to_all(spread, ("y", "z", "x"), 0, 0).reshape(lines, half)
    other = lax.ppermute(mine, "core", CORES)
    routed = pair_dev * SLOTS
    total = routed + OWN_ROWS
    slots = [((routed, width), bf16), ((OWN_ROWS, width), bf16), ((routed, 128), f32), ((8, total), f32)]
    fetched = (w_shared_gate.T, w_shared_up.T, w_shared_down)
    x_mine, own, scale, spot = kernel_call(
        pick_kernel,
        "pick",
        slots,
        room_for(fetched),
        (1_000_000_000, 20_000_000, 0),
        SCALARS + (pltpu.HBM,) * len(fetched),
        place,
        *in_hbm(*fetched),
        mine,
        route,
        resid,
    )
    other_out, outs, spot = kernel_call(
        expert_kernel,
        "experts",
        [((lines, half), bf16), ((total, width), bf16), ((8, total), jnp.int32)],
        [pltpu.VMEM((routed, width), bf16)],
        (3_000_000_000, 15_000_000, 300_000),
        SCALARS,
        place,
        x_mine,
        own,
        scale,
        spot,
        other,
        route,
        w_expert_gate.transpose(0, 2, 1),
        w_expert_up.transpose(0, 2, 1),
        w_expert_down,
    )
    arrived = lax.ppermute(other_out, "core", CORES)
    (own_out,) = kernel_call(
        put_kernel, "put", [((lines, half), bf16)], [], (500_000_000, 2_000_000, 0), (), outs, spot
    )
    own_out = own_out.astype(f32) + arrived.astype(f32)
    own_out = own_out.astype(bf16).reshape(chips, 2 * steps, half)
    result = jnp.sum(lax.all_to_all(own_out, ("x", "z", "y"), 0, 0).astype(f32), axis=0)
    return result.reshape(steps, 1, width)


def solution(mesh):
    devices = mesh.devices.reshape(4, 4, 4, 2)
    split = Mesh(devices, ("x", "z", "y", "core"))
    placed = (
        P(None, BEAM, None),
        P(),
        P(None, BLK),
        P(),
        P(),
        P(BLK, None, None),
        P(BLK, None, None),
        P(BLK, None),
        P(),
        P(None, BLK),
        P(None, BLK),
        P(BLK, None),
        P(BLK, None, BEAM),
        P(BLK, None, BEAM),
        P(BLK, BEAM, None),
        P(BEAM, BLK, None, None),
        P(BEAM, None, None),
        P(BEAM),
        P(None, BEAM, None),
        P(),
        P(),
    )
    return jax.shard_map(
        per_device,
        mesh=split,
        in_specs=placed,
        out_specs=P(None, OUT_ORDER, None),
        check_vma=False,
    )
```

```python
import functools

import jax
import jax.numpy as jnp
import numpy as np
from jax import lax
from jax.experimental import pallas as pl
from jax.experimental.pallas import tpu as pltpu
from jax.sharding import Mesh, PartitionSpec as P

FFE = 1408
THETA = 50000.0
EPS = 1e-06
NEG = -1e30
CAPACITY = 24
SLOTS = 4 * CAPACITY
OWN_ROWS = 64

BLK = ("x", "z")
BEAM = ("y", "core")
OUT_ORDER = BLK + BEAM
CORES = [(0, 1), (1, 0)]
SCALARS = (pltpu.SMEM,)
VMEM_MIB = {"attend": 20, "pick": 16, "experts": 16, "put": 12}

f32, bf16 = jnp.float32, jnp.bfloat16
LAST = (((1,), (1,)), ((), ()))


def lanes(shape):
    return lax.broadcasted_iota(jnp.int32, shape, len(shape) - 1)


def sublanes(shape):
    return lax.broadcasted_iota(jnp.int32, shape, len(shape) - 2)


def kernel_call(body, name, outs, scratch, cost, first, *args):
    vmem = pl.BlockSpec(memory_space=pltpu.VMEM)
    first = [pl.BlockSpec(memory_space=space) for space in first]
    return pl.pallas_call(
        body,
        out_shape=[jax.ShapeDtypeStruct(shape, dtype) for shape, dtype in outs],
        in_specs=first + [vmem] * (len(args) - len(first)),
        out_specs=[vmem] * len(outs),
        scratch_shapes=scratch,
        compiler_params=pltpu.CompilerParams(vmem_limit_bytes=VMEM_MIB.get(name, 6) << 20),
        cost_estimate=pl.CostEstimate(flops=cost[0], bytes_accessed=cost[1], transcendentals=cost[2]),
        name=name,
    )(*args)


def fetch(sources, targets, sems):
    copies = [pltpu.make_async_copy(a, b, sems.at[k]) for k, (a, b) in enumerate(zip(sources, targets))]
    for copy in copies:
        copy.start()
    return copies


def in_hbm(*arrays):
    return [pltpu.with_memory_space_constraint(a, pltpu.HBM) for a in arrays]


def room_for(arrays):
    return [pltpu.VMEM(a.shape, a.dtype) for a in arrays] + [pltpu.SemaphoreType.DMA((len(arrays),))]


def shifted(value, turn, by):
    pairs = []
    for x in range(4):
        for z in range(4):
            for core in range(2):
                along_x = core == turn
                to = ((x + by) % 4, z) if along_x else (x, (z + by) % 4)
                pairs.append((8 * x + 2 * z + core, 8 * to[0] + 2 * to[1] + core))
    return lax.ppermute(value, ("x", "z", "core"), pairs)


def gather(value, turn):
    arrived = {s: shifted(value, turn, s) for s in (1, 3, 2)}
    return [value] + [arrived[s] for s in range(1, 4)]


def rope_parts(cos_ref, rows):
    cosine, sine = cos_ref[:, :64], cos_ref[:, 64:]
    wide = lambda v: jnp.concatenate([jnp.broadcast_to(v[k : k + 1], (8, 64)) for k in range(rows // 8)], axis=0)
    return wide(cosine), wide(sine)


def turned(values, precision=None):
    i, j = sublanes((64, 64)), lanes((64, 64))
    turn = jnp.where(i == j - 32, 1.0, 0.0) - jnp.where(i == j + 32, 1.0, 0.0)
    return jnp.dot(values, turn.astype(values.dtype), precision=precision, preferred_element_type=f32)


def query_kernel(
    embeds_hbm, query_hbm, key_up_hbm, gain_hbm, frequency_hbm, counts_hbm, latent_hbm,
    result_ref, normed_ref, cos_ref, latent_ref,
    embeds_ref, query_ref, key_up_ref, gain_ref, frequency_ref, counts_ref, sems,
):
    steps, _, width = embeds_ref.shape
    copies = fetch(
        (embeds_hbm, query_hbm, key_up_hbm, gain_hbm, frequency_hbm, counts_hbm, latent_hbm),
        (embeds_ref, query_ref, key_up_ref, gain_ref, frequency_ref, counts_ref, latent_ref),
        sems,
    )
    copies[4].wait()
    copies[5].wait()
    line = sublanes((8, 128))
    position = jnp.where(line < steps, counts_ref[0], counts_ref[1]) * 128 + (line & (steps - 1))
    angles = position.astype(f32) * frequency_ref[...]
    cos_ref[...] = jnp.where(lanes((8, 128)) < 64, jnp.cos(angles), jnp.sin(angles))
    copies[0].wait()
    copies[3].wait()
    tokens = [embeds_ref[t].astype(f32) for t in range(steps)]
    tokens = jnp.concatenate([tokens[t][8 * g : 8 * g + 8] for g in range(2) for t in range(steps)], axis=0)
    mean_sq = jnp.sum(tokens * tokens, axis=1, keepdims=True) * (1.0 / width)
    normed = (tokens * lax.rsqrt(mean_sq + EPS) * gain_ref[...]).astype(bf16)
    normed_ref[...] = normed
    copies[1].wait()
    queries = lax.dot_general(normed, query_ref[...], LAST, preferred_element_type=f32).astype(bf16)
    copies[2].wait()
    latent = jnp.dot(queries[:, :128], key_up_ref[0], preferred_element_type=f32).astype(bf16)
    rope = queries[:, 128:]
    cosine, sine = rope_parts(cos_ref, 64)
    rope = (rope.astype(f32) * cosine + turned(rope) * sine).astype(bf16)
    result_ref[:64, :] = latent
    result_ref[64:, :] = jnp.concatenate([rope[8 * k : 8 * k + 8] for k in range(8)], axis=1)
    copies[6].wait()


def entry_kernel(normed_ref, latent_ref, gain_ref, cos_ref, out_ref):
    projected = lax.dot_general(normed_ref[...], latent_ref[...], LAST, preferred_element_type=f32)
    latent, rope = projected[:, :512], projected[:, 512:]
    mean_sq = jnp.sum(latent * latent, axis=1, keepdims=True) * (1.0 / 512)
    out_ref[:, :512] = (latent * lax.rsqrt(mean_sq + EPS) * gain_ref[...]).astype(bf16)
    cosine, sine = rope_parts(cos_ref, 64)
    out_ref[:, 512:] = (rope * cosine + turned(rope, lax.Precision.HIGHEST) * sine).astype(bf16)


def split_terms(lines):
    place = sublanes((8, lines[0].shape[1]))
    tile = jnp.zeros(place.shape, f32)
    for k, line in enumerate(lines):
        first = line.astype(bf16).astype(f32)
        second = (line - first).astype(bf16).astype(f32)
        for j, term in enumerate((first, second, line - first - second)):
            tile = jnp.where(place == 3 * k + j, term, tile)
    return tile.astype(bf16)


def joined_terms(tile, k):
    tile = tile.astype(f32)[3 * k : 3 * k + 3]
    return tile[0:1] + tile[1:2] + tile[2:3]


def as_line(column, offset=0):
    shape = (column.shape[0], 128)
    return jnp.sum(jnp.where(lanes(shape) == sublanes(shape) + offset, column, 0.0), axis=0, keepdims=True)


def as_column(line, count, offset=0):
    shape = (count, 128)
    return jnp.sum(jnp.where(lanes(shape) == sublanes(shape) + offset, line, 0.0), axis=1, keepdims=True)


def attend_kernel(info_ref, *refs):
    q_refs, out_refs = refs[:4], refs[8:12]
    cache_ref, entry_ref, parent_ref, table_ref = refs[4:8]
    sum_ref = refs[12]
    near, heads, rows_all, width = 4, 16, 64, entry_ref.shape[1]
    groups, beams, _ = table_ref.shape
    rows = rows_all // groups
    pool, _, block_len = cache_ref.shape[1:]
    latent = out_refs[0].shape[1]
    steps = rows // beams
    scale = (width - latent + 128) ** (-0.5)
    blk = info_ref[0]
    for g in range(groups):
        shape = (beams, 128)
        origin = (lanes(shape) == sublanes(shape)).astype(f32)
        kept = []
        for t in range(steps):
            diagonal = lanes((beams, beams)) == sublanes((beams, beams))
            parent = jnp.where(diagonal, parent_ref[t, g : g + 1, :].astype(f32), 0.0)
            parent = jnp.sum(parent, axis=1, keepdims=True).astype(jnp.int32)
            choose = (lanes((beams, beams)) == parent).astype(f32)
            origin = jnp.dot(choose, origin, preferred_element_type=f32)
            origin = origin + (lanes(shape) == sublanes(shape) + beams * (1 + t)).astype(f32)
            kept.append(origin)
        origin = jnp.concatenate(kept, axis=0)
        table = table_ref[g]
        live = lanes(table.shape) < info_ref[1 + g]
        used = jnp.zeros((beams, 128), f32)
        for p in range(pool):
            hit = jnp.where((table == blk * pool + p) & live, 1.0, 0.0)
            hit = jnp.max(hit, axis=1, keepdims=True)
            used = used + jnp.where(lanes(used.shape) == p, hit, 0.0)
        used = jnp.dot(origin[:, :beams], used, preferred_element_type=f32)
        bias = jnp.concatenate(
            [jnp.broadcast_to(used[:, p : p + 1], (rows, block_len)) for p in range(pool)], axis=1
        )
        bias = jnp.where(bias > 0.5, 0.0, NEG)
        seen = origin[:, beams : beams + rows]
        recent_bias = jnp.where((seen > 0.5) & (blk == 0), 0.0, NEG)

        part = slice(g * rows, (g + 1) * rows)
        lat_part = jnp.concatenate([ref[:, part, :] for ref in q_refs], axis=0)
        rope_tile = jnp.concatenate([ref[:, rows_all:, :] for ref in q_refs], axis=0)
        rope_part = [rope_tile[:, :, 64 * k : 64 * k + 64] for k in range(steps * g, steps * g + steps)]
        q = jnp.concatenate([lat_part, jnp.concatenate(rope_part, axis=1)], axis=2).reshape(heads * rows, width)
        keys = jnp.concatenate([cache_ref[g, p] for p in range(pool)], axis=1)
        entry = entry_ref[part]
        scores = jnp.dot(q, keys, preferred_element_type=f32)
        scores = scores.reshape(heads, rows, pool * block_len) * scale + bias[None]
        recent = lax.dot_general(q, entry, LAST, preferred_element_type=f32)
        recent = recent.reshape(heads, rows, rows) * scale + recent_bias[None]
        top = jnp.maximum(
            jnp.max(scores, axis=-1, keepdims=True), jnp.max(recent, axis=-1, keepdims=True)
        )
        weights = jnp.exp(scores - top)
        recent = jnp.exp(recent - top)
        total = jnp.sum(weights, axis=-1, keepdims=True) + jnp.sum(recent, axis=-1, keepdims=True)
        weights = weights.astype(bf16).reshape(heads * rows, pool * block_len)
        recent = recent.astype(bf16).reshape(heads * rows, rows)
        lat = lax.dot_general(weights, keys[:latent], LAST, preferred_element_type=f32)
        lat = lat + jnp.dot(recent, entry[:, :latent], preferred_element_type=f32)
        lat = (lat.reshape(heads, rows, latent) * (1.0 / total)).astype(bf16)
        lse = jnp.where(top > 0.1 * NEG, top + jnp.log(total), NEG)
        lse = jnp.broadcast_to(lse, (heads, rows, 128))
        for s in range(near):
            for f in range(4):
                first = f * rows_all + g * rows
                out_refs[s][first : first + rows, :] = lat[f * near + s]
                sum_ref[s, first : first + rows, :] = lse[f * near + s]
    for s, ref in enumerate(out_refs):
        lines = [as_line(sum_ref[s, 128 * k : 128 * k + 128, :]) for k in range(2)]
        ref[4 * rows_all :, :128] = split_terms(lines)
        ref[4 * rows_all :, 128:] = jnp.zeros((8, latent - 128), bf16)


def shares(sums):
    best = functools.reduce(jnp.maximum, sums)
    parts = [jnp.exp(v - best) for v in sums]
    whole = functools.reduce(jnp.add, parts)
    return [p / whole for p in parts], best + jnp.log(whole)


def merge_kernel(*refs):
    parts, outs = refs[:4], refs[4:]
    rows = 64
    lines = []
    for k in range(2):
        part_share, whole = shares([joined_terms(ref[4 * rows :, :128], k) for ref in parts])
        lines.append(whole)
        own = slice(128 * k, 128 * k + 128)
        merged = sum(as_column(p, 128) * ref[own, :].astype(f32) for p, ref in zip(part_share, parts))
        merged = merged.astype(bf16)
        for f in range(2):
            outs[2 * k + f][:rows, :] = merged[rows * f : rows * f + rows]
    tile = split_terms(lines)
    for ref in outs:
        ref[rows:, :128] = tile
        ref[rows:, 128:] = jnp.zeros((8, ref.shape[1] - 128), bf16)


def output_kernel(*refs):
    parts, (value_ref, out_ref, result_ref) = refs[:4], refs[4:]
    rows = 64
    sums = [as_column(joined_terms(ref[rows:, :128], f // 2), rows, rows * (f % 2)) for f, ref in enumerate(parts)]
    part_share, _ = shares(sums)
    joined = sum(p * ref[:rows, :].astype(f32) for p, ref in zip(part_share, parts))
    head_out = jnp.dot(joined.astype(bf16), value_ref[0], preferred_element_type=f32).astype(bf16)
    line, row = sublanes((128, rows)), lanes((128, rows))
    source = 32 * (line >> 6) + 8 * ((line >> 1) & 3) + ((line >> 3) & 7)
    result = None
    for q in range(2):
        take = jnp.where((source == row) & ((line & 1) == q), 1.0, 0.0).astype(bf16)
        picked_rows = jnp.dot(take, head_out, preferred_element_type=f32).astype(bf16)
        term = jnp.dot(picked_rows, out_ref[:, q * 1024 : (q + 1) * 1024], preferred_element_type=f32)
        result = term if result is None else result + term
    result_ref[...] = result.astype(bf16)


def norm_kernel(info_ref, parts_ref, embeds_ref, gain_ref, spread_ref, resid_ref):
    blk = info_ref[1]
    steps, rows, width = embeds_ref.shape
    half = width // 2
    line = sublanes((2 * steps, half))
    resid = jnp.sum(parts_ref[...].astype(f32), axis=0)
    gain = jnp.zeros((2 * steps, half), f32)
    for q in range(2):
        columns = slice(q * half, (q + 1) * half)
        gain = gain + jnp.where((line & 1) == q, gain_ref[:, columns], 0.0)
        for t in range(steps):
            token = jnp.where(sublanes((rows, half)) == blk, embeds_ref[t, :, columns].astype(f32), 0.0)
            token = jnp.sum(token, axis=0, keepdims=True)
            resid = resid + jnp.where(line == 2 * t + q, token, 0.0)
    resid_ref[...] = resid
    sums = jnp.broadcast_to(jnp.sum(resid * resid, axis=1, keepdims=True), (2 * steps, 128))
    pair = jnp.where((sublanes((8, 8)) >> 1) == (lanes((8, 8)) >> 1), 1.0, 0.0)
    sums = jnp.dot(pair, sums, precision=lax.Precision.HIGHEST, preferred_element_type=f32)
    normed = (resid * lax.rsqrt(sums[:, :1] * (1.0 / width) + EPS) * gain).astype(bf16)
    spread_ref[...] = jnp.broadcast_to(normed[None], spread_ref.shape)


def line_row(line, core):
    chip = (line >> 3) & 63
    return 32 * (chip >> 4) + 16 * ((line >> 9) ^ core) + 4 * (chip & 3) + ((chip >> 2) & 3)


def route_kernel(
    info_ref, gate_hbm, up_hbm, down_hbm, ids_ref, weights_ref, out_ref, gate_ref, up_ref, down_ref, sems
):
    core = info_ref[0]
    copies = fetch((gate_hbm, up_hbm, down_hbm), (gate_ref, up_ref, down_ref), sems)
    top, steps, rows = ids_ref.shape
    line = lanes((rows, out_ref.shape[1]))
    row = line_row(line, core)
    earlier = jnp.where(sublanes((rows, rows)) < lanes((rows, rows)), 1.0, 0.0).astype(bf16)
    slots, weights = [], []
    for e in range(2):
        expert = info_ref[3 + e]
        weight = jnp.zeros((steps, rows), f32)
        routed = jnp.zeros((steps, rows), f32)
        for k in range(top):
            match = ids_ref[k] == expert
            weight = weight + jnp.where(match, weights_ref[k], 0.0)
            routed = routed + jnp.where(match, 1.0, 0.0)
        wide = jnp.concatenate([routed, jnp.zeros((8 - steps, rows), f32)], axis=0).astype(bf16)
        rank = jnp.dot(wide, earlier, preferred_element_type=f32)[:steps]
        first = (sublanes((steps, rows)) * CAPACITY + 1).astype(f32)
        slots.append(jnp.where(routed > 0.5, rank + first, 0.0))
        weights.append(weight)
    total = jnp.zeros(out_ref.shape, f32)
    for t in range(steps):
        place = sublanes((8, rows))
        values = jnp.zeros((8, rows), f32)
        for k, value in enumerate(slots + weights):
            values = jnp.where(place == k, value[t : t + 1], values)
        take = jnp.where((sublanes(line.shape) == row) & (((line >> 1) & 3) == t), 1.0, 0.0)
        total = total + jnp.dot(values, take, precision=lax.Precision.HIGHEST, preferred_element_type=f32)
    out_ref[...] = total
    for copy in copies:
        copy.wait()


def line_places(line, core, lines):
    row = line_row(line, core)
    return ((row & 1) ^ core) * (lines // 2) + (row >> 1) * 4 + ((line >> 1) & 3)


def picked(source_ref, hit, line, place, weights):
    halves = []
    for q in range(2):
        pick = jnp.where((line & 1) == q, hit, 0.0).astype(bf16)
        halves.append(jnp.dot(pick, source_ref[...], preferred_element_type=f32))
    first = jnp.where((line & 1) == 0, 1.0, 0.0)
    scale = [
        jnp.sum(hit[e * SLOTS : (e + 1) * SLOTS] * (first * weights[e]), axis=1, keepdims=True)
        for e in range(len(weights))
    ]
    parts = jnp.where(sublanes((8, line.shape[1])) == 0, (place + 1) >> 4, (place + 1) & 15).astype(f32)
    spot = lax.dot_general((parts * first).astype(bf16), hit.astype(bf16), LAST, preferred_element_type=f32)
    return halves, jnp.concatenate(scale, axis=0), spot


def gated(x, gate, up):
    gate_val = lax.dot_general(x, gate, LAST, preferred_element_type=f32)
    up_val = lax.dot_general(x, up, LAST, preferred_element_type=f32)
    return (gate_val / (1.0 + jnp.exp(-gate_val)) * up_val).astype(bf16)


def pick_kernel(
    info_ref, mine_ref, route_ref, resid_ref, gate_ref, up_ref, down_ref,
    x_ref, own_ref, scale_ref, spot_ref,
):
    core, blk, y = info_ref[0], info_ref[1], info_ref[2]
    own_chip = 4 * (blk & 3) + (blk >> 2)
    lines, half = mine_ref.shape
    routed = 2 * SLOTS
    line = lanes((1, lines))
    hits = [sublanes((SLOTS, lines)) + 1 == route_ref[e : e + 1, :lines].astype(jnp.int32) for e in range(2)]
    hits.append(sublanes((OWN_ROWS, lines)) == (line >> 1) - y * OWN_ROWS)
    hit = jnp.concatenate([jnp.where(h, 1.0, 0.0) for h in hits], axis=0)
    place = line_places(line, core, lines)
    halves, scale, spot = picked(mine_ref, hit, line, place, [route_ref[2 + e : 3 + e, :lines] for e in range(2)])
    for q in range(2):
        x_ref[:, q * half : (q + 1) * half] = halves[q][:routed].astype(bf16)
    scale_ref[...] = jnp.broadcast_to(scale, scale_ref.shape)
    spot_ref[...] = spot
    own_rows = jnp.concatenate([v[routed:].astype(bf16) for v in halves], axis=1)
    act = gated(own_rows, gate_ref[...], up_ref[...])
    own = jnp.dot(act, down_ref[...], preferred_element_type=f32)
    for t in range(4):
        whole = jnp.concatenate([resid_ref[2 * t + q : 2 * t + q + 1, :] for q in range(2)], axis=1)
        own = own + jnp.where(sublanes((OWN_ROWS, 1)) == own_chip * 4 + t, whole, 0.0)
    own_ref[...] = own.astype(bf16)


def put(ref, y_ref, spot, side):
    lines, half = ref.shape
    line = sublanes((lines, 1))
    found = jnp.where((line >> 1) + side * (lines // 2) == spot, 1.0, 0.0)
    result = None
    for q in range(2):
        found_q = jnp.where((line & 1) == q, found, 0.0).astype(bf16)
        term = jnp.dot(found_q, y_ref[:, q * half : (q + 1) * half], preferred_element_type=f32)
        result = term if result is None else result + term
    ref[...] = result.astype(bf16)


def expert_kernel(
    info_ref, mine_x_ref, own_ref, mine_scale_ref, mine_spot_ref, other_ref, route_ref,
    gate_ref, up_ref, down_ref,
    other_out_ref, y_ref, spot_ref, x_ref,
):
    core = info_ref[0]
    lines, half = other_ref.shape
    line = lanes((1, lines)) + lines
    hits = [sublanes((SLOTS, lines)) + 1 == route_ref[e : e + 1, lines:].astype(jnp.int32) for e in range(2)]
    hit = jnp.concatenate([jnp.where(h, 1.0, 0.0) for h in hits], axis=0)
    place = line_places(line, core, lines)
    halves, scale, spot = picked(other_ref, hit, line, place, [route_ref[2 + e : 3 + e, lines:] for e in range(2)])
    routed = 2 * SLOTS
    for q in range(2):
        columns = slice(q * half, (q + 1) * half)
        x_ref[:, columns] = (mine_x_ref[:, columns].astype(f32) + halves[q]).astype(bf16)
    scale = scale + mine_scale_ref[:, :1]
    spot = jnp.concatenate([spot, jnp.zeros((8, OWN_ROWS), f32)], axis=1) + mine_spot_ref[...]
    spot = (spot[0:1] * 16.0 + spot[1:2] - 1.0).astype(jnp.int32)
    spot_ref[...] = jnp.broadcast_to(spot, spot_ref.shape)

    for e in range(2):
        part = slice(e * SLOTS, (e + 1) * SLOTS)
        act = gated(x_ref[part, :], gate_ref[e], up_ref[e])
        down = jnp.dot(act, down_ref[e], preferred_element_type=f32)
        y_ref[part, :] = (down * scale[part]).astype(bf16)
    y_ref[routed:, :] = own_ref[...]
    put(other_out_ref, y_ref, spot, 1)


def put_kernel(y_ref, spot_ref, out_ref):
    put(out_ref, y_ref, spot_ref[0:1], 0)


def per_device(
    embeds,
    attn_gain,
    w_query,
    w_latent,
    latent_gain,
    w_key_up,
    w_value_up,
    w_out,
    ffn_gain,
    w_shared_gate,
    w_shared_up,
    w_shared_down,
    w_expert_gate,
    w_expert_up,
    w_expert_down,
    cache_pool,
    block_tables,
    block_counts,
    parents,
    expert_ids,
    expert_weights,
):
    steps, row_dev, width = embeds.shape
    groups, beams, _ = block_tables.shape
    latent = w_key_up.shape[2]
    entry_width = cache_pool.shape[3]
    rope = entry_width - latent
    pair_dev, _, unit_dev = w_expert_gate.shape
    half = width // 2
    chips = expert_ids.shape[1] // 2
    lines = chips * 2 * steps
    y, core = lax.axis_index("y"), lax.axis_index("core")
    blk, beam = lax.axis_index(BLK), lax.axis_index(BEAM)
    expert = blk * pair_dev * 2 + beam * unit_dev // FFE
    place = jnp.stack([core, blk, y, expert, expert + 2]).astype(jnp.int32)
    counts = jnp.concatenate([blk[None], block_counts]).astype(jnp.int32)

    frequency = np.float64(THETA) ** (-np.arange(rope // 2) * 2.0 / rope)
    frequency = np.tile(frequency.astype(np.float32), 4).reshape(1, 128)
    rows_all = groups * steps * beams
    blk_size = lax.axis_size("x") * lax.axis_size("z")
    sources = (embeds, w_query.T, w_key_up, attn_gain.reshape(1, width), jnp.asarray(frequency), block_counts, w_latent.T)
    query, normed, cosines, latent_weights = kernel_call(
        query_kernel,
        "query",
        [((rows_all + 8, latent), bf16), ((rows_all, width), bf16), ((8, 128), f32), ((entry_width, width), bf16)],
        [pltpu.VMEM(a.shape, a.dtype) for a in sources[:-2]]
        + [pltpu.SMEM(block_counts.shape, jnp.int32), pltpu.SemaphoreType.DMA((len(sources),))],
        (60_000_000, 20_000_000, 0),
        (pltpu.HBM,) * len(sources),
        *in_hbm(*sources),
    )
    query = jnp.stack(gather(query, 0))
    queries = gather(query, 1)
    _, normed, expert_ids = lax.optimization_barrier((query, normed, expert_ids))
    (entries,) = kernel_call(
        entry_kernel,
        "entry",
        [((rows_all, entry_width), bf16)],
        [],
        (150_000_000, 3_000_000, 0),
        (),
        normed,
        latent_weights,
        latent_gain.reshape(1, latent),
        cosines,
    )
    cache = cache_pool.transpose(0, 1, 3, 2)
    fetched = (w_shared_gate.T, w_shared_up.T, w_shared_down)
    route, *shared = kernel_call(
        route_kernel,
        "route",
        [((8, 2 * lines), f32)] + [(a.shape, bf16) for a in fetched],
        room_for(fetched)[-1:],
        (60_000_000, 60_000, 0),
        SCALARS + (pltpu.HBM,) * len(fetched),
        place,
        *in_hbm(*fetched),
        expert_ids.transpose(2, 0, 1),
        expert_weights.transpose(2, 0, 1),
    )
    counts, route = lax.optimization_barrier((counts, route))
    part = ((4 * rows_all + 8, latent), bf16)
    parts = kernel_call(
        attend_kernel,
        "attend",
        [part] * 4,
        [pltpu.VMEM((4, 4 * rows_all, 128), f32)],
        (1_800_000_000, 5_000_000, 800_000),
        SCALARS,
        counts,
        *queries,
        cache,
        entries,
        parents,
        block_tables,
    )
    moved = {s: shifted(parts[s], 0, -s) for s in (1, 3, 2)}
    parts = [parts[0]] + [moved[s] for s in range(1, 4)]
    last = ((rows_all + 8, latent), bf16)
    parts = kernel_call(merge_kernel, "merge", [last] * 4, [], (4_000_000, 30_000_000, 2_000), (), *parts)
    moved = {f: shifted(parts[f], 1, -f) for f in (1, 3, 2)}
    parts = [parts[0]] + [moved[f] for f in range(1, 4)]
    (attn_part,) = kernel_call(
        output_kernel,
        "output",
        [((row_dev * 2 * steps, half), bf16)],
        [],
        (80_000_000, 90_000_000, 1_000),
        (),
        *parts,
        w_value_up,
        w_out,
    )
    attn_part = lax.all_to_all(attn_part.reshape(row_dev, 2 * steps, half), BLK, 0, 0)
    spread, resid = kernel_call(
        norm_kernel,
        "norm",
        [((chips, 2 * steps, half), bf16), ((2 * steps, half), f32)],
        [],
        (1_000_000, 90_000_000, 0),
        SCALARS,
        place,
        attn_part,
        embeds,
        ffn_gain.reshape(1, width),
    )

    mine = lax.all_to_all(spread, ("y", "z", "x"), 0, 0).reshape(lines, half)
    other = lax.ppermute(mine, "core", CORES)
    routed = pair_dev * SLOTS
    total = routed + OWN_ROWS
    slots = [((routed, width), bf16), ((OWN_ROWS, width), bf16), ((routed, 128), f32), ((8, total), f32)]
    x_mine, own, scale, spot = kernel_call(
        pick_kernel,
        "pick",
        slots,
        [],
        (1_000_000_000, 20_000_000, 0),
        SCALARS,
        place,
        mine,
        route,
        resid,
        *shared,
    )
    other_out, outs, spot = kernel_call(
        expert_kernel,
        "experts",
        [((lines, half), bf16), ((total, width), bf16), ((8, total), jnp.int32)],
        [pltpu.VMEM((routed, width), bf16)],
        (3_000_000_000, 15_000_000, 300_000),
        SCALARS,
        place,
        x_mine,
        own,
        scale,
        spot,
        other,
        route,
        w_expert_gate.transpose(0, 2, 1),
        w_expert_up.transpose(0, 2, 1),
        w_expert_down,
    )
    arrived = lax.ppermute(other_out, "core", CORES)
    (own_out,) = kernel_call(
        put_kernel, "put", [((lines, half), bf16)], [], (500_000_000, 2_000_000, 0), (), outs, spot
    )
    own_out = own_out.astype(f32) + arrived.astype(f32)
    own_out = own_out.astype(bf16).reshape(chips, 2 * steps, half)
    result = jnp.sum(lax.all_to_all(own_out, ("x", "z", "y"), 0, 0).astype(f32), axis=0)
    return result.reshape(steps, 1, width)


def solution(mesh):
    devices = mesh.devices.reshape(4, 4, 4, 2)
    split = Mesh(devices, ("x", "z", "y", "core"))
    placed = (
        P(None, BEAM, None),
        P(),
        P(None, BLK),
        P(),
        P(),
        P(BLK, None, None),
        P(BLK, None, None),
        P(BLK, None),
        P(),
        P(None, BLK),
        P(None, BLK),
        P(BLK, None),
        P(BLK, None, BEAM),
        P(BLK, None, BEAM),
        P(BLK, BEAM, None),
        P(BEAM, BLK, None, None),
        P(BEAM, None, None),
        P(BEAM),
        P(None, BEAM, None),
        P(),
        P(),
    )
    return jax.shard_map(
        per_device,
        mesh=split,
        in_specs=placed,
        out_specs=P(None, OUT_ORDER, None),
        check_vma=False,
    )
```

```python
import functools

import jax
import jax.numpy as jnp
import numpy as np
from jax import lax
from jax.experimental import pallas as pl
from jax.experimental.pallas import tpu as pltpu
from jax.sharding import Mesh, PartitionSpec as P

FFE = 1408
THETA = 50000.0
EPS = 1e-06
NEG = -1e30
CAPACITY = 24
SLOTS = 4 * CAPACITY
OWN_ROWS = 64

BLK = ("x", "z")
BEAM = ("y", "core")
OUT_ORDER = BLK + BEAM
CORES = [(0, 1), (1, 0)]
SCALARS = (pltpu.SMEM,)
VMEM_MIB = {"attend": 20, "pick": 16, "experts": 16, "put": 12}

f32, bf16 = jnp.float32, jnp.bfloat16
LAST = (((1,), (1,)), ((), ()))


def lanes(shape):
    return lax.broadcasted_iota(jnp.int32, shape, len(shape) - 1)


def sublanes(shape):
    return lax.broadcasted_iota(jnp.int32, shape, len(shape) - 2)


def kernel_call(body, name, outs, scratch, cost, first, *args):
    vmem = pl.BlockSpec(memory_space=pltpu.VMEM)
    first = [pl.BlockSpec(memory_space=space) for space in first]
    return pl.pallas_call(
        body,
        out_shape=[jax.ShapeDtypeStruct(shape, dtype) for shape, dtype in outs],
        in_specs=first + [vmem] * (len(args) - len(first)),
        out_specs=[vmem] * len(outs),
        scratch_shapes=scratch,
        compiler_params=pltpu.CompilerParams(vmem_limit_bytes=VMEM_MIB.get(name, 6) << 20),
        cost_estimate=pl.CostEstimate(flops=cost[0], bytes_accessed=cost[1], transcendentals=cost[2]),
        name=name,
    )(*args)


def fetch(sources, targets, sems):
    copies = [pltpu.make_async_copy(a, b, sems.at[k]) for k, (a, b) in enumerate(zip(sources, targets))]
    for copy in copies:
        copy.start()
    return copies


def in_hbm(*arrays):
    return [pltpu.with_memory_space_constraint(a, pltpu.HBM) for a in arrays]


def room_for(arrays):
    return [pltpu.VMEM(a.shape, a.dtype) for a in arrays] + [pltpu.SemaphoreType.DMA((len(arrays),))]


def shifted(value, turn, by):
    pairs = []
    for x in range(4):
        for z in range(4):
            for core in range(2):
                along_x = core == turn
                to = ((x + by) % 4, z) if along_x else (x, (z + by) % 4)
                pairs.append((8 * x + 2 * z + core, 8 * to[0] + 2 * to[1] + core))
    return lax.ppermute(value, ("x", "z", "core"), pairs)


def gather(value, turn):
    arrived = {s: shifted(value, turn, s) for s in (1, 3, 2)}
    return [value] + [arrived[s] for s in range(1, 4)]


def rope_parts(cos_ref, rows):
    cosine, sine = cos_ref[:, :64], cos_ref[:, 64:]
    wide = lambda v: jnp.concatenate([jnp.broadcast_to(v[k : k + 1], (8, 64)) for k in range(rows // 8)], axis=0)
    return wide(cosine), wide(sine)


def turned(values, precision=None):
    i, j = sublanes((64, 64)), lanes((64, 64))
    turn = jnp.where(i == j - 32, 1.0, 0.0) - jnp.where(i == j + 32, 1.0, 0.0)
    return jnp.dot(values, turn.astype(values.dtype), precision=precision, preferred_element_type=f32)


def query_kernel(
    embeds_hbm, query_hbm, key_up_hbm, gain_hbm, frequency_hbm, counts_hbm, latent_hbm,
    result_ref, normed_ref, cos_ref, latent_ref,
    embeds_ref, query_ref, key_up_ref, gain_ref, frequency_ref, counts_ref, sems,
):
    steps, _, width = embeds_ref.shape
    copies = fetch(
        (embeds_hbm, query_hbm, key_up_hbm, gain_hbm, frequency_hbm, counts_hbm, latent_hbm),
        (embeds_ref, query_ref, key_up_ref, gain_ref, frequency_ref, counts_ref, latent_ref),
        sems,
    )
    copies[4].wait()
    copies[5].wait()
    line = sublanes((8, 128))
    position = jnp.where(line < steps, counts_ref[0], counts_ref[1]) * 128 + (line & (steps - 1))
    angles = position.astype(f32) * frequency_ref[...]
    cos_ref[...] = jnp.where(lanes((8, 128)) < 64, jnp.cos(angles), jnp.sin(angles))
    copies[0].wait()
    copies[3].wait()
    tokens = [embeds_ref[t].astype(f32) for t in range(steps)]
    tokens = jnp.concatenate([tokens[t][8 * g : 8 * g + 8] for g in range(2) for t in range(steps)], axis=0)
    mean_sq = jnp.sum(tokens * tokens, axis=1, keepdims=True) * (1.0 / width)
    normed = (tokens * lax.rsqrt(mean_sq + EPS) * gain_ref[...]).astype(bf16)
    normed_ref[...] = normed
    copies[1].wait()
    queries = lax.dot_general(normed, query_ref[...], LAST, preferred_element_type=f32).astype(bf16)
    copies[2].wait()
    latent = jnp.dot(queries[:, :128], key_up_ref[0], preferred_element_type=f32).astype(bf16)
    rope = queries[:, 128:]
    cosine, sine = rope_parts(cos_ref, 64)
    rope = (rope.astype(f32) * cosine + turned(rope) * sine).astype(bf16)
    result_ref[:64, :] = latent
    result_ref[64:, :] = jnp.concatenate([rope[8 * k : 8 * k + 8] for k in range(8)], axis=1)
    copies[6].wait()


def entry_kernel(normed_ref, latent_ref, gain_ref, cos_ref, out_ref):
    projected = lax.dot_general(normed_ref[...], latent_ref[...], LAST, preferred_element_type=f32)
    latent, rope = projected[:, :512], projected[:, 512:]
    mean_sq = jnp.sum(latent * latent, axis=1, keepdims=True) * (1.0 / 512)
    out_ref[:, :512] = (latent * lax.rsqrt(mean_sq + EPS) * gain_ref[...]).astype(bf16)
    cosine, sine = rope_parts(cos_ref, 64)
    out_ref[:, 512:] = (rope * cosine + turned(rope, lax.Precision.HIGHEST) * sine).astype(bf16)


def split_terms(lines):
    place = sublanes((8, lines[0].shape[1]))
    tile = jnp.zeros(place.shape, f32)
    for k, line in enumerate(lines):
        first = line.astype(bf16).astype(f32)
        second = (line - first).astype(bf16).astype(f32)
        for j, term in enumerate((first, second, line - first - second)):
            tile = jnp.where(place == 3 * k + j, term, tile)
    return tile.astype(bf16)


def joined_terms(tile, k):
    tile = tile.astype(f32)[3 * k : 3 * k + 3]
    return tile[0:1] + tile[1:2] + tile[2:3]


def as_line(column, offset=0):
    shape = (column.shape[0], 128)
    return jnp.sum(jnp.where(lanes(shape) == sublanes(shape) + offset, column, 0.0), axis=0, keepdims=True)


def as_column(line, count, offset=0):
    shape = (count, 128)
    return jnp.sum(jnp.where(lanes(shape) == sublanes(shape) + offset, line, 0.0), axis=1, keepdims=True)


def attend_kernel(info_ref, *refs):
    q_refs, out_refs = refs[:4], refs[8:12]
    cache_ref, entry_ref, parent_ref, table_ref = refs[4:8]
    sum_ref = refs[12]
    near, heads, rows_all, width = 4, 16, 64, entry_ref.shape[1]
    groups, beams, _ = table_ref.shape
    rows = rows_all // groups
    pool, _, block_len = cache_ref.shape[1:]
    latent = out_refs[0].shape[1]
    steps = rows // beams
    scale = (width - latent + 128) ** (-0.5)
    blk = info_ref[0]
    for g in range(groups):
        shape = (beams, 128)
        origin = (lanes(shape) == sublanes(shape)).astype(f32)
        kept = []
        for t in range(steps):
            diagonal = lanes((beams, beams)) == sublanes((beams, beams))
            parent = jnp.where(diagonal, parent_ref[t, g : g + 1, :].astype(f32), 0.0)
            parent = jnp.sum(parent, axis=1, keepdims=True).astype(jnp.int32)
            choose = (lanes((beams, beams)) == parent).astype(f32)
            origin = jnp.dot(choose, origin, preferred_element_type=f32)
            origin = origin + (lanes(shape) == sublanes(shape) + beams * (1 + t)).astype(f32)
            kept.append(origin)
        origin = jnp.concatenate(kept, axis=0)
        table = table_ref[g]
        live = lanes(table.shape) < info_ref[1 + g]
        used = jnp.zeros((beams, 128), f32)
        for p in range(pool):
            hit = jnp.where((table == blk * pool + p) & live, 1.0, 0.0)
            hit = jnp.max(hit, axis=1, keepdims=True)
            used = used + jnp.where(lanes(used.shape) == p, hit, 0.0)
        used = jnp.dot(origin[:, :beams], used, preferred_element_type=f32)
        bias = jnp.concatenate(
            [jnp.broadcast_to(used[:, p : p + 1], (rows, block_len)) for p in range(pool)], axis=1
        )
        bias = jnp.where(bias > 0.5, 0.0, NEG)
        seen = origin[:, beams : beams + rows]
        recent_bias = jnp.where((seen > 0.5) & (blk == 0), 0.0, NEG)

        part = slice(g * rows, (g + 1) * rows)
        lat_part = jnp.concatenate([ref[:, part, :] for ref in q_refs], axis=0)
        rope_tile = jnp.concatenate([ref[:, rows_all:, :] for ref in q_refs], axis=0)
        rope_part = [rope_tile[:, :, 64 * k : 64 * k + 64] for k in range(steps * g, steps * g + steps)]
        q = jnp.concatenate([lat_part, jnp.concatenate(rope_part, axis=1)], axis=2).reshape(heads * rows, width)
        keys = jnp.concatenate([cache_ref[g, p] for p in range(pool)], axis=1)
        entry = entry_ref[part]
        scores = jnp.dot(q, keys, preferred_element_type=f32)
        scores = scores.reshape(heads, rows, pool * block_len) * scale + bias[None]
        recent = lax.dot_general(q, entry, LAST, preferred_element_type=f32)
        recent = recent.reshape(heads, rows, rows) * scale + recent_bias[None]
        top = jnp.maximum(
            jnp.max(scores, axis=-1, keepdims=True), jnp.max(recent, axis=-1, keepdims=True)
        )
        weights = jnp.exp(scores - top)
        recent = jnp.exp(recent - top)
        total = jnp.sum(weights, axis=-1, keepdims=True) + jnp.sum(recent, axis=-1, keepdims=True)
        weights = weights.astype(bf16).reshape(heads * rows, pool * block_len)
        recent = recent.astype(bf16).reshape(heads * rows, rows)
        lat = lax.dot_general(weights, keys[:latent], LAST, preferred_element_type=f32)
        lat = lat + jnp.dot(recent, entry[:, :latent], preferred_element_type=f32)
        lat = (lat.reshape(heads, rows, latent) * (1.0 / total)).astype(bf16)
        lse = jnp.where(top > 0.1 * NEG, top + jnp.log(total), NEG)
        lse = jnp.broadcast_to(lse, (heads, rows, 128))
        for s in range(near):
            for f in range(4):
                first = f * rows_all + g * rows
                out_refs[s][first : first + rows, :] = lat[f * near + s]
                sum_ref[s, first : first + rows, :] = lse[f * near + s]
    for s, ref in enumerate(out_refs):
        lines = [as_line(sum_ref[s, 128 * k : 128 * k + 128, :]) for k in range(2)]
        ref[4 * rows_all :, :128] = split_terms(lines)
        ref[4 * rows_all :, 128:] = jnp.zeros((8, latent - 128), bf16)


def shares(sums):
    best = functools.reduce(jnp.maximum, sums)
    parts = [jnp.exp(v - best) for v in sums]
    whole = functools.reduce(jnp.add, parts)
    return [p / whole for p in parts], best + jnp.log(whole)


def merge_kernel(*refs):
    parts, outs = refs[:4], refs[4:]
    rows = 64
    lines = []
    for k in range(2):
        part_share, whole = shares([joined_terms(ref[4 * rows :, :128], k) for ref in parts])
        lines.append(whole)
        own = slice(128 * k, 128 * k + 128)
        merged = sum(as_column(p, 128) * ref[own, :].astype(f32) for p, ref in zip(part_share, parts))
        merged = merged.astype(bf16)
        for f in range(2):
            outs[2 * k + f][:rows, :] = merged[rows * f : rows * f + rows]
    tile = split_terms(lines)
    for ref in outs:
        ref[rows:, :128] = tile
        ref[rows:, 128:] = jnp.zeros((8, ref.shape[1] - 128), bf16)


def output_kernel(*refs):
    parts, (value_ref, out_ref, result_ref) = refs[:4], refs[4:]
    rows = 64
    sums = [as_column(joined_terms(ref[rows:, :128], f // 2), rows, rows * (f % 2)) for f, ref in enumerate(parts)]
    part_share, _ = shares(sums)
    joined = sum(p * ref[:rows, :].astype(f32) for p, ref in zip(part_share, parts))
    head_out = jnp.dot(joined.astype(bf16), value_ref[0], preferred_element_type=f32).astype(bf16)
    line, row = sublanes((128, rows)), lanes((128, rows))
    source = 32 * (line >> 6) + 8 * ((line >> 1) & 3) + ((line >> 3) & 7)
    result = None
    for q in range(2):
        take = jnp.where((source == row) & ((line & 1) == q), 1.0, 0.0).astype(bf16)
        picked_rows = jnp.dot(take, head_out, preferred_element_type=f32).astype(bf16)
        term = jnp.dot(picked_rows, out_ref[:, q * 1024 : (q + 1) * 1024], preferred_element_type=f32)
        result = term if result is None else result + term
    result_ref[...] = result.astype(bf16)


def norm_kernel(info_ref, parts_ref, embeds_ref, gain_ref, spread_ref, resid_ref):
    blk = info_ref[1]
    steps, rows, width = embeds_ref.shape
    half = width // 2
    line = sublanes((2 * steps, half))
    resid = jnp.sum(parts_ref[...].astype(f32), axis=0)
    gain = jnp.zeros((2 * steps, half), f32)
    for q in range(2):
        columns = slice(q * half, (q + 1) * half)
        gain = gain + jnp.where((line & 1) == q, gain_ref[:, columns], 0.0)
        for t in range(steps):
            token = jnp.where(sublanes((rows, half)) == blk, embeds_ref[t, :, columns].astype(f32), 0.0)
            token = jnp.sum(token, axis=0, keepdims=True)
            resid = resid + jnp.where(line == 2 * t + q, token, 0.0)
    resid_ref[...] = resid
    sums = jnp.broadcast_to(jnp.sum(resid * resid, axis=1, keepdims=True), (2 * steps, 128))
    pair = jnp.where((sublanes((8, 8)) >> 1) == (lanes((8, 8)) >> 1), 1.0, 0.0)
    sums = jnp.dot(pair, sums, precision=lax.Precision.HIGHEST, preferred_element_type=f32)
    normed = (resid * lax.rsqrt(sums[:, :1] * (1.0 / width) + EPS) * gain).astype(bf16)
    spread_ref[...] = jnp.broadcast_to(normed[None], spread_ref.shape)


def line_row(line, core):
    chip = (line >> 3) & 63
    return 32 * (chip >> 4) + 16 * ((line >> 9) ^ core) + (chip & 15)


def route_kernel(
    info_ref, gate_hbm, up_hbm, down_hbm, ids_ref, weights_ref, out_ref, gate_ref, up_ref, down_ref, sems
):
    core = info_ref[0]
    copies = fetch((gate_hbm, up_hbm, down_hbm), (gate_ref, up_ref, down_ref), sems)
    top, steps, rows = ids_ref.shape
    line = lanes((rows, out_ref.shape[1]))
    row = line_row(line, core)
    earlier = jnp.where(sublanes((rows, rows)) < lanes((rows, rows)), 1.0, 0.0).astype(bf16)
    slots, weights = [], []
    for e in range(2):
        expert = info_ref[3 + e]
        weight = jnp.zeros((steps, rows), f32)
        routed = jnp.zeros((steps, rows), f32)
        for k in range(top):
            match = ids_ref[k] == expert
            weight = weight + jnp.where(match, weights_ref[k], 0.0)
            routed = routed + jnp.where(match, 1.0, 0.0)
        wide = jnp.concatenate([routed, jnp.zeros((8 - steps, rows), f32)], axis=0).astype(bf16)
        rank = jnp.dot(wide, earlier, preferred_element_type=f32)[:steps]
        first = (sublanes((steps, rows)) * CAPACITY + 1).astype(f32)
        slots.append(jnp.where(routed > 0.5, rank + first, 0.0))
        weights.append(weight)
    total = jnp.zeros(out_ref.shape, f32)
    for t in range(steps):
        place = sublanes((8, rows))
        values = jnp.zeros((8, rows), f32)
        for k, value in enumerate(slots + weights):
            values = jnp.where(place == k, value[t : t + 1], values)
        take = jnp.where((sublanes(line.shape) == row) & (((line >> 1) & 3) == t), 1.0, 0.0)
        total = total + jnp.dot(values, take, precision=lax.Precision.HIGHEST, preferred_element_type=f32)
    out_ref[...] = total
    for copy in copies:
        copy.wait()


def line_places(line, core, lines):
    row = line_row(line, core)
    return ((row & 1) ^ core) * (lines // 2) + (row >> 1) * 4 + ((line >> 1) & 3)


def picked(source_ref, hit, line, place, weights):
    halves = []
    for q in range(2):
        pick = jnp.where((line & 1) == q, hit, 0.0).astype(bf16)
        halves.append(jnp.dot(pick, source_ref[...], preferred_element_type=f32))
    first = jnp.where((line & 1) == 0, 1.0, 0.0)
    scale = [
        jnp.sum(hit[e * SLOTS : (e + 1) * SLOTS] * (first * weights[e]), axis=1, keepdims=True)
        for e in range(len(weights))
    ]
    parts = jnp.where(sublanes((8, line.shape[1])) == 0, (place + 1) >> 4, (place + 1) & 15).astype(f32)
    spot = lax.dot_general((parts * first).astype(bf16), hit.astype(bf16), LAST, preferred_element_type=f32)
    return halves, jnp.concatenate(scale, axis=0), spot


def gated(x, gate, up):
    gate_val = lax.dot_general(x, gate, LAST, preferred_element_type=f32)
    up_val = lax.dot_general(x, up, LAST, preferred_element_type=f32)
    return (gate_val / (1.0 + jnp.exp(-gate_val)) * up_val).astype(bf16)


def pick_kernel(
    info_ref, mine_ref, route_ref, resid_ref, gate_ref, up_ref, down_ref,
    x_ref, own_ref, scale_ref, spot_ref,
):
    core, blk, y = info_ref[0], info_ref[1], info_ref[2]
    own_chip = blk
    lines, half = mine_ref.shape
    routed = 2 * SLOTS
    line = lanes((1, lines))
    hits = [sublanes((SLOTS, lines)) + 1 == route_ref[e : e + 1, :lines].astype(jnp.int32) for e in range(2)]
    hits.append(sublanes((OWN_ROWS, lines)) == (line >> 1) - y * OWN_ROWS)
    hit = jnp.concatenate([jnp.where(h, 1.0, 0.0) for h in hits], axis=0)
    place = line_places(line, core, lines)
    halves, scale, spot = picked(mine_ref, hit, line, place, [route_ref[2 + e : 3 + e, :lines] for e in range(2)])
    for q in range(2):
        x_ref[:, q * half : (q + 1) * half] = halves[q][:routed].astype(bf16)
    scale_ref[...] = jnp.broadcast_to(scale, scale_ref.shape)
    spot_ref[...] = spot
    own_rows = jnp.concatenate([v[routed:].astype(bf16) for v in halves], axis=1)
    act = gated(own_rows, gate_ref[...], up_ref[...])
    own = jnp.dot(act, down_ref[...], preferred_element_type=f32)
    for t in range(4):
        whole = jnp.concatenate([resid_ref[2 * t + q : 2 * t + q + 1, :] for q in range(2)], axis=1)
        own = own + jnp.where(sublanes((OWN_ROWS, 1)) == own_chip * 4 + t, whole, 0.0)
    own_ref[...] = own.astype(bf16)


def put(ref, y_ref, spot, side):
    lines, half = ref.shape
    line = sublanes((lines, 1))
    found = jnp.where((line >> 1) + side * (lines // 2) == spot, 1.0, 0.0)
    result = None
    for q in range(2):
        found_q = jnp.where((line & 1) == q, found, 0.0).astype(bf16)
        term = jnp.dot(found_q, y_ref[:, q * half : (q + 1) * half], preferred_element_type=f32)
        result = term if result is None else result + term
    ref[...] = result.astype(bf16)


def expert_kernel(
    info_ref, mine_x_ref, own_ref, mine_scale_ref, mine_spot_ref, other_ref, route_ref,
    gate_ref, up_ref, down_ref,
    other_out_ref, y_ref, spot_ref, x_ref,
):
    core = info_ref[0]
    lines, half = other_ref.shape
    line = lanes((1, lines)) + lines
    hits = [sublanes((SLOTS, lines)) + 1 == route_ref[e : e + 1, lines:].astype(jnp.int32) for e in range(2)]
    hit = jnp.concatenate([jnp.where(h, 1.0, 0.0) for h in hits], axis=0)
    place = line_places(line, core, lines)
    halves, scale, spot = picked(other_ref, hit, line, place, [route_ref[2 + e : 3 + e, lines:] for e in range(2)])
    routed = 2 * SLOTS
    for q in range(2):
        columns = slice(q * half, (q + 1) * half)
        x_ref[:, columns] = (mine_x_ref[:, columns].astype(f32) + halves[q]).astype(bf16)
    scale = scale + mine_scale_ref[:, :1]
    spot = jnp.concatenate([spot, jnp.zeros((8, OWN_ROWS), f32)], axis=1) + mine_spot_ref[...]
    spot = (spot[0:1] * 16.0 + spot[1:2] - 1.0).astype(jnp.int32)
    spot_ref[...] = jnp.broadcast_to(spot, spot_ref.shape)

    for e in range(2):
        part = slice(e * SLOTS, (e + 1) * SLOTS)
        act = gated(x_ref[part, :], gate_ref[e], up_ref[e])
        down = jnp.dot(act, down_ref[e], preferred_element_type=f32)
        y_ref[part, :] = (down * scale[part]).astype(bf16)
    y_ref[routed:, :] = own_ref[...]
    put(other_out_ref, y_ref, spot, 1)


def put_kernel(y_ref, spot_ref, out_ref):
    put(out_ref, y_ref, spot_ref[0:1], 0)


def per_device(
    embeds,
    attn_gain,
    w_query,
    w_latent,
    latent_gain,
    w_key_up,
    w_value_up,
    w_out,
    ffn_gain,
    w_shared_gate,
    w_shared_up,
    w_shared_down,
    w_expert_gate,
    w_expert_up,
    w_expert_down,
    cache_pool,
    block_tables,
    block_counts,
    parents,
    expert_ids,
    expert_weights,
):
    steps, row_dev, width = embeds.shape
    groups, beams, _ = block_tables.shape
    latent = w_key_up.shape[2]
    entry_width = cache_pool.shape[3]
    rope = entry_width - latent
    pair_dev, _, unit_dev = w_expert_gate.shape
    half = width // 2
    chips = expert_ids.shape[1] // 2
    lines = chips * 2 * steps
    y, core = lax.axis_index("y"), lax.axis_index("core")
    blk, beam = lax.axis_index(BLK), lax.axis_index(BEAM)
    expert = blk * pair_dev * 2 + beam * unit_dev // FFE
    place = jnp.stack([core, blk, y, expert, expert + 2]).astype(jnp.int32)
    counts = jnp.concatenate([blk[None], block_counts]).astype(jnp.int32)

    frequency = np.float64(THETA) ** (-np.arange(rope // 2) * 2.0 / rope)
    frequency = np.tile(frequency.astype(np.float32), 4).reshape(1, 128)
    rows_all = groups * steps * beams
    blk_size = lax.axis_size("x") * lax.axis_size("z")
    sources = (embeds, w_query.T, w_key_up, attn_gain.reshape(1, width), jnp.asarray(frequency), block_counts, w_latent.T)
    query, normed, cosines, latent_weights = kernel_call(
        query_kernel,
        "query",
        [((rows_all + 8, latent), bf16), ((rows_all, width), bf16), ((8, 128), f32), ((entry_width, width), bf16)],
        [pltpu.VMEM(a.shape, a.dtype) for a in sources[:-2]]
        + [pltpu.SMEM(block_counts.shape, jnp.int32), pltpu.SemaphoreType.DMA((len(sources),))],
        (60_000_000, 20_000_000, 0),
        (pltpu.HBM,) * len(sources),
        *in_hbm(*sources),
    )
    query = jnp.stack(gather(query, 0))
    queries = gather(query, 1)
    _, normed, expert_ids = lax.optimization_barrier((query, normed, expert_ids))
    (entries,) = kernel_call(
        entry_kernel,
        "entry",
        [((rows_all, entry_width), bf16)],
        [],
        (150_000_000, 3_000_000, 0),
        (),
        normed,
        latent_weights,
        latent_gain.reshape(1, latent),
        cosines,
    )
    cache = cache_pool.transpose(0, 1, 3, 2)
    fetched = (w_shared_gate.T, w_shared_up.T, w_shared_down)
    route, *shared = kernel_call(
        route_kernel,
        "route",
        [((8, 2 * lines), f32)] + [(a.shape, bf16) for a in fetched],
        room_for(fetched)[-1:],
        (60_000_000, 60_000, 0),
        SCALARS + (pltpu.HBM,) * len(fetched),
        place,
        *in_hbm(*fetched),
        expert_ids.transpose(2, 0, 1),
        expert_weights.transpose(2, 0, 1),
    )
    counts, route = lax.optimization_barrier((counts, route))
    part = ((4 * rows_all + 8, latent), bf16)
    parts = kernel_call(
        attend_kernel,
        "attend",
        [part] * 4,
        [pltpu.VMEM((4, 4 * rows_all, 128), f32)],
        (1_800_000_000, 5_000_000, 800_000),
        SCALARS,
        counts,
        *queries,
        cache,
        entries,
        parents,
        block_tables,
    )
    moved = {s: shifted(parts[s], 0, -s) for s in (1, 3, 2)}
    parts = [parts[0]] + [moved[s] for s in range(1, 4)]
    last = ((rows_all + 8, latent), bf16)
    parts = kernel_call(merge_kernel, "merge", [last] * 4, [], (4_000_000, 30_000_000, 2_000), (), *parts)
    moved = {f: shifted(parts[f], 1, -f) for f in (1, 3, 2)}
    parts = [parts[0]] + [moved[f] for f in range(1, 4)]
    (attn_part,) = kernel_call(
        output_kernel,
        "output",
        [((row_dev * 2 * steps, half), bf16)],
        [],
        (80_000_000, 90_000_000, 1_000),
        (),
        *parts,
        w_value_up,
        w_out,
    )
    attn_part = lax.all_to_all(attn_part.reshape(row_dev, 2 * steps, half), BLK, 0, 0)
    spread, resid = kernel_call(
        norm_kernel,
        "norm",
        [((chips, 2 * steps, half), bf16), ((2 * steps, half), f32)],
        [],
        (1_000_000, 90_000_000, 0),
        SCALARS,
        place,
        attn_part,
        embeds,
        ffn_gain.reshape(1, width),
    )

    mine = lax.all_to_all(spread, ("y", "x", "z"), 0, 0).reshape(lines, half)
    other = lax.ppermute(mine, "core", CORES)
    routed = pair_dev * SLOTS
    total = routed + OWN_ROWS
    slots = [((routed, width), bf16), ((OWN_ROWS, width), bf16), ((routed, 128), f32), ((8, total), f32)]
    x_mine, own, scale, spot = kernel_call(
        pick_kernel,
        "pick",
        slots,
        [],
        (1_000_000_000, 20_000_000, 0),
        SCALARS,
        place,
        mine,
        route,
        resid,
        *shared,
    )
    other_out, outs, spot = kernel_call(
        expert_kernel,
        "experts",
        [((lines, half), bf16), ((total, width), bf16), ((8, total), jnp.int32)],
        [pltpu.VMEM((routed, width), bf16)],
        (3_000_000_000, 15_000_000, 300_000),
        SCALARS,
        place,
        x_mine,
        own,
        scale,
        spot,
        other,
        route,
        w_expert_gate.transpose(0, 2, 1),
        w_expert_up.transpose(0, 2, 1),
        w_expert_down,
    )
    arrived = lax.ppermute(other_out, "core", CORES)
    (own_out,) = kernel_call(
        put_kernel, "put", [((lines, half), bf16)], [], (500_000_000, 2_000_000, 0), (), outs, spot
    )
    own_out = own_out.astype(f32) + arrived.astype(f32)
    own_out = own_out.astype(bf16).reshape(chips, 2 * steps, half)
    result = jnp.sum(lax.all_to_all(own_out, ("x", "z", "y"), 0, 0).astype(f32), axis=0)
    return result.reshape(steps, 1, width)


def solution(mesh):
    devices = mesh.devices.reshape(4, 4, 4, 2)
    split = Mesh(devices, ("x", "z", "y", "core"))
    placed = (
        P(None, BEAM, None),
        P(),
        P(None, BLK),
        P(),
        P(),
        P(BLK, None, None),
        P(BLK, None, None),
        P(BLK, None),
        P(),
        P(None, BLK),
        P(None, BLK),
        P(BLK, None),
        P(BLK, None, BEAM),
        P(BLK, None, BEAM),
        P(BLK, BEAM, None),
        P(BEAM, BLK, None, None),
        P(BEAM, None, None),
        P(BEAM),
        P(None, BEAM, None),
        P(),
        P(),
    )
    return jax.shard_map(
        per_device,
        mesh=split,
        in_specs=placed,
        out_specs=P(None, OUT_ORDER, None),
        check_vma=False,
    )
```
